32 devices in a mesh: rep: 4 (over y, x), ep: 8 (over z, core).
Axes of the slice: x: 2, y: 2, z: 4, core: 2. Of those that a mesh axis runs over, the one named last changes fastest.
Arguments:
- tokens_in: bfloat16 [16384, 1024], P(('rep', 'ep')), may hold values from -6 to 6
- token_ids: int32 [16384], P(('rep', 'ep')), may hold values from 0 to 8191, as said below
- hash_table: int32 [8192], replicated, may hold values from 0 to 7, as said below
- doc_lengths: int32 [32, 4], P(('rep', 'ep')), may hold values from 0 to 512, as said below
- gain_one: float32 [1024], replicated, may hold values from 0.5 to 1.5
- shift_one: float32 [1024], replicated, may hold values from -1.2 to 1.2
- project_in: bfloat16 [1024, 3072], replicated, may hold values from -0.1875 to 0.1875
- project_out: bfloat16 [1024, 1024], replicated, may hold values from -0.5 to 0.5
- gain_two: float32 [1024], replicated, may hold values from 0.5 to 1.5
- shift_two: float32 [1024], replicated, may hold values from -1.2 to 1.2
- expert_in: bfloat16 [8, 1024, 4096], P('ep'), may hold values from -0.1875 to 0.1875
- expert_out: bfloat16 [8, 4096, 1024], P('ep'), may hold values from -0.09375 to 0.09375
- out_grad: bfloat16 [16384, 1024], P(('rep', 'ep')), may hold values from -6 to 6
Outputs:
- block_out: bfloat16 [16384, 1024], P(('rep', 'ep'))
- grad_in: float32 [16384, 1024], P(('rep', 'ep'))
- grad_project_in: float32 [1024, 3072], P(('rep', 'ep'))
- grad_project_out: float32 [1024, 1024], P(('rep', 'ep'))
- grad_gain_one: float32 [1024], P(('rep', 'ep'))
- grad_shift_one: float32 [1024], P(('rep', 'ep'))
- grad_gain_two: float32 [1024], P(('rep', 'ep'))
- grad_shift_two: float32 [1024], P(('rep', 'ep'))
- grad_expert_in: float32 [8, 1024, 4096], P('ep', 'rep')
- grad_expert_out: float32 [8, 4096, 1024], P('ep', 'rep')
The draws below stay inside these ranges and needn't reach their ends.
Inputs may be any that keep to these rules, and one draw needn't show every extreme that they name: `token_ids`: each device's 512 ids send at most 128 tokens to one expert, and on every device some experts get exactly 128. `hash_table`: each expert serves 8192 // 8 ids. `doc_lengths`: each row sums to 512; a 0 is an empty document. Some device holds a single document.
All inputs are finite; a program needn't handle non-finite values.
Results may differ from the reference program's by a relative error of at most 0.012.
Values may be sent and summed in bfloat16 or wider, within the bound.
No kernel may reach another device: no remote copies, remote signals or barrier semaphores. Data moves between devices by JAX's collectives and lax.ppermute only.
A program may use at most 192 MiB of HBM per device.

```python
import math
import jax
import jax.numpy as jnp
from jax import lax

D = 1024
HEADS = 16
FF = 4096
VOCAB = 8192
DOCS = 4
TOK_DEV = 512
EXPERTS = 8
CAP = 128
HOT = 1
TOKENS = 16384


def route_tables(key):
    order = jax.random.permutation(jax.random.fold_in(key, 11), VOCAB).astype(jnp.int32)
    inverse = jnp.argsort(order, stable=True).astype(jnp.int32)
    return (order, inverse)


def draw_hash_table(key, part):
    order, inverse = route_tables(key)
    return (order % EXPERTS).astype(jnp.int32)


def draw_token_ids(key, part):
    order, inverse = route_tables(key)
    shuffled = jax.random.permutation(jax.random.fold_in(key, 12), EXPERTS).astype(jnp.int32)
    is_hot = (shuffled < HOT).astype(jnp.int32)
    slot_expert = jnp.arange(EXPERTS * CAP, dtype=jnp.int32) // CAP
    slot_hot = is_hot[slot_expert]
    device_count = TOKENS // TOK_DEV

    def one_device(device_key):
        priority = jax.random.permutation(jax.random.fold_in(device_key, 1), EXPERTS * CAP).astype(jnp.int32) + slot_hot * (EXPERTS * CAP)
        chosen = jnp.argsort(-priority, stable=True)[:TOK_DEV]
        picked_expert = slot_expert[chosen]
        placed = picked_expert[jax.random.permutation(jax.random.fold_in(device_key, 2), TOK_DEV)]
        within = jax.random.randint(jax.random.fold_in(device_key, 3), (TOK_DEV,), 0, VOCAB // EXPERTS)
        return inverse[placed + EXPERTS * within]
    base_key = jax.random.fold_in(key, 13)
    device_keys = jax.vmap(lambda index: jax.random.fold_in(base_key, index))(jnp.arange(device_count))
    return jax.vmap(one_device)(device_keys).reshape(-1).astype(jnp.int32)


def draw_doc_lengths(key, part):
    device_count = TOKENS // TOK_DEV
    quarter = TOK_DEV // 4
    offsets = jax.random.randint(jax.random.fold_in(key, 21), (device_count, DOCS - 1), -(TOK_DEV // 8), TOK_DEV // 8 + 1).astype(jnp.int32)
    zero_column = jnp.zeros((device_count, 1), jnp.int32)
    padded = jnp.concatenate([zero_column, offsets, zero_column], 1)
    short_rows = quarter + padded[:, 1:] - padded[:, :-1]
    single = jax.random.randint(jax.random.fold_in(key, 22), (device_count,), 0, 2).astype(jnp.int32)
    single = single.at[0].set(1)
    long_row = jnp.zeros((DOCS,), jnp.int32).at[0].set(TOK_DEV)
    return jnp.where(single[:, None] == 1, long_row[None, :], short_rows).astype(jnp.int32)


def block_levels(key, shape, shards, least, largest):
    loudness, own = 1.0, jax.random.fold_in(key, 6)
    for dim, shards_of in shards:
        draws = jnp.exp(jax.random.uniform(jax.random.fold_in(own, dim), (shards_of,), jnp.float32, least / len(shards), largest / len(shards)))
        loudness = loudness * jnp.repeat(draws, shape[dim] // shards_of).reshape([-1 if axis == dim else 1 for axis in range(len(shape))])
    return loudness


def scatter_about(key, extent, width, reach, pieces=(), held_as=jnp.bfloat16):
    values = jax.random.normal(key, extent, jnp.float32) * width
    if len(pieces) > 0:
        values = block_levels(key, extent, pieces, -0.22, 0.18) * values
    return jnp.clip(values, min=-reach, max=reach).astype(held_as)


def setup_inputs(seed: int = 0) -> dict:
    key_of = jax.random.split(jax.random.key(seed), 14)
    tokens_in = scatter_about(key_of[0], (TOKENS, D), 1.0, 6.0, ((0, 32),))
    token_ids = draw_token_ids(jax.random.fold_in(key_of[13], 71), 0)
    hash_table = draw_hash_table(jax.random.fold_in(key_of[13], 71), 0)
    doc_lengths = draw_doc_lengths(jax.random.fold_in(key_of[13], 71), 0)
    gain_one = jnp.clip(1.0 + 0.1 * jax.random.normal(key_of[4], (D,), jnp.float32), 0.5, 1.5)
    shift_one = scatter_about(key_of[5], (D,), 0.2, 1.2, (), jnp.float32)
    project_in = scatter_about(key_of[6], (D, 3 * D), D ** -0.5, 0.1875)
    project_out = scatter_about(key_of[7], (D, D), (D // 8) ** -0.5, 0.5)
    gain_two = jnp.clip(1.0 + 0.1 * jax.random.normal(key_of[8], (D,), jnp.float32), 0.5, 1.5)
    shift_two = scatter_about(key_of[9], (D,), 0.2, 1.2, (), jnp.float32)
    expert_in = scatter_about(key_of[10], (EXPERTS, D, FF), D ** -0.5, 0.1875, ((0, 8),))
    expert_out = scatter_about(key_of[11], (EXPERTS, FF, D), FF ** -0.5, 0.09375, ((0, 8),))
    out_grad = scatter_about(key_of[12], (TOKENS, D), 1.0, 6.0, ((0, 32),))
    return dict(tokens_in=tokens_in, token_ids=token_ids, hash_table=hash_table, doc_lengths=doc_lengths, gain_one=gain_one, shift_one=shift_one, project_in=project_in, project_out=project_out, gain_two=gain_two, shift_two=shift_two, expert_in=expert_in, expert_out=expert_out, out_grad=out_grad)


NEG_LARGE = -1e+30
EPSILON = 1e-05
HIGHEST = lax.Precision.HIGHEST

@jax.custom_vjp
def low(v):
    return lax.optimization_barrier(v.astype(jnp.bfloat16)).astype(jnp.float32)

@jax.custom_vjp
def low_back(v):
    return v

def low_keep(v):
    return (low(v), None)

def low_pass(kept, grad):
    return (grad,)

def back_keep(v):
    return (v, None)

def back_low(kept, grad):
    return (low(grad),)
low.defvjp(low_keep, low_pass)
low_back.defvjp(back_keep, back_low)

def layer_norm(values, gain_vec, shift_vec):
    center = lax.optimization_barrier(jnp.mean(values, -1, keepdims=True))
    centered = values - center
    spread = lax.optimization_barrier(jnp.mean(centered * centered, -1, keepdims=True))
    return centered * lax.rsqrt(spread + EPSILON) * gain_vec + shift_vec

def document_mask(lengths, length_total):
    bounds = jnp.cumsum(lengths).astype(jnp.int32)
    position = jnp.arange(length_total, dtype=jnp.int32)
    doc_index = lax.optimization_barrier(jnp.sum((position[:, None] >= bounds[None, :]).astype(jnp.int32), 1)).astype(jnp.int32)
    same_doc = doc_index[:, None] == doc_index[None, :]
    causal = position[:, None] >= position[None, :]
    return jnp.logical_and(same_doc, causal)

def slot_ranks(expert_ids, expert_count):
    one_hot = (expert_ids[:, None] == jnp.arange(expert_count, dtype=jnp.int32)[None, :]).astype(jnp.int32)
    earlier = jnp.cumsum(one_hot, 0).astype(jnp.int32) - one_hot
    return lax.optimization_barrier(jnp.sum(earlier * one_hot, 1)).astype(jnp.int32)

def reference(tokens_in, token_ids, hash_table, doc_lengths, gain_one, shift_one, project_in, project_out, gain_two, shift_two, expert_in, expert_out, out_grad):
    device_count = TOKENS // TOK_DEV
    expert_ids = hash_table[token_ids].astype(jnp.int32).reshape(device_count, TOK_DEV)
    slot_rank = jax.vmap(lambda expert_row: slot_ranks(expert_row, EXPERTS))(expert_ids)
    slot_row = (jnp.arange(device_count, dtype=jnp.int32)[:, None] * CAP + slot_rank).reshape(-1).astype(jnp.int32)
    expert_flat = expert_ids.reshape(-1)
    masks = jax.vmap(lambda lengths: document_mask(lengths, TOK_DEV))(doc_lengths)
    score_scale = 1.0 / math.sqrt(D // HEADS)

    def attend_block(members):
        joined, attend_mask = members
        query_rows = joined[:, :D].reshape(TOK_DEV, HEADS, -1)
        key_rows = joined[:, D:2 * D].reshape(TOK_DEV, HEADS, -1)
        value_rows = joined[:, 2 * D:].reshape(TOK_DEV, HEADS, -1)
        scores = low_back(jnp.einsum('qhd,khd->hqk', query_rows, key_rows, precision=HIGHEST) * score_scale)
        scores = jnp.where(attend_mask[None], scores, NEG_LARGE)
        weights = low(jax.nn.softmax(scores, -1))
        mixture = jnp.einsum('hqk,khd->qhd', weights, value_rows, precision=HIGHEST)
        return mixture.reshape(TOK_DEV, D)

    def expert_block(members):
        routed_rows, first_weight, second_weight = members
        pre_act = low_back(jnp.dot(routed_rows, first_weight, precision=HIGHEST))
        activation = low(jax.nn.gelu(pre_act, approximate=True))
        return low_back(low(jnp.dot(activation, second_weight, precision=HIGHEST)))

    def forward(inputs, gain_a, shift_a, proj_in, proj_out, gain_b, shift_b, first_all, second_all):
        normed = low(layer_norm(inputs, gain_a, shift_a))
        joined = low_back(low(jnp.dot(normed, proj_in, precision=HIGHEST)))
        mixture = lax.map(jax.checkpoint(attend_block), (joined.reshape(device_count, TOK_DEV, 3 * D), masks))
        mixture = low_back(low(mixture.reshape(TOKENS, D)))
        hidden = inputs + low_back(jnp.dot(mixture, proj_out, precision=HIGHEST))
        routed = low_back(low(layer_norm(hidden, gain_b, shift_b)))
        buffer = jnp.zeros((EXPERTS, device_count * CAP, D), routed.dtype).at[expert_flat, slot_row].set(routed)
        results = lax.map(jax.checkpoint(expert_block), (buffer, first_all, second_all))
        return hidden + results[expert_flat, slot_row]
    primal = (tokens_in.astype(jnp.float32), gain_one, shift_one, project_in.astype(jnp.float32), project_out.astype(jnp.float32), gain_two, shift_two, expert_in.astype(jnp.float32), expert_out.astype(jnp.float32))
    block_sum, pullback = jax.vjp(forward, *primal)
    grads = pullback(out_grad.astype(jnp.float32))
    return (block_sum.astype(jnp.bfloat16), grads[0], grads[3], grads[4], grads[1], grads[2], grads[5], grads[6], grads[7], grads[8])
```

```python
import math

import jax
import jax.numpy as jnp
from jax import lax
from jax.sharding import PartitionSpec as P

HEADS = 16


NEG_LARGE = -1e30
EPSILON = 1e-05


def layer_norm(values, gain_vec, shift_vec):
    center = jnp.mean(values, -1, keepdims=True)
    centered = values - center
    spread = jnp.mean(centered * centered, -1, keepdims=True)
    return centered * lax.rsqrt(spread + EPSILON) * gain_vec + shift_vec


def smooth_gate(values):
    return jax.nn.gelu(values, approximate=True)


def document_mask(lengths, length_total):
    bounds = jnp.cumsum(lengths)
    position = jnp.arange(length_total, dtype=jnp.int32)
    doc_index = jnp.sum((position[:, None] >= bounds[None, :]).astype(jnp.int32), 1)
    same_doc = doc_index[:, None] == doc_index[None, :]
    causal = position[:, None] >= position[None, :]
    return jnp.logical_and(same_doc, causal)


def slot_ranks(expert_ids, expert_count):
    one_hot = (expert_ids[:, None] == jnp.arange(expert_count, dtype=jnp.int32)[None, :]).astype(
        jnp.int32
    )
    earlier = jnp.cumsum(one_hot, 0) - one_hot
    return jnp.sum(earlier * one_hot, 1)


def split_heads(matrix, group_count):
    tok_rows = matrix.shape[0]
    return jnp.moveaxis(matrix.reshape(tok_rows, group_count, 4, -1), 1, 0)


def join_heads(pieces):
    regrouped = jnp.moveaxis(pieces, 0, 1)
    return regrouped.reshape(regrouped.shape[0], -1)


def masked_scores(query_part, key_part, attend_mask, score_scale):
    scores = (
        jnp.einsum("qhd,khd->hqk", query_part, key_part, preferred_element_type=jnp.float32)
        * score_scale
    )
    return jnp.where(attend_mask[None], scores, NEG_LARGE)


def attend_forward(query_heads, key_heads, value_heads, attend_mask, score_scale):

    def head_group(members):
        query_part, key_part, value_part = members
        scores = masked_scores(query_part, key_part, attend_mask, score_scale)
        row_max = jnp.max(scores, -1, keepdims=True)
        exponent = jnp.exp(scores - row_max)
        row_total = jnp.sum(exponent, -1, keepdims=True)
        weights_low = (exponent / row_total).astype(jnp.bfloat16)
        mixture = jnp.einsum(
            "hqk,khd->qhd", weights_low, value_part, preferred_element_type=jnp.float32
        )
        return (mixture.astype(jnp.bfloat16), (row_max + jnp.log(row_total))[..., 0])

    return lax.map(head_group, (query_heads, key_heads, value_heads))


def attend_backward(
    query_heads, key_heads, value_heads, grad_heads, log_totals, attend_mask, score_scale
):

    def head_group(members):
        query_part, key_part, value_part, grad_part, total_part = members
        scores = masked_scores(query_part, key_part, attend_mask, score_scale)
        weights = jnp.exp(scores - total_part[..., None])
        grad_weights = jnp.einsum(
            "qhd,khd->hqk", grad_part, value_part, preferred_element_type=jnp.float32
        )
        grad_scores = (
            weights * (grad_weights - jnp.sum(weights * grad_weights, -1, keepdims=True))
        ).astype(jnp.bfloat16)
        grad_query = (
            jnp.einsum("hqk,khd->qhd", grad_scores, key_part, preferred_element_type=jnp.float32)
            * score_scale
        )
        grad_key = (
            jnp.einsum("hqk,qhd->khd", grad_scores, query_part, preferred_element_type=jnp.float32)
            * score_scale
        )
        grad_value = jnp.einsum(
            "hqk,qhd->khd",
            weights.astype(jnp.bfloat16),
            grad_part,
            preferred_element_type=jnp.float32,
        )
        return (grad_query, grad_key, grad_value)

    return lax.map(head_group, (query_heads, key_heads, value_heads, grad_heads, log_totals))


def gather_slots(slot_hot, buffer):
    rows = buffer.reshape(-1, buffer.shape[-1])
    return jnp.einsum("st,sd->td", slot_hot, rows, preferred_element_type=jnp.float32)


def scatter_sum(parts):
    rep_size, ep_size = lax.axis_size("rep"), lax.axis_size("ep")
    rows, width = parts.shape
    tile = rows // (rep_size * ep_size)
    parts = jnp.swapaxes(parts.reshape(rep_size, ep_size, tile, width), 0, 1)
    parts = parts.reshape(rows, width)
    parts = lax.psum_scatter(parts, "ep", scatter_dimension=0, tiled=True)
    return lax.psum_scatter(parts, "rep", scatter_dimension=0, tiled=True)


def local(
    tokens_in,
    token_ids,
    hash_table,
    doc_lengths,
    gain_one,
    shift_one,
    project_in,
    project_out,
    gain_two,
    shift_two,
    expert_in,
    expert_out,
    out_grad,
):
    tok_rows, model_width = tokens_in.shape
    group_count = HEADS // 4
    score_scale = 1.0 / math.sqrt(model_width // HEADS)
    expert_count = expert_in.shape[0] * lax.axis_size("ep")
    capacity = 2 * tok_rows // expert_count
    inputs = tokens_in.astype(jnp.float32)
    expert_ids = jnp.take(hash_table, token_ids)
    slot_rank = slot_ranks(expert_ids, expert_count)
    slot_of = expert_ids * capacity + slot_rank
    slot_hot = (
        jnp.arange(expert_count * capacity, dtype=jnp.int32)[:, None] == slot_of[None, :]
    ).astype(jnp.bfloat16)
    grad_buffer = (
        jnp.dot(slot_hot, out_grad, preferred_element_type=jnp.float32)
        .astype(jnp.bfloat16)
        .reshape(expert_count, capacity, model_width)
    )
    grad_received = lax.all_to_all(grad_buffer, "ep", split_axis=0, concat_axis=0, tiled=True)
    attend_mask = document_mask(doc_lengths[0], tok_rows)
    normed_one, pull_one = jax.vjp(layer_norm, inputs, gain_one, shift_one)
    normed_one_low = normed_one.astype(jnp.bfloat16)
    joined = jnp.dot(normed_one_low, project_in, preferred_element_type=jnp.float32).astype(
        jnp.bfloat16
    )
    query_heads = split_heads(joined[:, :model_width], group_count)
    key_heads = split_heads(joined[:, model_width : 2 * model_width], group_count)
    value_heads = split_heads(joined[:, 2 * model_width :], group_count)
    mixture_heads, log_totals = attend_forward(
        query_heads, key_heads, value_heads, attend_mask, score_scale
    )
    mixture = join_heads(mixture_heads)
    hidden = inputs + jnp.dot(mixture, project_out, preferred_element_type=jnp.float32)
    normed_two, pull_two = jax.vjp(layer_norm, hidden, gain_two, shift_two)
    routed = normed_two.astype(jnp.bfloat16)
    dispatch_buffer = jnp.dot(
        slot_hot, routed, preferred_element_type=jnp.float32
    ).astype(jnp.bfloat16).reshape(expert_count, capacity, model_width)
    first_weight = expert_in[0]
    second_weight = expert_out[0]
    received = lax.all_to_all(dispatch_buffer, "ep", split_axis=0, concat_axis=0, tiled=True)
    pre_act = jnp.einsum("scd,df->scf", received, first_weight, preferred_element_type=jnp.float32)
    gate_value, gate_pull = jax.vjp(smooth_gate, pre_act)
    activation = gate_value.astype(jnp.bfloat16)
    grad_second = jnp.einsum(
        "scf,scd->fd", activation, grad_received, preferred_element_type=jnp.float32
    )
    grad_act = jnp.einsum(
        "scd,fd->scf", grad_received, second_weight, preferred_element_type=jnp.float32
    )
    grad_pre = gate_pull(grad_act)[0].astype(jnp.bfloat16)
    grad_first = jnp.einsum("scd,scf->df", received, grad_pre, preferred_element_type=jnp.float32)
    grad_routed = jnp.einsum(
        "scf,df->scd", grad_pre, first_weight, preferred_element_type=jnp.float32
    ).astype(jnp.bfloat16)
    grad_back = lax.all_to_all(grad_routed, "ep", split_axis=0, concat_axis=0, tiled=True)
    result = jnp.einsum(
        "scf,fd->scd", activation, second_weight, preferred_element_type=jnp.float32
    ).astype(jnp.bfloat16)
    returned = lax.all_to_all(result, "ep", split_axis=0, concat_axis=0, tiled=True)
    block_out = (hidden + gather_slots(slot_hot, returned)).astype(jnp.bfloat16)
    grad_out = out_grad.astype(jnp.float32)
    grad_normed_two = gather_slots(slot_hot, grad_back)
    hidden_part, grad_gain_two, grad_shift_two = pull_two(grad_normed_two)
    grad_hidden = grad_out + hidden_part
    grad_hidden_low = grad_hidden.astype(jnp.bfloat16)
    grad_project_out = jnp.einsum(
        "td,te->de", mixture, grad_hidden_low, preferred_element_type=jnp.float32
    )
    grad_mixture = jnp.einsum(
        "te,de->td", grad_hidden_low, project_out, preferred_element_type=jnp.float32
    ).astype(jnp.bfloat16)
    grad_heads = split_heads(grad_mixture, group_count)
    grad_query, grad_key, grad_value = attend_backward(
        query_heads, key_heads, value_heads, grad_heads, log_totals, attend_mask, score_scale
    )
    grad_joined = jnp.concatenate(
        [join_heads(grad_query), join_heads(grad_key), join_heads(grad_value)], 1
    ).astype(jnp.bfloat16)
    grad_project_in = jnp.einsum(
        "td,te->de", normed_one_low, grad_joined, preferred_element_type=jnp.float32
    )
    grad_normed_one = jnp.einsum(
        "te,de->td", grad_joined, project_in, preferred_element_type=jnp.float32
    )
    input_part, grad_gain_one, grad_shift_one = pull_one(grad_normed_one)
    grad_in = grad_hidden + input_part
    summed_first, summed_second = (
        lax.psum_scatter(
            grad_first[None].astype(jnp.bfloat16), "rep", scatter_dimension=1, tiled=True
        ).astype(jnp.float32),
        lax.psum_scatter(
            grad_second[None].astype(jnp.bfloat16), "rep", scatter_dimension=1, tiled=True
        ).astype(jnp.float32),
    )
    small = jnp.stack([grad_gain_one, grad_shift_one, grad_gain_two, grad_shift_two], 1)
    small = jnp.pad(small, ((0, 0), (0, 124))).astype(jnp.bfloat16)
    dense = jnp.concatenate(
        [grad_project_in.astype(jnp.bfloat16), grad_project_out.astype(jnp.bfloat16), small], 1
    )
    summed = scatter_sum(dense).astype(jnp.float32)
    return (
        block_out,
        grad_in,
        summed[:, : 3 * model_width],
        summed[:, 3 * model_width : 4 * model_width],
        summed[:, 4 * model_width],
        summed[:, 4 * model_width + 1],
        summed[:, 4 * model_width + 2],
        summed[:, 4 * model_width + 3],
        summed_first,
        summed_second,
    )


def solution(mesh):
    in_specs = (
        P(("rep", "ep"), None),
        P(("rep", "ep")),
        P(),
        P(("rep", "ep"), None),
        P(),
        P(),
        P(),
        P(),
        P(),
        P(),
        P("ep", None, None),
        P("ep", None, None),
        P(("rep", "ep"), None),
    )
    out_specs = (
        P(("rep", "ep"), None),
        P(("rep", "ep"), None),
        P(("rep", "ep"), None),
        P(("rep", "ep"), None),
        P(("rep", "ep")),
        P(("rep", "ep")),
        P(("rep", "ep")),
        P(("rep", "ep")),
        P("ep", "rep", None),
        P("ep", "rep", None),
    )
    return jax.shard_map(local, mesh=mesh, in_specs=in_specs, out_specs=out_specs, check_vma=False)
```

```python
import functools
import math

import jax
import jax.numpy as jnp
from jax import lax
from jax.experimental import pallas as pl
from jax.experimental.pallas import tpu as pltpu
from jax.sharding import PartitionSpec as P

HEADS = 16
GROUP = 4
LANES = 128
NEG_LARGE = -1e30
EPSILON = 1e-05
BF16 = jnp.bfloat16
F32 = jnp.float32


def dot_nn(a, b):
    return lax.dot_general(a, b, (((1,), (0,)), ((), ())), preferred_element_type=F32)


def dot_nt(a, b):
    return lax.dot_general(a, b, (((1,), (1,)), ((), ())), preferred_element_type=F32)


def dot_tn(a, b):
    return lax.dot_general(a, b, (((0,), (0,)), ((), ())), preferred_element_type=F32)


def iota(shape, axis):
    return lax.broadcasted_iota(jnp.int32, shape, axis)


def whole(shape):
    return pl.BlockSpec(shape, lambda *_: (0,) * len(shape))


def norm_parts(values):
    center = jnp.mean(values, -1, keepdims=True)
    centered = values - center
    spread = jnp.mean(centered * centered, -1, keepdims=True)
    factor = lax.rsqrt(spread + EPSILON)
    return centered * factor, factor


def norm_back(grad, gain, xhat, factor):
    scaled = grad * gain
    mean_scaled = jnp.mean(scaled, -1, keepdims=True)
    mean_cross = jnp.mean(scaled * xhat, -1, keepdims=True)
    return factor * (scaled - mean_scaled - xhat * mean_cross)


def slot_matrix(slot_row, slot_total):
    tok_rows = slot_row.shape[1]
    return (iota((slot_total, tok_rows), 0) == slot_row).astype(F32).astype(BF16)


def route_kernel(expert_count, capacity, ids_ref, table_ref, grad_ref, slot_ref, buffer_ref):
    tok_rows = ids_ref.shape[1]
    ids = ids_ref[...]
    table_rows = table_ref.shape[0]
    high = ids // LANES
    low = ids - high * LANES
    high_hot = (iota((table_rows, tok_rows), 0) == high).astype(F32).astype(BF16)
    picked = dot_tn(table_ref[...].astype(F32).astype(BF16), high_hot)
    low_hot = iota((LANES, tok_rows), 0) == low
    expert = jnp.sum(jnp.where(low_hot, picked, 0.0), 0, keepdims=True).astype(jnp.int32)
    expert_hot = (iota((expert_count, tok_rows), 0) == expert).astype(F32)
    before = (iota((tok_rows, tok_rows), 0) < iota((tok_rows, tok_rows), 1)).astype(F32)
    earlier = dot_nn(expert_hot.astype(BF16), before.astype(BF16))
    rank = jnp.sum(earlier * expert_hot, 0, keepdims=True).astype(jnp.int32)
    slot = expert * capacity + rank
    slot_ref[...] = slot
    slot_hot = slot_matrix(slot, expert_count * capacity)
    buffer_ref[...] = dot_nn(slot_hot, grad_ref[...]).astype(BF16)


def route(token_ids, hash_table, out_grad, expert_count, capacity):
    tok_rows, width = out_grad.shape
    slot_total = expert_count * capacity
    table_rows = hash_table.shape[0] // LANES
    return pl.pallas_call(
        functools.partial(route_kernel, expert_count, capacity),
        out_shape=(
            jax.ShapeDtypeStruct((1, tok_rows), jnp.int32),
            jax.ShapeDtypeStruct((slot_total, width), BF16),
        ),
        cost_estimate=pl.CostEstimate(
            flops=2 * slot_total * tok_rows * width, bytes_accessed=4 << 20, transcendentals=0
        ),
        name="route",
    )(token_ids.reshape(1, tok_rows), hash_table.reshape(table_rows, LANES), out_grad)


def front_kernel(
    slot_total,
    head_size,
    lengths_ref,
    tokens_ref,
    slot_ref,
    gain_one_ref,
    shift_one_ref,
    query_weight_ref,
    key_weight_ref,
    value_weight_ref,
    out_weight_ref,
    gain_two_ref,
    shift_two_ref,
    normed_ref,
    query_ref,
    key_ref,
    value_ref,
    probs_ref,
    mixture_ref,
    hidden_ref,
    buffer_ref,
    mask_ref,
):
    step = pl.program_id(0)
    tok_rows = tokens_ref.shape[0]
    group_width = query_ref.shape[1]

    @pl.when(step == 0)
    def _():
        inputs = tokens_ref[...].astype(F32)
        xhat, _ = norm_parts(inputs)
        normed_ref[...] = (xhat * gain_one_ref[...] + shift_one_ref[...]).astype(BF16)
        position = iota((1, tok_rows), 1)
        start = jnp.zeros((1, tok_rows), jnp.int32)
        bound = jnp.int32(0)
        for index in range(lengths_ref.shape[1]):
            bound = bound + lengths_ref[0, index]
            start = jnp.where(position >= bound, bound, start)
        key_position = iota((tok_rows, tok_rows), 0)
        allowed = jnp.logical_and(key_position >= start, key_position <= position)
        mask_ref[...] = jnp.where(allowed, 0.0, NEG_LARGE)
        hidden_ref[...] = inputs

    normed = normed_ref[...]
    query = dot_nn(normed, query_weight_ref[...]).astype(BF16)
    key = dot_nn(normed, key_weight_ref[...]).astype(BF16)
    value = dot_nn(normed, value_weight_ref[...]).astype(BF16)
    query_ref[...] = query
    key_ref[...] = key
    value_ref[...] = value
    lane_head = iota((1, group_width), 1) // head_size
    scale = 1.0 / math.sqrt(head_size)
    total = jnp.zeros((tok_rows, group_width), F32)
    for head in range(GROUP):
        chosen = lane_head == head
        key_part = key * jnp.where(chosen, scale, 0.0).astype(BF16)
        value_part = value * jnp.where(chosen, 1.0, 0.0).astype(BF16)
        scores = dot_nt(key_part, query) + mask_ref[...]
        exponent = jnp.exp(scores - jnp.max(scores, 0, keepdims=True))
        inverse = 1.0 / jnp.sum(exponent, 0, keepdims=True)
        weights = (exponent * inverse).astype(BF16)
        probs_ref[head] = weights
        total = total + dot_tn(weights, value_part)
    mixture = total.astype(BF16)
    mixture_ref[...] = mixture
    hidden_ref[...] += dot_nn(mixture, out_weight_ref[...])

    @pl.when(step == pl.num_programs(0) - 1)
    def _():
        xhat, _ = norm_parts(hidden_ref[...])
        routed = (xhat * gain_two_ref[...] + shift_two_ref[...]).astype(BF16)
        slot_hot = slot_matrix(slot_ref[...], slot_total)
        buffer_ref[...] = dot_nn(slot_hot, routed).astype(BF16)


def front(
    doc_lengths,
    tokens_in,
    slot_row,
    gain_one,
    shift_one,
    project_in,
    project_out,
    gain_two,
    shift_two,
    slot_total,
):
    tok_rows, width = tokens_in.shape
    head_size = width // HEADS
    group_width = GROUP * head_size
    steps = HEADS // GROUP
    vector = whole((1, width))

    def weight_spec(part):
        return pl.BlockSpec((width, group_width), lambda step: (0, part * steps + step))

    column_spec = pl.BlockSpec((tok_rows, group_width), lambda step: (0, step))
    return pl.pallas_call(
        functools.partial(front_kernel, slot_total, head_size),
        grid=(steps,),
        in_specs=[
            pl.BlockSpec(memory_space=pltpu.SMEM),
            whole((tok_rows, width)),
            whole((1, tok_rows)),
            vector,
            vector,
            weight_spec(0),
            weight_spec(1),
            weight_spec(2),
            pl.BlockSpec((group_width, width), lambda step: (step, 0)),
            vector,
            vector,
        ],
        out_specs=(
            whole((tok_rows, width)),
            column_spec,
            column_spec,
            column_spec,
            pl.BlockSpec((GROUP, tok_rows, tok_rows), lambda step: (step, 0, 0)),
            column_spec,
            whole((tok_rows, width)),
            whole((slot_total, width)),
        ),
        out_shape=(
            jax.ShapeDtypeStruct((tok_rows, width), BF16),
            jax.ShapeDtypeStruct((tok_rows, width), BF16),
            jax.ShapeDtypeStruct((tok_rows, width), BF16),
            jax.ShapeDtypeStruct((tok_rows, width), BF16),
            jax.ShapeDtypeStruct((HEADS, tok_rows, tok_rows), BF16),
            jax.ShapeDtypeStruct((tok_rows, width), BF16),
            jax.ShapeDtypeStruct((tok_rows, width), F32),
            jax.ShapeDtypeStruct((slot_total, width), BF16),
        ),
        scratch_shapes=[pltpu.VMEM((tok_rows, tok_rows), F32)],
        cost_estimate=pl.CostEstimate(
            flops=14 * 10**9, bytes_accessed=30 << 20, transcendentals=1 << 22
        ),
        name="front",
    )(
        doc_lengths,
        tokens_in,
        slot_row,
        gain_one.reshape(1, width),
        shift_one.reshape(1, width),
        project_in,
        project_in,
        project_in,
        project_out,
        gain_two.reshape(1, width),
        shift_two.reshape(1, width),
    )


def back_kernel(
    head_size,
    buffer_ref,
    slot_ref,
    hidden_ref,
    gain_two_ref,
    out_grad_ref,
    mixture_ref,
    out_weight_ref,
    query_ref,
    key_ref,
    value_ref,
    probs_ref,
    normed_ref,
    query_weight_ref,
    key_weight_ref,
    value_weight_ref,
    tokens_ref,
    gain_one_ref,
    dense_ref,
    small_ref,
    grad_in_ref,
    hidden_low_ref,
    normed_grad_ref,
):
    step = pl.program_id(0)
    width = tokens_ref.shape[1]
    group_width = query_ref.shape[1]

    @pl.when(step == 0)
    def _():
        slot_hot = slot_matrix(slot_ref[...], buffer_ref.shape[0])
        grad_routed = dot_tn(slot_hot, buffer_ref[...])
        xhat, factor = norm_parts(hidden_ref[...])
        small_ref[0:1, :] = jnp.sum(grad_routed * xhat, 0, keepdims=True)
        small_ref[1:2, :] = jnp.sum(grad_routed, 0, keepdims=True)
        grad_hidden = out_grad_ref[...].astype(F32) + norm_back(
            grad_routed, gain_two_ref[...], xhat, factor
        )
        grad_in_ref[...] = grad_hidden
        hidden_low_ref[...] = grad_hidden.astype(BF16)
        normed_grad_ref[...] = jnp.zeros_like(normed_grad_ref)

    hidden_low = hidden_low_ref[...]
    dense_ref[pl.ds(pl.multiple_of(step * group_width, group_width), group_width), 3 * width :] = (
        dot_tn(mixture_ref[...], hidden_low).astype(BF16)
    )
    grad_mixture = dot_nt(hidden_low, out_weight_ref[...]).astype(BF16)
    query, key, value = query_ref[...], key_ref[...], value_ref[...]
    lane_head = iota((1, group_width), 1) // head_size
    scale = 1.0 / math.sqrt(head_size)
    grad_query = jnp.zeros(query.shape, F32)
    grad_key = jnp.zeros(query.shape, F32)
    grad_value = jnp.zeros(query.shape, F32)
    for head in range(GROUP):
        chosen = jnp.where(lane_head == head, 1.0, 0.0).astype(BF16)
        scaled = jnp.where(lane_head == head, scale, 0.0).astype(BF16)
        grad_part = grad_mixture * chosen
        weights_low = probs_ref[head]
        weights = weights_low.astype(F32)
        grad_weights = dot_nt(value, grad_part)
        inner = jnp.sum(weights * grad_weights, 0, keepdims=True)
        grad_scores = (weights * (grad_weights - inner)).astype(BF16)
        grad_query = grad_query + dot_tn(grad_scores, key * scaled)
        grad_key = grad_key + dot_nn(grad_scores, query * scaled)
        grad_value = grad_value + dot_nn(weights_low, grad_part)
    normed = normed_ref[...]
    for part, (grad, weight_ref) in enumerate(
        (
            (grad_query, query_weight_ref),
            (grad_key, key_weight_ref),
            (grad_value, value_weight_ref),
        )
    ):
        grad = grad.astype(BF16)
        column = pl.multiple_of(part * width + step * group_width, group_width)
        dense_ref[:, pl.ds(column, group_width)] = dot_tn(normed, grad).astype(BF16)
        normed_grad_ref[...] += dot_nt(grad, weight_ref[...])

    @pl.when(step == pl.num_programs(0) - 1)
    def _():
        grad_normed = normed_grad_ref[...]
        xhat, factor = norm_parts(tokens_ref[...].astype(F32))
        small_ref[2:3, :] = jnp.sum(grad_normed * xhat, 0, keepdims=True)
        small_ref[3:4, :] = jnp.sum(grad_normed, 0, keepdims=True)
        small_ref[4:8, :] = jnp.zeros((4, width), F32)
        grad_in_ref[...] += norm_back(grad_normed, gain_one_ref[...], xhat, factor)


def back(
    grad_buffer,
    slot_row,
    hidden,
    gain_two,
    out_grad,
    mixture,
    project_out,
    query,
    key,
    value,
    probs,
    normed,
    project_in,
    tokens_in,
    gain_one,
):
    tok_rows, width = tokens_in.shape
    head_size = width // HEADS
    group_width = GROUP * head_size
    steps = HEADS // GROUP
    vector = whole((1, width))
    tokens_spec = whole((tok_rows, width))

    def weight_spec(part):
        return pl.BlockSpec((width, group_width), lambda step: (0, part * steps + step))

    column_spec = pl.BlockSpec((tok_rows, group_width), lambda step: (0, step))
    return pl.pallas_call(
        functools.partial(back_kernel, head_size),
        grid=(steps,),
        in_specs=[
            whole(grad_buffer.shape),
            whole((1, tok_rows)),
            tokens_spec,
            vector,
            tokens_spec,
            column_spec,
            pl.BlockSpec((group_width, width), lambda step: (step, 0)),
            column_spec,
            column_spec,
            column_spec,
            pl.BlockSpec((GROUP, tok_rows, tok_rows), lambda step: (step, 0, 0)),
            tokens_spec,
            weight_spec(0),
            weight_spec(1),
            weight_spec(2),
            tokens_spec,
            vector,
        ],
        out_specs=(
            whole((width, 4 * width)),
            whole((8, width)),
            tokens_spec,
        ),
        out_shape=(
            jax.ShapeDtypeStruct((width, 4 * width), BF16),
            jax.ShapeDtypeStruct((8, width), F32),
            jax.ShapeDtypeStruct((tok_rows, width), F32),
        ),
        scratch_shapes=[
            pltpu.VMEM((tok_rows, width), BF16),
            pltpu.VMEM((tok_rows, width), F32),
        ],
        cost_estimate=pl.CostEstimate(
            flops=24 * 10**9, bytes_accessed=50 << 20, transcendentals=0
        ),
        name="back",
    )(
        grad_buffer,
        slot_row,
        hidden,
        gain_two.reshape(1, width),
        out_grad,
        mixture,
        project_out,
        query,
        key,
        value,
        probs,
        normed,
        project_in,
        project_in,
        project_in,
        tokens_in,
        gain_one.reshape(1, width),
    )


def finish_kernel(hidden_ref, slot_ref, buffer_ref, out_ref):
    slot_hot = slot_matrix(slot_ref[...], buffer_ref.shape[0])
    out_ref[...] = (hidden_ref[...] + dot_tn(slot_hot, buffer_ref[...])).astype(BF16)


def finish(hidden, slot_row, buffer):
    return pl.pallas_call(
        finish_kernel,
        out_shape=jax.ShapeDtypeStruct(hidden.shape, BF16),
        cost_estimate=pl.CostEstimate(
            flops=10**9, bytes_accessed=5 << 20, transcendentals=0
        ),
        name="finish",
    )(hidden, slot_row, buffer)


def exchange(buffer, expert_count):
    shape = buffer.shape
    buffer = buffer.reshape(expert_count, shape[0] // expert_count, shape[1])
    buffer = lax.all_to_all(buffer, "ep", split_axis=0, concat_axis=0, tiled=True)
    return buffer.reshape(shape)


def smooth_gate(values):
    return jax.nn.gelu(values, approximate=True)


def local(
    tokens_in,
    token_ids,
    hash_table,
    doc_lengths,
    gain_one,
    shift_one,
    project_in,
    project_out,
    gain_two,
    shift_two,
    expert_in,
    expert_out,
    out_grad,
):
    tok_rows, width = tokens_in.shape
    expert_count = expert_in.shape[0] * lax.axis_size("ep")
    capacity = 2 * tok_rows // expert_count
    slot_total = expert_count * capacity
    first_weight, second_weight = expert_in[0], expert_out[0]

    slot_row, grad_buffer = route(token_ids, hash_table, out_grad, expert_count, capacity)
    grad_received = exchange(grad_buffer, expert_count)
    normed, query, key, value, probs, mixture, hidden, buffer = front(
        doc_lengths,
        tokens_in,
        slot_row,
        gain_one,
        shift_one,
        project_in,
        project_out,
        gain_two,
        shift_two,
        slot_total,
    )
    received = exchange(buffer, expert_count)
    grad_act = jnp.einsum("sd,fd->sf", grad_received, second_weight, preferred_element_type=F32)
    grad_act = grad_act.astype(BF16)
    pre_act = jnp.einsum("sd,df->sf", received, first_weight, preferred_element_type=F32)
    gate_value, gate_pull = jax.vjp(smooth_gate, pre_act)
    activation = gate_value.astype(BF16)
    grad_pre = gate_pull(grad_act.astype(F32))[0].astype(BF16)
    grad_routed = jnp.einsum(
        "sf,df->sd", grad_pre, first_weight, preferred_element_type=F32
    ).astype(BF16)
    grad_back = exchange(grad_routed, expert_count)
    grad_second = jnp.einsum(
        "sf,sd->fd", activation, grad_received, preferred_element_type=F32
    ).astype(BF16)
    grad_first = jnp.einsum("sd,sf->df", received, grad_pre, preferred_element_type=F32).astype(
        BF16
    )
    summed_second = lax.psum_scatter(grad_second, "rep", scatter_dimension=0, tiled=True)
    summed_first = lax.psum_scatter(grad_first, "rep", scatter_dimension=0, tiled=True)
    result = jnp.einsum(
        "sf,fd->sd", activation, second_weight, preferred_element_type=F32
    ).astype(BF16)
    grad_back, grad_second, grad_first, result = lax.optimization_barrier(
        (grad_back, grad_second, grad_first, result)
    )
    returned = exchange(result, expert_count)
    dense, small, grad_in = back(
        grad_back,
        slot_row,
        hidden,
        gain_two,
        out_grad,
        mixture,
        project_out,
        query,
        key,
        value,
        probs,
        normed,
        project_in,
        tokens_in,
        gain_one,
    )
    columns = jnp.pad(small, ((0, LANES - small.shape[0]), (0, 0))).T.astype(BF16)
    dense = jnp.concatenate([dense, columns], 1)
    dense = lax.psum_scatter(dense, "rep", scatter_dimension=0, tiled=True)
    dense = lax.psum_scatter(dense, "ep", scatter_dimension=0, tiled=True).astype(F32)
    block_out = finish(hidden, slot_row, returned)
    return (
        block_out,
        grad_in,
        dense[:, : 3 * width],
        dense[:, 3 * width : 4 * width],
        dense[:, 4 * width + 2],
        dense[:, 4 * width + 3],
        dense[:, 4 * width],
        dense[:, 4 * width + 1],
        summed_first.astype(F32)[None],
        summed_second.astype(F32)[None],
    )


def solution(mesh):
    in_specs = (
        P(("rep", "ep"), None),
        P(("rep", "ep")),
        P(),
        P(("rep", "ep"), None),
        P(),
        P(),
        P(),
        P(),
        P(),
        P(),
        P("ep", None, None),
        P("ep", None, None),
        P(("rep", "ep"), None),
    )
    out_specs = (
        P(("rep", "ep"), None),
        P(("rep", "ep"), None),
        P(("rep", "ep"), None),
        P(("rep", "ep"), None),
        P(("rep", "ep")),
        P(("rep", "ep")),
        P(("rep", "ep")),
        P(("rep", "ep")),
        P("ep", "rep", None),
        P("ep", "rep", None),
    )
    return jax.shard_map(local, mesh=mesh, in_specs=in_specs, out_specs=out_specs, check_vma=False)
```

```python
import functools
import math

import jax
import jax.numpy as jnp
from jax import lax
from jax.experimental import pallas as pl
from jax.experimental.pallas import tpu as pltpu
from jax.sharding import PartitionSpec as P

HEADS = 16
GROUP = 4
LANES = 128
NEG_LARGE = -1e30
EPSILON = 1e-05
BF16 = jnp.bfloat16
F32 = jnp.float32
GATE_A = math.sqrt(2.0 / math.pi)
GATE_B = GATE_A * 0.044715


def dot_nn(a, b):
    return lax.dot_general(a, b, (((1,), (0,)), ((), ())), preferred_element_type=F32)


def dot_nt(a, b):
    return lax.dot_general(a, b, (((1,), (1,)), ((), ())), preferred_element_type=F32)


def dot_tn(a, b):
    return lax.dot_general(a, b, (((0,), (0,)), ((), ())), preferred_element_type=F32)


def iota(shape, axis):
    return lax.broadcasted_iota(jnp.int32, shape, axis)


def whole(shape):
    return pl.BlockSpec(shape, lambda *_: (0,) * len(shape))


def norm_parts(values):
    center = jnp.mean(values, -1, keepdims=True)
    centered = values - center
    spread = jnp.mean(centered * centered, -1, keepdims=True)
    factor = lax.rsqrt(spread + EPSILON)
    return centered * factor, factor


def norm_back(grad, gain, xhat, factor):
    scaled = grad * gain
    mean_scaled = jnp.mean(scaled, -1, keepdims=True)
    mean_cross = jnp.mean(scaled * xhat, -1, keepdims=True)
    return factor * (scaled - mean_scaled - xhat * mean_cross)


def slot_matrix(slot_row, slot_total):
    tok_rows = slot_row.shape[1]
    return (iota((slot_total, tok_rows), 0) == slot_row).astype(F32).astype(BF16)


def route_kernel(
    expert_count, capacity, flip_ref, ids_ref, table_ref, grad_ref, slot_ref, buffer_ref
):
    tok_rows = ids_ref.shape[1]
    ids = ids_ref[...]
    table_rows = table_ref.shape[0]
    high = ids // LANES
    low = ids - high * LANES
    high_hot = (iota((table_rows, tok_rows), 0) == high).astype(F32).astype(BF16)
    picked = dot_tn(table_ref[...].astype(F32).astype(BF16), high_hot)
    low_hot = iota((LANES, tok_rows), 0) == low
    expert = jnp.sum(jnp.where(low_hot, picked, 0.0), 0, keepdims=True).astype(jnp.int32)
    expert_hot = (iota((expert_count, tok_rows), 0) == expert).astype(F32)
    before = (iota((tok_rows, tok_rows), 0) < iota((tok_rows, tok_rows), 1)).astype(F32)
    earlier = dot_nn(expert_hot.astype(BF16), before.astype(BF16))
    rank = jnp.sum(earlier * expert_hot, 0, keepdims=True).astype(jnp.int32)
    slot = (expert ^ flip_ref[0]) * capacity + rank
    slot_ref[...] = slot
    slot_hot = slot_matrix(slot, expert_count * capacity)
    buffer_ref[...] = dot_nn(slot_hot, grad_ref[...]).astype(BF16)


def route(flip, token_ids, hash_table, out_grad, expert_count, capacity):
    tok_rows, width = out_grad.shape
    slot_total = expert_count * capacity
    table_rows = hash_table.shape[0] // LANES
    return pl.pallas_call(
        functools.partial(route_kernel, expert_count, capacity),
        in_specs=[
            pl.BlockSpec(memory_space=pltpu.SMEM),
            whole((1, tok_rows)),
            whole((table_rows, LANES)),
            whole((tok_rows, width)),
        ],
        out_specs=(whole((1, tok_rows)), whole((slot_total, width))),
        out_shape=(
            jax.ShapeDtypeStruct((1, tok_rows), jnp.int32),
            jax.ShapeDtypeStruct((slot_total, width), BF16),
        ),
        cost_estimate=pl.CostEstimate(
            flops=2 * slot_total * tok_rows * width, bytes_accessed=4 << 20, transcendentals=0
        ),
        name="route",
    )(flip, token_ids.reshape(1, tok_rows), hash_table.reshape(table_rows, LANES), out_grad)


def front_kernel(
    slot_total,
    head_size,
    lengths_ref,
    tokens_ref,
    slot_ref,
    gain_one_ref,
    shift_one_ref,
    query_weight_ref,
    key_weight_ref,
    value_weight_ref,
    out_weight_ref,
    gain_two_ref,
    shift_two_ref,
    normed_ref,
    query_ref,
    key_ref,
    value_ref,
    probs_ref,
    mixture_ref,
    hidden_ref,
    buffer_ref,
    mask_ref,
):
    step = pl.program_id(0)
    tok_rows = tokens_ref.shape[0]
    group_width = query_ref.shape[1]

    @pl.when(step == 0)
    def _():
        inputs = tokens_ref[...].astype(F32)
        xhat, _ = norm_parts(inputs)
        normed_ref[...] = (xhat * gain_one_ref[...] + shift_one_ref[...]).astype(BF16)
        position = iota((1, tok_rows), 1)
        start = jnp.zeros((1, tok_rows), jnp.int32)
        bound = jnp.int32(0)
        for index in range(lengths_ref.shape[1]):
            bound = bound + lengths_ref[0, index]
            start = jnp.where(position >= bound, bound, start)
        key_position = iota((tok_rows, tok_rows), 0)
        allowed = jnp.logical_and(key_position >= start, key_position <= position)
        mask_ref[...] = jnp.where(allowed, 0.0, NEG_LARGE)
        hidden_ref[...] = inputs

    normed = normed_ref[...]
    query = dot_nn(normed, query_weight_ref[...]).astype(BF16)
    key = dot_nn(normed, key_weight_ref[...]).astype(BF16)
    value = dot_nn(normed, value_weight_ref[...]).astype(BF16)
    query_ref[...] = query
    key_ref[...] = key
    value_ref[...] = value
    lane_head = iota((1, group_width), 1) // head_size
    scale = 1.0 / math.sqrt(head_size)
    total = jnp.zeros((tok_rows, group_width), F32)
    for head in range(GROUP):
        chosen = lane_head == head
        key_part = key * jnp.where(chosen, scale, 0.0).astype(BF16)
        value_part = value * jnp.where(chosen, 1.0, 0.0).astype(BF16)
        scores = dot_nt(key_part, query) + mask_ref[...]
        exponent = jnp.exp(scores - jnp.max(scores, 0, keepdims=True))
        inverse = 1.0 / jnp.sum(exponent, 0, keepdims=True)
        weights = (exponent * inverse).astype(BF16)
        probs_ref[head] = weights
        total = total + dot_tn(weights, value_part)
    mixture = total.astype(BF16)
    mixture_ref[...] = mixture
    hidden_ref[...] += dot_nn(mixture, out_weight_ref[...])

    @pl.when(step == pl.num_programs(0) - 1)
    def _():
        xhat, _ = norm_parts(hidden_ref[...])
        routed = (xhat * gain_two_ref[...] + shift_two_ref[...]).astype(BF16)
        slot_hot = slot_matrix(slot_ref[...], slot_total)
        buffer_ref[...] = dot_nn(slot_hot, routed).astype(BF16)


def front(
    doc_lengths,
    tokens_in,
    slot_row,
    gain_one,
    shift_one,
    project_in,
    project_out,
    gain_two,
    shift_two,
    slot_total,
):
    tok_rows, width = tokens_in.shape
    head_size = width // HEADS
    group_width = GROUP * head_size
    steps = HEADS // GROUP
    vector = whole((1, width))

    def weight_spec(part):
        return pl.BlockSpec((width, group_width), lambda step: (0, part * steps + step))

    column_spec = pl.BlockSpec((tok_rows, group_width), lambda step: (0, step))
    return pl.pallas_call(
        functools.partial(front_kernel, slot_total, head_size),
        grid=(steps,),
        in_specs=[
            pl.BlockSpec(memory_space=pltpu.SMEM),
            whole((tok_rows, width)),
            whole((1, tok_rows)),
            vector,
            vector,
            weight_spec(0),
            weight_spec(1),
            weight_spec(2),
            pl.BlockSpec((group_width, width), lambda step: (step, 0)),
            vector,
            vector,
        ],
        out_specs=(
            whole((tok_rows, width)),
            column_spec,
            column_spec,
            column_spec,
            pl.BlockSpec((GROUP, tok_rows, tok_rows), lambda step: (step, 0, 0)),
            column_spec,
            whole((tok_rows, width)),
            whole((slot_total, width)),
        ),
        out_shape=(
            jax.ShapeDtypeStruct((tok_rows, width), BF16),
            jax.ShapeDtypeStruct((tok_rows, width), BF16),
            jax.ShapeDtypeStruct((tok_rows, width), BF16),
            jax.ShapeDtypeStruct((tok_rows, width), BF16),
            jax.ShapeDtypeStruct((HEADS, tok_rows, tok_rows), BF16),
            jax.ShapeDtypeStruct((tok_rows, width), BF16),
            jax.ShapeDtypeStruct((tok_rows, width), F32),
            jax.ShapeDtypeStruct((slot_total, width), BF16),
        ),
        scratch_shapes=[pltpu.VMEM((tok_rows, tok_rows), F32)],
        cost_estimate=pl.CostEstimate(
            flops=14 * 10**9, bytes_accessed=30 << 20, transcendentals=1 << 22
        ),
        name="front",
    )(
        doc_lengths,
        tokens_in,
        slot_row,
        gain_one.reshape(1, width),
        shift_one.reshape(1, width),
        project_in,
        project_in,
        project_in,
        project_out,
        gain_two.reshape(1, width),
        shift_two.reshape(1, width),
    )


def spread_bits(index, layout):
    spot = 0
    for place, bit in enumerate(layout):
        spot = spot | (((index >> bit) & 1) << place)
    return spot


def store_rows(dense_ref, first, column, values, tile, layout, spot):
    for index in range(values.shape[0] // tile):
        place = spread_bits(first + index, layout) ^ spot
        row = pl.multiple_of(place * tile, tile)
        dense_ref[pl.ds(row, tile), column] = values[index * tile : (index + 1) * tile]


def back_kernel(
    head_size,
    tile,
    layout,
    spot_ref,
    buffer_ref,
    slot_ref,
    hidden_ref,
    gain_two_ref,
    out_grad_ref,
    mixture_ref,
    out_weight_ref,
    query_ref,
    key_ref,
    value_ref,
    probs_ref,
    normed_ref,
    query_weight_ref,
    key_weight_ref,
    value_weight_ref,
    tokens_ref,
    gain_one_ref,
    dense_ref,
    grad_in_ref,
    hidden_low_ref,
    normed_grad_ref,
    small_ref,
):
    step = pl.program_id(0)
    width = tokens_ref.shape[1]
    group_width = query_ref.shape[1]

    @pl.when(step == 0)
    def _():
        slot_hot = slot_matrix(slot_ref[...], buffer_ref.shape[0])
        grad_routed = dot_tn(slot_hot, buffer_ref[...])
        xhat, factor = norm_parts(hidden_ref[...])
        small_ref[0:1, :] = jnp.sum(grad_routed * xhat, 0, keepdims=True)
        small_ref[1:2, :] = jnp.sum(grad_routed, 0, keepdims=True)
        grad_hidden = out_grad_ref[...].astype(F32) + norm_back(
            grad_routed, gain_two_ref[...], xhat, factor
        )
        grad_in_ref[...] = grad_hidden
        hidden_low_ref[...] = grad_hidden.astype(BF16)
        normed_grad_ref[...] = jnp.zeros_like(normed_grad_ref)
        small_ref[4:, :] = jnp.zeros((LANES - 4, width), F32)

    hidden_low = hidden_low_ref[...]
    spot = spot_ref[0]
    store_rows(
        dense_ref,
        step * (group_width // tile),
        slice(3 * width, 4 * width),
        dot_tn(mixture_ref[...], hidden_low).astype(BF16),
        tile,
        layout,
        spot,
    )
    grad_mixture = dot_nt(hidden_low, out_weight_ref[...]).astype(BF16)
    query, key, value = query_ref[...], key_ref[...], value_ref[...]
    lane_head = iota((1, group_width), 1) // head_size
    scale = 1.0 / math.sqrt(head_size)
    grad_query = jnp.zeros(query.shape, F32)
    grad_key = jnp.zeros(query.shape, F32)
    grad_value = jnp.zeros(query.shape, F32)
    for head in range(GROUP):
        chosen = jnp.where(lane_head == head, 1.0, 0.0).astype(BF16)
        scaled = jnp.where(lane_head == head, scale, 0.0).astype(BF16)
        grad_part = grad_mixture * chosen
        weights_low = probs_ref[head]
        weights = weights_low.astype(F32)
        grad_weights = dot_nt(value, grad_part)
        inner = jnp.sum(weights * grad_weights, 0, keepdims=True)
        grad_scores = (weights * (grad_weights - inner)).astype(BF16)
        grad_query = grad_query + dot_tn(grad_scores, key * scaled)
        grad_key = grad_key + dot_nn(grad_scores, query * scaled)
        grad_value = grad_value + dot_nn(weights_low, grad_part)
    normed = normed_ref[...]
    for part, (grad, weight_ref) in enumerate(
        (
            (grad_query, query_weight_ref),
            (grad_key, key_weight_ref),
            (grad_value, value_weight_ref),
        )
    ):
        grad = grad.astype(BF16)
        column = pl.multiple_of(part * width + step * group_width, group_width)
        store_rows(
            dense_ref,
            0,
            pl.ds(column, group_width),
            dot_tn(normed, grad).astype(BF16),
            tile,
            layout,
            spot,
        )
        normed_grad_ref[...] += dot_nt(grad, weight_ref[...])

    @pl.when(step == pl.num_programs(0) - 1)
    def _():
        grad_normed = normed_grad_ref[...]
        xhat, factor = norm_parts(tokens_ref[...].astype(F32))
        small_ref[2:3, :] = jnp.sum(grad_normed * xhat, 0, keepdims=True)
        small_ref[3:4, :] = jnp.sum(grad_normed, 0, keepdims=True)
        store_rows(
            dense_ref,
            0,
            slice(4 * width, 4 * width + LANES),
            small_ref[...].T.astype(BF16),
            tile,
            layout,
            spot,
        )
        grad_in_ref[...] += norm_back(grad_normed, gain_one_ref[...], xhat, factor)


def back(
    tile,
    layout,
    spot,
    grad_buffer,
    slot_row,
    hidden,
    gain_two,
    out_grad,
    mixture,
    project_out,
    query,
    key,
    value,
    probs,
    normed,
    project_in,
    tokens_in,
    gain_one,
):
    tok_rows, width = tokens_in.shape
    head_size = width // HEADS
    group_width = GROUP * head_size
    steps = HEADS // GROUP
    vector = whole((1, width))
    tokens_spec = whole((tok_rows, width))

    def weight_spec(part):
        return pl.BlockSpec((width, group_width), lambda step: (0, part * steps + step))

    column_spec = pl.BlockSpec((tok_rows, group_width), lambda step: (0, step))
    return pl.pallas_call(
        functools.partial(back_kernel, head_size, tile, layout),
        grid=(steps,),
        in_specs=[
            pl.BlockSpec(memory_space=pltpu.SMEM),
            whole(grad_buffer.shape),
            whole((1, tok_rows)),
            tokens_spec,
            vector,
            tokens_spec,
            column_spec,
            pl.BlockSpec((group_width, width), lambda step: (step, 0)),
            column_spec,
            column_spec,
            column_spec,
            pl.BlockSpec((GROUP, tok_rows, tok_rows), lambda step: (step, 0, 0)),
            tokens_spec,
            weight_spec(0),
            weight_spec(1),
            weight_spec(2),
            tokens_spec,
            vector,
        ],
        out_specs=(
            whole((width, 4 * width + LANES)),
            tokens_spec,
        ),
        out_shape=(
            jax.ShapeDtypeStruct((width, 4 * width + LANES), BF16),
            jax.ShapeDtypeStruct((tok_rows, width), F32),
        ),
        scratch_shapes=[
            pltpu.VMEM((tok_rows, width), BF16),
            pltpu.VMEM((tok_rows, width), F32),
            pltpu.VMEM((LANES, width), F32),
        ],
        cost_estimate=pl.CostEstimate(
            flops=24 * 10**9, bytes_accessed=50 << 20, transcendentals=0
        ),
        name="back",
    )(
        spot,
        grad_buffer,
        slot_row,
        hidden,
        gain_two.reshape(1, width),
        out_grad,
        mixture,
        project_out,
        query,
        key,
        value,
        probs,
        normed,
        project_in,
        project_in,
        project_in,
        tokens_in,
        gain_one.reshape(1, width),
    )


def finish_kernel(hidden_ref, slot_ref, buffer_ref, out_ref):
    slot_hot = slot_matrix(slot_ref[...], buffer_ref.shape[0])
    out_ref[...] = (hidden_ref[...] + dot_tn(slot_hot, buffer_ref[...])).astype(BF16)


def finish(hidden, slot_row, buffer):
    return pl.pallas_call(
        finish_kernel,
        out_shape=jax.ShapeDtypeStruct(hidden.shape, BF16),
        cost_estimate=pl.CostEstimate(
            flops=10**9, bytes_accessed=5 << 20, transcendentals=0
        ),
        name="finish",
    )(hidden, slot_row, buffer)


def gate_parts(pre):
    square = pre * pre
    curve = jnp.tanh(pre * (GATE_A + GATE_B * square))
    half = 0.5 * curve + 0.5
    slope = half + (0.5 * pre) * (1.0 - curve * curve) * (GATE_A + (3.0 * GATE_B) * square)
    return pre * half, slope


def expert_kernel(
    tile, routed_ref, grad_act_ref, weight_ref, act_ref, grad_pre_ref, out_ref, total_ref
):
    step = pl.program_id(0)

    @pl.when(step == 0)
    def _():
        total_ref[...] = jnp.zeros_like(total_ref)

    weight = weight_ref[...]
    for first in range(0, routed_ref.shape[0], tile):
        rows = slice(first, first + tile)
        act, slope = gate_parts(dot_nn(routed_ref[rows, :], weight))
        act_ref[rows, :] = act.astype(BF16)
        grad_pre = (grad_act_ref[rows, :].astype(F32) * slope).astype(BF16)
        grad_pre_ref[rows, :] = grad_pre
        total_ref[rows, :] += dot_nt(grad_pre, weight)

    @pl.when(step == pl.num_programs(0) - 1)
    def _():
        out_ref[...] = total_ref[...].astype(BF16)


def expert(routed, grad_act, weight, chunk=1024, tile=256):
    rows, width = routed.shape
    hidden_units = weight.shape[1]
    column_spec = pl.BlockSpec((rows, chunk), lambda step: (0, step))
    return pl.pallas_call(
        functools.partial(expert_kernel, tile),
        grid=(hidden_units // chunk,),
        in_specs=[
            whole((rows, width)),
            column_spec,
            pl.BlockSpec((width, chunk), lambda step: (0, step)),
        ],
        out_specs=(column_spec, column_spec, whole((rows, width))),
        out_shape=(
            jax.ShapeDtypeStruct((rows, hidden_units), BF16),
            jax.ShapeDtypeStruct((rows, hidden_units), BF16),
            jax.ShapeDtypeStruct((rows, width), BF16),
        ),
        scratch_shapes=[pltpu.VMEM((rows, width), F32)],
        cost_estimate=pl.CostEstimate(
            flops=4 * rows * width * hidden_units,
            bytes_accessed=36 << 20,
            transcendentals=rows * hidden_units,
        ),
        name="expert",
    )(routed, grad_act, weight)


def first_grad_kernel(flip_ref, routed_ref, grad_ref, *refs):
    step = pl.program_id(0)
    half_steps = pl.num_programs(0) // 2
    product_ref = refs[-1]
    product_ref[...] = dot_tn(routed_ref[...], grad_ref[...]).astype(BF16)
    owned = product_ref.shape[0] // 4

    def piece(place):
        row = pl.multiple_of((place ^ flip_ref[0]) * owned, owned)
        return product_ref[pl.ds(row, owned), :]

    keep_a, send_a, keep_b, send_b = refs[:-1]

    @pl.when(step < half_steps)
    def _():
        for index, (kept, sent) in enumerate(((0, 1), (2, 3))):
            keep_a[index] = piece(kept)
            send_a[index] = piece(sent)

    @pl.when(step >= half_steps)
    def _():
        for index, (kept, sent) in enumerate(((0, 2), (1, 3))):
            keep_b[index] = piece(kept)
            send_b[index] = piece(sent)


def first_grad(flip, routed, grad, chunk=1024):
    rows, width = routed.shape
    columns = grad.shape[1]
    steps = columns // chunk
    shape = jax.ShapeDtypeStruct((2, width // 4, columns // 2), BF16)
    block = (2, width // 4, chunk)
    spec_a = pl.BlockSpec(block, lambda step: (0, 0, jnp.minimum(step, steps // 2 - 1)))
    spec_b = pl.BlockSpec(block, lambda step: (0, 0, jnp.maximum(step - steps // 2, 0)))
    return pl.pallas_call(
        first_grad_kernel,
        grid=(steps,),
        in_specs=[
            pl.BlockSpec(memory_space=pltpu.SMEM),
            whole((rows, width)),
            pl.BlockSpec((rows, chunk), lambda step: (0, step)),
        ],
        out_specs=(spec_a, spec_a, spec_b, spec_b),
        out_shape=(shape,) * 4,
        scratch_shapes=[pltpu.VMEM((width, chunk), BF16)],
        cost_estimate=pl.CostEstimate(
            flops=2 * rows * width * columns, bytes_accessed=18 << 20, transcendentals=0
        ),
        name="first_grad",
    )(flip, routed, grad)


def second_grad_kernel(flip_ref, act_ref, grad_ref, keep_a, send_a, keep_b, send_b):
    step = pl.program_id(0)
    product = dot_tn(act_ref[...], grad_ref[...]).astype(BF16)
    half = product.shape[1] // 2

    @pl.when(step == 0)
    def _():
        send_a[0] = product[:, :half]
        send_b[0] = product[:, half:]

    @pl.when(step == 1)
    def _():
        send_a[0] = product[:, :half]
        keep_b[0] = product[:, half:]

    @pl.when(step == 2)
    def _():
        keep_a[0] = product[:, :half]
        send_b[0] = product[:, half:]

    @pl.when(step == 3)
    def _():
        keep_a[0] = product[:, :half]
        keep_b[0] = product[:, half:]


def second_grad(flip, act, grad):
    rows, width = grad.shape
    owned = act.shape[1] // 4
    shape = jax.ShapeDtypeStruct((2, owned, width // 2), BF16)
    block = (1, owned, width // 2)

    def spec(first_step):
        return pl.BlockSpec(
            block, lambda step, flip_ref: (1 - (step >= first_step).astype(jnp.int32), 0, 0)
        )

    return pl.pallas_call(
        second_grad_kernel,
        grid_spec=pltpu.PrefetchScalarGridSpec(
            num_scalar_prefetch=1,
            grid=(4,),
            in_specs=[
                pl.BlockSpec((rows, owned), lambda step, flip_ref: (0, place_of(step) ^ flip_ref[0])),
                pl.BlockSpec((rows, width), lambda step, flip_ref: (0, 0)),
            ],
            out_specs=(spec(3), spec(1), spec(3), spec(2)),
        ),
        out_shape=(shape,) * 4,
        cost_estimate=pl.CostEstimate(
            flops=2 * rows * width * act.shape[1], bytes_accessed=18 << 20, transcendentals=0
        ),
        name="second_grad",
    )(flip, act, grad)


def place_of(step):
    return jnp.where(step == 0, 3, jnp.where(step == 3, 0, step))


def swap(values, axis, bits):
    size = lax.axis_size(axis)
    return lax.ppermute(values, axis, [(index, index ^ bits) for index in range(size)])


def sum_over_copies(keep_a, send_a, keep_b, send_b):
    got_a = swap(send_a, "rep", 1)
    got_b = swap(send_b, "rep", 2)
    more_a = swap(add_low(keep_a[1], got_a[1]), "rep", 2)
    more_b = swap(add_low(keep_b[1], got_b[1]), "rep", 1)
    half_a = keep_a[0].astype(F32) + got_a[0].astype(F32) + more_a.astype(F32)
    half_b = keep_b[0].astype(F32) + got_b[0].astype(F32) + more_b.astype(F32)
    return jnp.concatenate([half_a, half_b], 1)


def add_low(left, right):
    return (left.astype(F32) + right.astype(F32)).astype(BF16)


def exchange(buffer, expert_count):
    shape = buffer.shape
    buffer = buffer.reshape(expert_count, shape[0] // expert_count, shape[1])
    if expert_count <= 8:
        pieces = [buffer[0]]
        for bits in range(1, expert_count):
            pieces.append(swap(buffer[bits], "ep", bits))
        return jnp.concatenate(pieces, 0)
    buffer = lax.all_to_all(buffer, "ep", split_axis=0, concat_axis=0, tiled=True)
    return buffer.reshape(shape)


def local(
    tokens_in,
    token_ids,
    hash_table,
    doc_lengths,
    gain_one,
    shift_one,
    project_in,
    project_out,
    gain_two,
    shift_two,
    expert_in,
    expert_out,
    out_grad,
):
    tok_rows, width = tokens_in.shape
    rep_size, ep_size = lax.axis_size("rep"), lax.axis_size("ep")
    rep_bits, ep_bits = rep_size.bit_length() - 1, ep_size.bit_length() - 1
    expert_count = expert_in.shape[0] * ep_size
    capacity = 2 * tok_rows // expert_count
    slot_total = expert_count * capacity
    tile = width // (rep_size * ep_size)
    paired = expert_count <= 8
    first_weight, second_weight = expert_in[0], expert_out[0]
    rep_index, ep_index = lax.axis_index("rep"), lax.axis_index("ep")
    ep_flip = jnp.reshape(ep_index if paired else 0, (1,)).astype(jnp.int32)
    rep_flip = jnp.reshape(rep_index, (1,)).astype(jnp.int32)
    layout = tuple(reversed(range(rep_bits + ep_bits)))
    spot = spread_bits(rep_index * ep_size + ep_index, layout)
    spot = jnp.reshape(spot, (1,)).astype(jnp.int32)
    if not paired:
        layout, spot = tuple(range(rep_bits + ep_bits)), jnp.zeros((1,), jnp.int32)

    slot_row, grad_buffer = route(
        ep_flip, token_ids, hash_table, out_grad, expert_count, capacity
    )
    grad_received = exchange(grad_buffer, expert_count)
    normed, query, key, value, probs, mixture, hidden, buffer = front(
        doc_lengths,
        tokens_in,
        slot_row,
        gain_one,
        shift_one,
        project_in,
        project_out,
        gain_two,
        shift_two,
        slot_total,
    )
    received = exchange(buffer, expert_count)
    grad_act = jnp.einsum("sd,fd->sf", grad_received, second_weight, preferred_element_type=F32)
    grad_act = grad_act.astype(BF16)
    act, grad_pre, grad_routed = expert(received, grad_act, first_weight)
    grad_back = exchange(grad_routed, expert_count)
    summed_second = sum_over_copies(*second_grad(rep_flip, act, grad_received))
    summed_first = sum_over_copies(*first_grad(rep_flip, received, grad_pre))
    result = jnp.einsum("sf,fd->sd", act, second_weight, preferred_element_type=F32).astype(BF16)
    grad_back, result = lax.optimization_barrier((grad_back, result))
    returned = exchange(result, expert_count)
    dense, grad_in = back(
        tile,
        layout,
        spot,
        grad_back,
        slot_row,
        hidden,
        gain_two,
        out_grad,
        mixture,
        project_out,
        query,
        key,
        value,
        probs,
        normed,
        project_in,
        tokens_in,
        gain_one,
    )
    if paired:
        for bits in [("ep", 1 << bit) for bit in range(ep_bits)] + [
            ("rep", 1 << bit) for bit in range(rep_bits)
        ]:
            half = dense.shape[0] // 2
            dense = add_low(dense[:half], swap(dense[half:], *bits))
    else:
        dense = lax.psum_scatter(dense, "rep", scatter_dimension=0, tiled=True)
        dense = lax.psum_scatter(dense, "ep", scatter_dimension=0, tiled=True)
    dense = dense.astype(F32)
    block_out = finish(hidden, slot_row, returned)
    return (
        block_out,
        grad_in,
        dense[:, : 3 * width],
        dense[:, 3 * width : 4 * width],
        dense[:, 4 * width + 2],
        dense[:, 4 * width + 3],
        dense[:, 4 * width],
        dense[:, 4 * width + 1],
        summed_first[None],
        summed_second[None],
    )


def solution(mesh):
    in_specs = (
        P(("rep", "ep"), None),
        P(("rep", "ep")),
        P(),
        P(("rep", "ep"), None),
        P(),
        P(),
        P(),
        P(),
        P(),
        P(),
        P("ep", None, None),
        P("ep", None, None),
        P(("rep", "ep"), None),
    )
    out_specs = (
        P(("rep", "ep"), None),
        P(("rep", "ep"), None),
        P(("rep", "ep"), None),
        P(("rep", "ep"), None),
        P(("rep", "ep")),
        P(("rep", "ep")),
        P(("rep", "ep")),
        P(("rep", "ep")),
        P("ep", "rep", None),
        P("ep", "rep", None),
    )
    return jax.shard_map(local, mesh=mesh, in_specs=in_specs, out_specs=out_specs, check_vma=False)
```

```python
import functools
import math

import jax
import jax.numpy as jnp
from jax import lax
from jax.experimental import pallas as pl
from jax.experimental.pallas import tpu as pltpu
from jax.sharding import PartitionSpec as P

HEADS = 16
GROUP = 4
LANES = 128
NEG_LARGE = -1e30
EPSILON = 1e-05
BF16 = jnp.bfloat16
F32 = jnp.float32
GATE_A = math.sqrt(2.0 / math.pi)
GATE_B = GATE_A * 0.044715
LIGHT = pl.CostEstimate(flops=1 << 20, bytes_accessed=1 << 16, transcendentals=0)


def dot_nn(a, b):
    return lax.dot_general(a, b, (((1,), (0,)), ((), ())), preferred_element_type=F32)


def dot_nt(a, b):
    return lax.dot_general(a, b, (((1,), (1,)), ((), ())), preferred_element_type=F32)


def dot_tn(a, b):
    return lax.dot_general(a, b, (((0,), (0,)), ((), ())), preferred_element_type=F32)


def iota(shape, axis):
    return lax.broadcasted_iota(jnp.int32, shape, axis)


def whole(shape):
    return pl.BlockSpec(shape, lambda *_: (0,) * len(shape))


def piece_specs(pieces):
    def spec(array, block):
        return pl.BlockSpec((None,) + array.shape[1:], lambda *_: (block, 0, 0))

    return [spec(array, block) for array, block in pieces]


def stack_pieces(refs):
    return jnp.concatenate([ref[...] for ref in refs], 0)


def store_blocks(refs, values):
    first = 0
    for ref in refs:
        for block in range(ref.shape[0]):
            ref[block] = values[first : first + ref.shape[1]]
            first += ref.shape[1]


def norm_parts(values):
    center = jnp.mean(values, -1, keepdims=True)
    centered = values - center
    spread = jnp.mean(centered * centered, -1, keepdims=True)
    factor = lax.rsqrt(spread + EPSILON)
    return centered * factor, factor


def norm_back(grad, gain, xhat, factor):
    scaled = grad * gain
    mean_scaled = jnp.mean(scaled, -1, keepdims=True)
    mean_cross = jnp.mean(scaled * xhat, -1, keepdims=True)
    return factor * (scaled - mean_scaled - xhat * mean_cross)


def slot_matrix(slot_row, slot_total):
    tok_rows = slot_row.shape[1]
    return (iota((slot_total, tok_rows), 0) == slot_row).astype(F32).astype(BF16)


def route_kernel(
    expert_count, capacity, flip_ref, ids_ref, table_ref, grad_ref, slot_ref, *buffer_refs
):
    tok_rows = ids_ref.shape[1]
    ids = ids_ref[...]
    table_rows = table_ref.shape[0]
    high = ids // LANES
    low = ids - high * LANES
    high_hot = (iota((table_rows, tok_rows), 0) == high).astype(F32).astype(BF16)
    picked = dot_tn(table_ref[...].astype(F32).astype(BF16), high_hot)
    low_hot = iota((LANES, tok_rows), 0) == low
    expert = jnp.sum(jnp.where(low_hot, picked, 0.0), 0, keepdims=True).astype(jnp.int32)
    expert_hot = (iota((expert_count, tok_rows), 0) == expert).astype(F32)
    before = (iota((tok_rows, tok_rows), 0) < iota((tok_rows, tok_rows), 1)).astype(F32)
    earlier = dot_nn(expert_hot.astype(BF16), before.astype(BF16))
    rank = jnp.sum(earlier * expert_hot, 0, keepdims=True).astype(jnp.int32)
    slot = (expert ^ flip_ref[0]) * capacity + rank
    slot_ref[...] = slot
    slot_hot = slot_matrix(slot, expert_count * capacity)
    store_blocks(buffer_refs, dot_nn(slot_hot, grad_ref[...]).astype(BF16))


def route(flip, token_ids, hash_table, out_grad, expert_count, capacity, block_shape):
    tok_rows, width = out_grad.shape
    slot_total = expert_count * capacity
    table_rows = hash_table.shape[0] // LANES
    blocks = slot_total // (block_shape[0] * block_shape[1])
    return pl.pallas_call(
        functools.partial(route_kernel, expert_count, capacity),
        in_specs=[
            pl.BlockSpec(memory_space=pltpu.SMEM),
            whole((1, tok_rows)),
            whole((table_rows, LANES)),
            whole((tok_rows, width)),
        ],
        out_specs=(whole((1, tok_rows)),) + (whole(block_shape),) * blocks,
        out_shape=(jax.ShapeDtypeStruct((1, tok_rows), jnp.int32),)
        + (jax.ShapeDtypeStruct(block_shape, BF16),) * blocks,
        cost_estimate=LIGHT,
        name="route",
    )(flip, token_ids.reshape(1, tok_rows), hash_table.reshape(table_rows, LANES), out_grad)


def front_kernel(
    slot_total,
    head_size,
    lengths_ref,
    tokens_ref,
    slot_ref,
    gain_one_ref,
    shift_one_ref,
    query_weight_ref,
    key_weight_ref,
    value_weight_ref,
    out_weight_ref,
    gain_two_ref,
    shift_two_ref,
    normed_ref,
    query_ref,
    key_ref,
    value_ref,
    probs_ref,
    mixture_ref,
    hidden_ref,
    *refs,
):
    buffer_refs, mask_ref = refs[:-1], refs[-1]
    step = pl.program_id(0)
    tok_rows = tokens_ref.shape[0]
    group_width = query_ref.shape[1]

    @pl.when(step == 0)
    def _():
        inputs = tokens_ref[...].astype(F32)
        xhat, _ = norm_parts(inputs)
        normed_ref[...] = (xhat * gain_one_ref[...] + shift_one_ref[...]).astype(BF16)
        position = iota((1, tok_rows), 1)
        start = jnp.zeros((1, tok_rows), jnp.int32)
        bound = jnp.int32(0)
        for index in range(lengths_ref.shape[1]):
            bound = bound + lengths_ref[0, index]
            start = jnp.where(position >= bound, bound, start)
        key_position = iota((tok_rows, tok_rows), 0)
        allowed = jnp.logical_and(key_position >= start, key_position <= position)
        mask_ref[...] = jnp.where(allowed, 0.0, NEG_LARGE)
        hidden_ref[...] = inputs

    normed = normed_ref[...]
    query = dot_nn(normed, query_weight_ref[...]).astype(BF16)
    key = dot_nn(normed, key_weight_ref[...]).astype(BF16)
    value = dot_nn(normed, value_weight_ref[...]).astype(BF16)
    query_ref[...] = query
    key_ref[...] = key
    value_ref[...] = value
    lane_head = iota((1, group_width), 1) // head_size
    scale = 1.0 / math.sqrt(head_size)
    total = jnp.zeros((tok_rows, group_width), F32)
    for head in range(GROUP):
        chosen = lane_head == head
        key_part = key * jnp.where(chosen, scale, 0.0).astype(BF16)
        value_part = value * jnp.where(chosen, 1.0, 0.0).astype(BF16)
        scores = dot_nt(key_part, query) + mask_ref[...]
        exponent = jnp.exp(scores - jnp.max(scores, 0, keepdims=True))
        inverse = 1.0 / jnp.sum(exponent, 0, keepdims=True)
        weights = (exponent * inverse).astype(BF16)
        probs_ref[head] = weights
        total = total + dot_tn(weights, value_part)
    mixture = total.astype(BF16)
    mixture_ref[...] = mixture
    hidden_ref[...] += dot_nn(mixture, out_weight_ref[...])

    @pl.when(step == pl.num_programs(0) - 1)
    def _():
        xhat, _ = norm_parts(hidden_ref[...])
        routed = (xhat * gain_two_ref[...] + shift_two_ref[...]).astype(BF16)
        slot_hot = slot_matrix(slot_ref[...], slot_total)
        store_blocks(buffer_refs, dot_nn(slot_hot, routed).astype(BF16))


def front(
    doc_lengths,
    tokens_in,
    slot_row,
    gain_one,
    shift_one,
    project_in,
    project_out,
    gain_two,
    shift_two,
    slot_total,
    block_shape,
):
    tok_rows, width = tokens_in.shape
    head_size = width // HEADS
    group_width = GROUP * head_size
    steps = HEADS // GROUP
    vector = whole((1, width))
    blocks = slot_total // (block_shape[0] * block_shape[1])

    def weight_spec(part):
        return pl.BlockSpec((width, group_width), lambda step: (0, part * steps + step))

    column_spec = pl.BlockSpec((tok_rows, group_width), lambda step: (0, step))
    return pl.pallas_call(
        functools.partial(front_kernel, slot_total, head_size),
        grid=(steps,),
        in_specs=[
            pl.BlockSpec(memory_space=pltpu.SMEM),
            whole((tok_rows, width)),
            whole((1, tok_rows)),
            vector,
            vector,
            weight_spec(0),
            weight_spec(1),
            weight_spec(2),
            pl.BlockSpec((group_width, width), lambda step: (step, 0)),
            vector,
            vector,
        ],
        out_specs=(
            whole((tok_rows, width)),
            column_spec,
            column_spec,
            column_spec,
            pl.BlockSpec((GROUP, tok_rows, tok_rows), lambda step: (step, 0, 0)),
            column_spec,
            whole((tok_rows, width)),
        )
        + (whole(block_shape),) * blocks,
        out_shape=(
            jax.ShapeDtypeStruct((tok_rows, width), BF16),
            jax.ShapeDtypeStruct((tok_rows, width), BF16),
            jax.ShapeDtypeStruct((tok_rows, width), BF16),
            jax.ShapeDtypeStruct((tok_rows, width), BF16),
            jax.ShapeDtypeStruct((HEADS, tok_rows, tok_rows), BF16),
            jax.ShapeDtypeStruct((tok_rows, width), BF16),
            jax.ShapeDtypeStruct((tok_rows, width), F32),
        )
        + (jax.ShapeDtypeStruct(block_shape, BF16),) * blocks,
        scratch_shapes=[pltpu.VMEM((tok_rows, tok_rows), F32)],
        cost_estimate=LIGHT,
        name="front",
    )(
        doc_lengths,
        tokens_in,
        slot_row,
        gain_one.reshape(1, width),
        shift_one.reshape(1, width),
        project_in,
        project_in,
        project_in,
        project_out,
        gain_two.reshape(1, width),
        shift_two.reshape(1, width),
    )


def spread_bits(index, layout):
    spot = 0
    for place, bit in enumerate(layout):
        spot = spot | (((index >> bit) & 1) << place)
    return spot


def store_rows(dense_ref, first, column, values, tile, layout, spot):
    for index in range(values.shape[0] // tile):
        place = spread_bits(first + index, layout) ^ spot
        row = pl.multiple_of(place * tile, tile)
        dense_ref[pl.ds(row, tile), column] = values[index * tile : (index + 1) * tile]


def back_kernel(
    head_size,
    tile,
    layouts,
    piece_count,
    spot_ref,
    slot_ref,
    hidden_ref,
    gain_two_ref,
    out_grad_ref,
    mixture_ref,
    out_weight_ref,
    query_ref,
    key_ref,
    value_ref,
    probs_ref,
    normed_ref,
    query_weight_ref,
    key_weight_ref,
    value_weight_ref,
    tokens_ref,
    gain_one_ref,
    *refs,
):
    piece_refs = refs[:piece_count]
    dense_a_ref, dense_b_ref, grad_in_ref = refs[piece_count : piece_count + 3]
    hidden_low_ref, normed_grad_ref, small_ref = refs[piece_count + 3 :]
    step = pl.program_id(0)
    width = tokens_ref.shape[1]
    group_width = query_ref.shape[1]

    @pl.when(step == 0)
    def _():
        buffer = stack_pieces(piece_refs)
        slot_hot = slot_matrix(slot_ref[...], buffer.shape[0])
        grad_routed = dot_tn(slot_hot, buffer)
        xhat, factor = norm_parts(hidden_ref[...])
        small_ref[0:1, :] = jnp.sum(grad_routed * xhat, 0, keepdims=True)
        small_ref[1:2, :] = jnp.sum(grad_routed, 0, keepdims=True)
        grad_hidden = out_grad_ref[...].astype(F32) + norm_back(
            grad_routed, gain_two_ref[...], xhat, factor
        )
        grad_in_ref[...] = grad_hidden
        hidden_low_ref[...] = grad_hidden.astype(BF16)
        normed_grad_ref[...] = jnp.zeros_like(normed_grad_ref)
        small_ref[4:, :] = jnp.zeros((LANES - 4, width), F32)

    hidden_low = hidden_low_ref[...]
    store_rows(
        dense_b_ref,
        step * (group_width // tile),
        slice(width, 2 * width),
        dot_tn(mixture_ref[...], hidden_low).astype(BF16),
        tile,
        layouts[1],
        spot_ref[1],
    )
    grad_mixture = dot_nt(hidden_low, out_weight_ref[...]).astype(BF16)
    query, key, value = query_ref[...], key_ref[...], value_ref[...]
    lane_head = iota((1, group_width), 1) // head_size
    scale = 1.0 / math.sqrt(head_size)
    grad_query = jnp.zeros(query.shape, F32)
    grad_key = jnp.zeros(query.shape, F32)
    grad_value = jnp.zeros(query.shape, F32)
    for head in range(GROUP):
        chosen = jnp.where(lane_head == head, 1.0, 0.0).astype(BF16)
        scaled = jnp.where(lane_head == head, scale, 0.0).astype(BF16)
        grad_part = grad_mixture * chosen
        weights_low = probs_ref[head]
        weights = weights_low.astype(F32)
        grad_weights = dot_nt(value, grad_part)
        inner = jnp.sum(weights * grad_weights, 0, keepdims=True)
        grad_scores = (weights * (grad_weights - inner)).astype(BF16)
        grad_query = grad_query + dot_tn(grad_scores, key * scaled)
        grad_key = grad_key + dot_nn(grad_scores, query * scaled)
        grad_value = grad_value + dot_nn(weights_low, grad_part)
    normed = normed_ref[...]
    for part, (grad, weight_ref) in enumerate(
        (
            (grad_query, query_weight_ref),
            (grad_key, key_weight_ref),
            (grad_value, value_weight_ref),
        )
    ):
        grad = grad.astype(BF16)
        dense_ref, first, order = (dense_b_ref, 0, 1) if part == 2 else (dense_a_ref, part * width, 0)
        column = pl.multiple_of(first + step * group_width, group_width)
        store_rows(
            dense_ref,
            0,
            pl.ds(column, group_width),
            dot_tn(normed, grad).astype(BF16),
            tile,
            layouts[order],
            spot_ref[order],
        )
        normed_grad_ref[...] += dot_nt(grad, weight_ref[...])

    @pl.when(step == pl.num_programs(0) - 1)
    def _():
        grad_normed = normed_grad_ref[...]
        xhat, factor = norm_parts(tokens_ref[...].astype(F32))
        small_ref[2:3, :] = jnp.sum(grad_normed * xhat, 0, keepdims=True)
        small_ref[3:4, :] = jnp.sum(grad_normed, 0, keepdims=True)
        store_rows(
            dense_b_ref,
            0,
            slice(2 * width, 2 * width + LANES),
            small_ref[...].T.astype(BF16),
            tile,
            layouts[1],
            spot_ref[1],
        )
        grad_in_ref[...] += norm_back(grad_normed, gain_one_ref[...], xhat, factor)


def back(
    tile,
    layouts,
    spots,
    pieces,
    slot_row,
    hidden,
    gain_two,
    out_grad,
    mixture,
    project_out,
    query,
    key,
    value,
    probs,
    normed,
    project_in,
    tokens_in,
    gain_one,
):
    tok_rows, width = tokens_in.shape
    head_size = width // HEADS
    group_width = GROUP * head_size
    steps = HEADS // GROUP
    vector = whole((1, width))
    tokens_spec = whole((tok_rows, width))

    def weight_spec(part):
        return pl.BlockSpec((width, group_width), lambda step: (0, part * steps + step))

    column_spec = pl.BlockSpec((tok_rows, group_width), lambda step: (0, step))
    return pl.pallas_call(
        functools.partial(back_kernel, head_size, tile, layouts, len(pieces)),
        grid=(steps,),
        in_specs=[
            pl.BlockSpec(memory_space=pltpu.SMEM),
            whole((1, tok_rows)),
            tokens_spec,
            vector,
            tokens_spec,
            column_spec,
            pl.BlockSpec((group_width, width), lambda step: (step, 0)),
            column_spec,
            column_spec,
            column_spec,
            pl.BlockSpec((GROUP, tok_rows, tok_rows), lambda step: (step, 0, 0)),
            tokens_spec,
            weight_spec(0),
            weight_spec(1),
            weight_spec(2),
            tokens_spec,
            vector,
        ]
        + piece_specs(pieces),
        out_specs=(
            whole((width, 2 * width)),
            whole((width, 2 * width + LANES)),
            tokens_spec,
        ),
        out_shape=(
            jax.ShapeDtypeStruct((width, 2 * width), BF16),
            jax.ShapeDtypeStruct((width, 2 * width + LANES), BF16),
            jax.ShapeDtypeStruct((tok_rows, width), F32),
        ),
        scratch_shapes=[
            pltpu.VMEM((tok_rows, width), BF16),
            pltpu.VMEM((tok_rows, width), F32),
            pltpu.VMEM((LANES, width), F32),
        ],
        cost_estimate=LIGHT,
        name="back",
    )(
        spots,
        slot_row,
        hidden,
        gain_two.reshape(1, width),
        out_grad,
        mixture,
        project_out,
        query,
        key,
        value,
        probs,
        normed,
        project_in,
        project_in,
        project_in,
        tokens_in,
        gain_one.reshape(1, width),
        *[array for array, _ in pieces],
    )


def finish_kernel(hidden_ref, slot_ref, *refs):
    buffer = stack_pieces(refs[:-1])
    slot_hot = slot_matrix(slot_ref[...], buffer.shape[0])
    refs[-1][...] = (hidden_ref[...] + dot_tn(slot_hot, buffer)).astype(BF16)


def finish(hidden, slot_row, pieces):
    return pl.pallas_call(
        finish_kernel,
        grid=(1,),
        in_specs=[whole(hidden.shape), whole(slot_row.shape)] + piece_specs(pieces),
        out_specs=whole(hidden.shape),
        out_shape=jax.ShapeDtypeStruct(hidden.shape, BF16),
        cost_estimate=LIGHT,
        name="finish",
    )(hidden, slot_row, *[array for array, _ in pieces])


def grad_act_kernel(weight_ref, *refs):
    rows_ref, out_ref = refs[-2:]

    @pl.when(pl.program_id(0) == 0)
    def _():
        rows_ref[...] = stack_pieces(refs[:-2])

    out_ref[...] = dot_nt(rows_ref[...], weight_ref[...]).astype(BF16)


def grad_act_of(weight, pieces, chunk=1024):
    hidden_units, width = weight.shape
    rows = sum(array.shape[1] for array, _ in pieces)
    return pl.pallas_call(
        grad_act_kernel,
        grid=(hidden_units // chunk,),
        in_specs=[pl.BlockSpec((chunk, width), lambda step: (step, 0))] + piece_specs(pieces),
        out_specs=(whole((rows, width)), pl.BlockSpec((rows, chunk), lambda step: (0, step))),
        out_shape=(
            jax.ShapeDtypeStruct((rows, width), BF16),
            jax.ShapeDtypeStruct((rows, hidden_units), BF16),
        ),
        cost_estimate=LIGHT,
        name="grad_act",
    )(weight, *[array for array, _ in pieces])


def result_kernel(act_a_ref, act_b_ref, weight_ref, *refs, places):
    step = pl.program_id(0)
    total_ref = refs[-1]
    half = act_a_ref.shape[0]

    @pl.when(step == 0)
    def _():
        total_ref[...] = jnp.zeros_like(total_ref)

    total_ref[:half] += dot_nn(act_a_ref[...], weight_ref[...])
    total_ref[half:] += dot_nn(act_b_ref[...], weight_ref[...])

    @pl.when(step == pl.num_programs(0) - 1)
    def _():
        store_places(refs[:-1], total_ref, places)


def store_places(refs, total_ref, places):
    for ref, firsts in zip(refs, places):
        for block, first in enumerate(firsts):
            ref[block] = total_ref[first : first + ref.shape[1]].astype(BF16)


def result_of(act_a, act_b, weight, places, block_rows, chunk=1024):
    half, hidden_units = act_a.shape
    width = weight.shape[1]
    shapes = [(len(firsts), block_rows, width) for firsts in places]
    act_spec = pl.BlockSpec((half, chunk), lambda step: (0, step))
    return pl.pallas_call(
        functools.partial(result_kernel, places=places),
        grid=(hidden_units // chunk,),
        in_specs=[act_spec, act_spec, pl.BlockSpec((chunk, width), lambda step: (step, 0))],
        out_specs=tuple(whole(shape) for shape in shapes),
        out_shape=tuple(jax.ShapeDtypeStruct(shape, BF16) for shape in shapes),
        scratch_shapes=[pltpu.VMEM((2 * half, width), F32)],
        cost_estimate=LIGHT,
        name="result",
    )(act_a, act_b, weight)


def gate_parts(pre):
    square = pre * pre
    curve = jnp.tanh(pre * (GATE_A + GATE_B * square))
    half = 0.5 * curve + 0.5
    slope = half + (0.5 * pre) * (1.0 - curve * curve) * (GATE_A + (3.0 * GATE_B) * square)
    return pre * half, slope


def expert_kernel(tile, places, piece_count, grad_act_ref, weight_ref, *refs):
    step = pl.program_id(0)
    act_ref, grad_pre_ref, rows_ref = refs[piece_count : piece_count + 3]
    out_refs, total_ref = refs[piece_count + 3 : -1], refs[-1]

    @pl.when(step == 0)
    def _():
        rows_ref[...] = stack_pieces(refs[:piece_count])
        total_ref[...] = jnp.zeros_like(total_ref)

    weight = weight_ref[...]
    for first in range(0, rows_ref.shape[0], tile):
        rows = slice(first, first + tile)
        act, slope = gate_parts(dot_nn(rows_ref[rows, :], weight))
        act_ref[rows, :] = act.astype(BF16)
        grad_pre = (grad_act_ref[rows, :].astype(F32) * slope).astype(BF16)
        grad_pre_ref[rows, :] = grad_pre
        total_ref[rows, :] += dot_nt(grad_pre, weight)

    @pl.when(step == pl.num_programs(0) - 1)
    def _():
        store_places(out_refs, total_ref, places)


def expert(half, grad_act, weight, pieces, places, block_rows, chunk=1024, tile=256):
    width, hidden_units = weight.shape
    rows = grad_act.shape[0] // 2
    column_spec = pl.BlockSpec((rows, chunk), lambda step: (0, step))
    shapes = [(len(firsts), block_rows, width) for firsts in places]
    return pl.pallas_call(
        functools.partial(expert_kernel, tile, places, len(pieces)),
        grid=(hidden_units // chunk,),
        in_specs=[
            pl.BlockSpec((rows, chunk), lambda step: (half, step)),
            pl.BlockSpec((width, chunk), lambda step: (0, step)),
        ]
        + piece_specs(pieces),
        out_specs=(column_spec, column_spec, whole((rows, width)))
        + tuple(whole(shape) for shape in shapes),
        out_shape=(
            jax.ShapeDtypeStruct((rows, hidden_units), BF16),
            jax.ShapeDtypeStruct((rows, hidden_units), BF16),
            jax.ShapeDtypeStruct((rows, width), BF16),
        )
        + tuple(jax.ShapeDtypeStruct(shape, BF16) for shape in shapes),
        scratch_shapes=[pltpu.VMEM((rows, width), F32)],
        cost_estimate=LIGHT,
        name="expert",
    )(grad_act, weight, *[array for array, _ in pieces])


def first_grad_kernel(flip_ref, rows_a_ref, rows_b_ref, grad_a_ref, grad_b_ref, *refs):
    step = pl.program_id(0)
    half_steps = pl.num_programs(0) // 2
    product_ref = refs[-1]
    product = dot_tn(rows_a_ref[...], grad_a_ref[...]) + dot_tn(rows_b_ref[...], grad_b_ref[...])
    product_ref[...] = product.astype(BF16)
    owned = product_ref.shape[0] // 4

    def piece(place):
        row = pl.multiple_of((place ^ flip_ref[0]) * owned, owned)
        return product_ref[pl.ds(row, owned), :]

    keep_a, send_a, keep_b, send_b = refs[:-1]

    @pl.when(step < half_steps)
    def _():
        for index, (kept, sent) in enumerate(((0, 1), (2, 3))):
            keep_a[index] = piece(kept)
            send_a[index] = piece(sent)

    @pl.when(step >= half_steps)
    def _():
        for index, (kept, sent) in enumerate(((0, 2), (1, 3))):
            keep_b[index] = piece(kept)
            send_b[index] = piece(sent)


def first_grad(flip, rows_a, rows_b, grad_a, grad_b, chunk=1024):
    rows, width = rows_a.shape
    columns = grad_a.shape[1]
    steps = columns // chunk
    shape = jax.ShapeDtypeStruct((2, width // 4, columns // 2), BF16)
    block = (2, width // 4, chunk)
    spec_a = pl.BlockSpec(block, lambda step: (0, 0, jnp.minimum(step, steps // 2 - 1)))
    spec_b = pl.BlockSpec(block, lambda step: (0, 0, jnp.maximum(step - steps // 2, 0)))
    return pl.pallas_call(
        first_grad_kernel,
        grid=(steps,),
        in_specs=[
            pl.BlockSpec(memory_space=pltpu.SMEM),
            whole((rows, width)),
            whole((rows, width)),
            pl.BlockSpec((rows, chunk), lambda step: (0, step)),
            pl.BlockSpec((rows, chunk), lambda step: (0, step)),
        ],
        out_specs=(spec_a, spec_a, spec_b, spec_b),
        out_shape=(shape,) * 4,
        scratch_shapes=[pltpu.VMEM((width, chunk), BF16)],
        cost_estimate=LIGHT,
        name="first_grad",
    )(flip, rows_a, rows_b, grad_a, grad_b)


def second_grad_kernel(
    flip_ref, act_a_ref, act_b_ref, grad_ref, keep_a, send_a, keep_b, send_b
):
    step = pl.program_id(0)
    rows = act_a_ref.shape[0]
    product = dot_tn(act_a_ref[...], grad_ref[:rows]) + dot_tn(act_b_ref[...], grad_ref[rows:])
    product = product.astype(BF16)
    half = product.shape[1] // 2

    @pl.when(step == 0)
    def _():
        send_a[0] = product[:, :half]
        send_b[0] = product[:, half:]

    @pl.when(step == 1)
    def _():
        send_a[0] = product[:, :half]
        keep_b[0] = product[:, half:]

    @pl.when(step == 2)
    def _():
        keep_a[0] = product[:, :half]
        send_b[0] = product[:, half:]

    @pl.when(step == 3)
    def _():
        keep_a[0] = product[:, :half]
        keep_b[0] = product[:, half:]


def second_grad(flip, act_a, act_b, grad):
    rows, width = grad.shape
    owned = act_a.shape[1] // 4
    act_spec = pl.BlockSpec(
        (rows // 2, owned), lambda step, flip_ref: (0, place_of(step) ^ flip_ref[0])
    )
    shape = jax.ShapeDtypeStruct((2, owned, width // 2), BF16)
    block = (1, owned, width // 2)

    def spec(first_step):
        return pl.BlockSpec(
            block, lambda step, flip_ref: (1 - (step >= first_step).astype(jnp.int32), 0, 0)
        )

    return pl.pallas_call(
        second_grad_kernel,
        grid_spec=pltpu.PrefetchScalarGridSpec(
            num_scalar_prefetch=1,
            grid=(4,),
            in_specs=[
                act_spec,
                act_spec,
                pl.BlockSpec((rows, width), lambda step, flip_ref: (0, 0)),
            ],
            out_specs=(spec(3), spec(1), spec(3), spec(2)),
        ),
        out_shape=(shape,) * 4,
        cost_estimate=LIGHT,
        name="second_grad",
    )(flip, act_a, act_b, grad)


def place_of(step):
    return jnp.where(step == 0, 3, jnp.where(step == 3, 0, step))


def swap(values, axis, bits):
    size = lax.axis_size(axis)
    return lax.ppermute(values, axis, [(index, index ^ bits) for index in range(size)])


def sum_over_copies(keep_a, send_a, keep_b, send_b):
    got_a = swap(send_a, "rep", 1)
    got_b = swap(send_b, "rep", 2)
    more_a = swap(add_low(keep_a[1], got_a[1]), "rep", 2)
    more_b = swap(add_low(keep_b[1], got_b[1]), "rep", 1)
    half_a = keep_a[0].astype(F32) + got_a[0].astype(F32) + more_a.astype(F32)
    half_b = keep_b[0].astype(F32) + got_b[0].astype(F32) + more_b.astype(F32)
    return jnp.concatenate([half_a, half_b], 1)


def sum_halves(values, steps):
    for axis, bit in steps[:-1]:
        half = values.shape[0] // 2
        values = add_low(values[:half], swap(values[half:], axis, 1 << bit))
    half = values.shape[0] // 2
    axis, bit = steps[-1]
    return values[:half].astype(F32) + swap(values[half:], axis, 1 << bit).astype(F32)


def add_low(left, right):
    return (left.astype(F32) + right.astype(F32)).astype(BF16)


def spread(blocks):
    return {bits: swap(block, "ep", bits) if bits else block for bits, block in blocks.items()}


def cross(blocks, members):
    return swap(jnp.concatenate([blocks[bits][1:] for bits in members], 0), "ep", 1)


def exchange(buffer):
    return lax.all_to_all(buffer, "ep", split_axis=0, concat_axis=0, tiled=True)


def local(
    tokens_in,
    token_ids,
    hash_table,
    doc_lengths,
    gain_one,
    shift_one,
    project_in,
    project_out,
    gain_two,
    shift_two,
    expert_in,
    expert_out,
    out_grad,
):
    tok_rows, width = tokens_in.shape
    rep_size, ep_size = lax.axis_size("rep"), lax.axis_size("ep")
    rep_bits, ep_bits = rep_size.bit_length() - 1, ep_size.bit_length() - 1
    expert_count = expert_in.shape[0] * ep_size
    capacity = 2 * tok_rows // expert_count
    slot_total = expert_count * capacity
    tile = width // (rep_size * ep_size)
    paired = expert_count <= 8
    first_weight, second_weight = expert_in[0], expert_out[0]
    rep_index, ep_index = lax.axis_index("rep"), lax.axis_index("ep")
    ep_flip = jnp.reshape(ep_index if paired else 0, (1,)).astype(jnp.int32)
    rep_flip = jnp.reshape(rep_index, (1,)).astype(jnp.int32)
    steps_a = [("ep", bit) for bit in range(ep_bits)] + [("rep", bit) for bit in range(rep_bits)]
    steps_b = steps_a[:1] + steps_a[ep_bits:] + steps_a[1:ep_bits]
    layouts, spots = [], []
    for steps in (steps_a, steps_b):
        places = [bit + (ep_bits if axis == "rep" else 0) for axis, bit in reversed(steps)]
        layouts.append(tuple(places) if paired else tuple(range(rep_bits + ep_bits)))
        spots.append(spread_bits(rep_index * ep_size + ep_index, layouts[-1]) if paired else 0)
    spots = jnp.stack([jnp.asarray(spot, jnp.int32) for spot in spots])

    fronts = (
        doc_lengths,
        tokens_in,
        gain_one,
        shift_one,
        project_in,
        project_out,
        gain_two,
        shift_two,
    )
    half_rows = slot_total // 2
    if paired:
        members = tuple(range(0, expert_count, 2))
        order = members[::2] + members[1::2]
        halves = (members[::2], members[1::2])
        block_rows, block_shape = capacity, (2, capacity, width)
    else:
        block_rows, block_shape = half_rows, (expert_count, capacity, width)
    slot_row, *buffers = route(
        ep_flip, token_ids, hash_table, out_grad, expert_count, capacity, block_shape
    )
    if paired:
        grads = spread(dict(zip(members, buffers)))
        crossed = cross(grads, order)
        grad_pieces = []
        for index, half in enumerate(halves):
            grad_pieces += [(grads[bits], 0) for bits in half]
            grad_pieces += [(crossed, index * len(half) + place) for place in range(len(half))]
    else:
        grads = exchange(buffers[0]).reshape(2, half_rows, width)
        grad_pieces = [(grads, 0), (grads, 1)]
    normed, query, key, value, probs, mixture, hidden, *buffers = front(
        *fronts[:2], slot_row, *fronts[2:], slot_total, block_shape
    )
    grad_rows, grad_act = grad_act_of(second_weight, grad_pieces)
    outs = []
    if paired:
        received = spread(dict(zip(members, buffers)))
        count = len(halves[0])
        places = [[place * capacity, (count + place) * capacity] for place in range(count)]
        back_pieces = {}
        for index, half in enumerate(halves):
            crossed = cross(received, half)
            pieces = [(received[bits], 0) for bits in half]
            pieces += [(crossed, place) for place in range(count)]
            *out, = expert(index, grad_act, first_weight, pieces, places, capacity)
            outs.append(out[:3])
            sent = spread(dict(zip(half, out[3:])))
            crossed = cross(sent, half)
            for place, bits in enumerate(half):
                back_pieces[bits], back_pieces[bits + 1] = (sent[bits], 0), (crossed, place)
        back_pieces = [back_pieces[place] for place in range(expert_count)]
        places += [[first + half_rows for first in firsts] for firsts in places]
    else:
        received = exchange(buffers[0]).reshape(2, half_rows, width)
        places = [[0]]
        for index in range(2):
            *out, = expert(index, grad_act, first_weight, [(received, index)], places, half_rows)
            outs.append(out)
        sent = jnp.concatenate([outs[0][3], outs[1][3]], 0).reshape(buffers[0].shape)
        back_pieces = [(exchange(sent).reshape(1, slot_total, width), 0)]
        places = [[0, half_rows]]
    (act_a, grad_pre_a, rows_a), (act_b, grad_pre_b, rows_b) = outs[0][:3], outs[1][:3]
    second_parts = second_grad(rep_flip, act_a, act_b, grad_rows)
    rows_a, second_parts = lax.optimization_barrier((rows_a, second_parts))
    first_parts = first_grad(rep_flip, rows_a, rows_b, grad_pre_a, grad_pre_b)
    act_a, first_parts = lax.optimization_barrier((act_a, first_parts))
    results = result_of(act_a, act_b, second_weight, places, block_rows)
    back_arrays = [array for array, _ in back_pieces]
    back_arrays, results = lax.optimization_barrier((back_arrays, results))
    back_pieces = [(array, piece[1]) for array, piece in zip(back_arrays, back_pieces)]
    summed_second = sum_over_copies(*second_parts)
    summed_first = sum_over_copies(*first_parts)
    if paired:
        sent = spread(dict(zip(order, results)))
        crossed = cross(sent, members)
        pieces = [
            ((sent[bits], 0), (crossed, place)) for place, bits in enumerate(members)
        ]
        pieces = [piece for pair in pieces for piece in pair]
    else:
        returned = exchange(results[0].reshape(expert_count, capacity, width))
        pieces = [(returned.reshape(1, slot_total, width), 0)]
    dense_a, dense_b, grad_in = back(
        tile,
        layouts,
        spots,
        back_pieces,
        slot_row,
        hidden,
        gain_two,
        out_grad,
        mixture,
        project_out,
        query,
        key,
        value,
        probs,
        normed,
        project_in,
        tokens_in,
        gain_one,
    )
    if paired:
        dense_a, dense_b = sum_halves(dense_a, steps_a), sum_halves(dense_b, steps_b)
    else:
        dense = jnp.concatenate([dense_a, dense_b], 1)
        dense = lax.psum_scatter(dense, "rep", scatter_dimension=0, tiled=True)
        dense = lax.psum_scatter(dense, "ep", scatter_dimension=0, tiled=True).astype(F32)
        dense_a, dense_b = dense[:, : 2 * width], dense[:, 2 * width :]
    block_out = finish(hidden, slot_row, pieces)
    return (
        block_out,
        grad_in,
        jnp.concatenate([dense_a, dense_b[:, :width]], 1),
        dense_b[:, width : 2 * width],
        dense_b[:, 2 * width + 2],
        dense_b[:, 2 * width + 3],
        dense_b[:, 2 * width],
        dense_b[:, 2 * width + 1],
        summed_first[None],
        summed_second[None],
    )


def solution(mesh):
    in_specs = (
        P(("rep", "ep"), None),
        P(("rep", "ep")),
        P(),
        P(("rep", "ep"), None),
        P(),
        P(),
        P(),
        P(),
        P(),
        P(),
        P("ep", None, None),
        P("ep", None, None),
        P(("rep", "ep"), None),
    )
    out_specs = (
        P(("rep", "ep"), None),
        P(("rep", "ep"), None),
        P(("rep", "ep"), None),
        P(("rep", "ep"), None),
        P(("rep", "ep")),
        P(("rep", "ep")),
        P(("rep", "ep")),
        P(("rep", "ep")),
        P("ep", "rep", None),
        P("ep", "rep", None),
    )
    return jax.shard_map(local, mesh=mesh, in_specs=in_specs, out_specs=out_specs, check_vma=False)
```

```python
import functools
import math

import jax
import jax.numpy as jnp
from jax import lax
from jax.experimental import pallas as pl
from jax.experimental.pallas import tpu as pltpu
from jax.sharding import PartitionSpec as P

HEADS = 16
GROUP = 4
LANES = 128
NEG_LARGE = -1e30
EPSILON = 1e-05
BF16 = jnp.bfloat16
F32 = jnp.float32
GATE_A = math.sqrt(2.0 / math.pi)
GATE_B = GATE_A * 0.044715
LIGHT = pl.CostEstimate(flops=1 << 20, bytes_accessed=1 << 16, transcendentals=0)


def dot_nn(a, b):
    return lax.dot_general(a, b, (((1,), (0,)), ((), ())), preferred_element_type=F32)


def dot_nt(a, b):
    return lax.dot_general(a, b, (((1,), (1,)), ((), ())), preferred_element_type=F32)


def dot_tn(a, b):
    return lax.dot_general(a, b, (((0,), (0,)), ((), ())), preferred_element_type=F32)


def iota(shape, axis):
    return lax.broadcasted_iota(jnp.int32, shape, axis)


def whole(shape):
    return pl.BlockSpec(shape, lambda *_: (0,) * len(shape))


def piece_specs(pieces):
    def spec(array, block):
        return pl.BlockSpec((None,) + array.shape[1:], lambda *_: (block, 0, 0))

    return [spec(array, block) for array, block in pieces]


def stack_pieces(refs):
    return jnp.concatenate([ref[...] for ref in refs], 0)


def store_blocks(refs, values):
    first = 0
    for ref in refs:
        for block in range(ref.shape[0]):
            ref[block] = values[first : first + ref.shape[1]]
            first += ref.shape[1]


def norm_parts(values):
    center = jnp.mean(values, -1, keepdims=True)
    centered = values - center
    spread = jnp.mean(centered * centered, -1, keepdims=True)
    factor = lax.rsqrt(spread + EPSILON)
    return centered * factor, factor


def norm_back(grad, gain, xhat, factor):
    scaled = grad * gain
    mean_scaled = jnp.mean(scaled, -1, keepdims=True)
    mean_cross = jnp.mean(scaled * xhat, -1, keepdims=True)
    return factor * (scaled - mean_scaled - xhat * mean_cross)


def slot_matrix(slot_row, slot_total):
    tok_rows = slot_row.shape[1]
    return (iota((slot_total, tok_rows), 0) == slot_row).astype(F32).astype(BF16)


def route_kernel(
    expert_count, capacity, flip_ref, ids_ref, table_ref, grad_ref, slot_ref, *buffer_refs
):
    tok_rows = ids_ref.shape[1]
    ids = ids_ref[...]
    table_rows = table_ref.shape[0]
    high = ids // LANES
    low = ids - high * LANES
    high_hot = (iota((table_rows, tok_rows), 0) == high).astype(F32).astype(BF16)
    picked = dot_tn(table_ref[...].astype(F32).astype(BF16), high_hot)
    low_hot = iota((LANES, tok_rows), 0) == low
    expert = jnp.sum(jnp.where(low_hot, picked, 0.0), 0, keepdims=True).astype(jnp.int32)
    expert_hot = (iota((expert_count, tok_rows), 0) == expert).astype(F32)
    before = (iota((tok_rows, tok_rows), 0) < iota((tok_rows, tok_rows), 1)).astype(F32)
    earlier = dot_nn(expert_hot.astype(BF16), before.astype(BF16))
    rank = jnp.sum(earlier * expert_hot, 0, keepdims=True).astype(jnp.int32)
    slot = (expert ^ flip_ref[0]) * capacity + rank
    slot_ref[...] = slot
    slot_hot = slot_matrix(slot, expert_count * capacity)
    store_blocks(buffer_refs, dot_nn(slot_hot, grad_ref[...]).astype(BF16))


def route(flip, token_ids, hash_table, out_grad, expert_count, capacity, block_shape):
    tok_rows, width = out_grad.shape
    slot_total = expert_count * capacity
    table_rows = hash_table.shape[0] // LANES
    blocks = slot_total // (block_shape[0] * block_shape[1])
    return pl.pallas_call(
        functools.partial(route_kernel, expert_count, capacity),
        in_specs=[
            pl.BlockSpec(memory_space=pltpu.SMEM),
            whole((1, tok_rows)),
            whole((table_rows, LANES)),
            whole((tok_rows, width)),
        ],
        out_specs=(whole((1, tok_rows)),) + (whole(block_shape),) * blocks,
        out_shape=(jax.ShapeDtypeStruct((1, tok_rows), jnp.int32),)
        + (jax.ShapeDtypeStruct(block_shape, BF16),) * blocks,
        cost_estimate=LIGHT,
        name="route",
    )(flip, token_ids.reshape(1, tok_rows), hash_table.reshape(table_rows, LANES), out_grad)


def front_kernel(
    slot_total,
    head_size,
    lengths_ref,
    tokens_ref,
    slot_ref,
    gain_one_ref,
    shift_one_ref,
    query_weight_ref,
    key_weight_ref,
    value_weight_ref,
    out_weight_ref,
    gain_two_ref,
    shift_two_ref,
    normed_ref,
    query_ref,
    key_ref,
    value_ref,
    probs_ref,
    mixture_ref,
    hidden_ref,
    *refs,
):
    buffer_refs, mask_ref = refs[:-1], refs[-1]
    step = pl.program_id(0)
    tok_rows = tokens_ref.shape[0]
    group_width = query_ref.shape[1]

    @pl.when(step == 0)
    def _():
        inputs = tokens_ref[...].astype(F32)
        xhat, _ = norm_parts(inputs)
        normed_ref[...] = (xhat * gain_one_ref[...] + shift_one_ref[...]).astype(BF16)
        position = iota((1, tok_rows), 1)
        start = jnp.zeros((1, tok_rows), jnp.int32)
        bound = jnp.int32(0)
        for index in range(lengths_ref.shape[1]):
            bound = bound + lengths_ref[0, index]
            start = jnp.where(position >= bound, bound, start)
        key_position = iota((tok_rows, tok_rows), 0)
        allowed = jnp.logical_and(key_position >= start, key_position <= position)
        mask_ref[...] = jnp.where(allowed, 0.0, NEG_LARGE)
        hidden_ref[...] = inputs

    normed = normed_ref[...]
    query = dot_nn(normed, query_weight_ref[...]).astype(BF16)
    key = dot_nn(normed, key_weight_ref[...]).astype(BF16)
    value = dot_nn(normed, value_weight_ref[...]).astype(BF16)
    query_ref[...] = query
    key_ref[...] = key
    value_ref[...] = value
    lane_head = iota((1, group_width), 1) // head_size
    scale = 1.0 / math.sqrt(head_size)
    total = jnp.zeros((tok_rows, group_width), F32)
    for head in range(GROUP):
        chosen = lane_head == head
        key_part = key * jnp.where(chosen, scale, 0.0).astype(BF16)
        value_part = value * jnp.where(chosen, 1.0, 0.0).astype(BF16)
        scores = dot_nt(key_part, query) + mask_ref[...]
        exponent = jnp.exp(scores - jnp.max(scores, 0, keepdims=True))
        inverse = 1.0 / jnp.sum(exponent, 0, keepdims=True)
        weights = (exponent * inverse).astype(BF16)
        probs_ref[head] = weights
        total = total + dot_tn(weights, value_part)
    mixture = total.astype(BF16)
    mixture_ref[...] = mixture
    hidden_ref[...] += dot_nn(mixture, out_weight_ref[...])

    @pl.when(step == pl.num_programs(0) - 1)
    def _():
        xhat, _ = norm_parts(hidden_ref[...])
        routed = (xhat * gain_two_ref[...] + shift_two_ref[...]).astype(BF16)
        slot_hot = slot_matrix(slot_ref[...], slot_total)
        store_blocks(buffer_refs, dot_nn(slot_hot, routed).astype(BF16))


def front(
    doc_lengths,
    tokens_in,
    slot_row,
    gain_one,
    shift_one,
    project_in,
    project_out,
    gain_two,
    shift_two,
    slot_total,
    block_shape,
):
    tok_rows, width = tokens_in.shape
    head_size = width // HEADS
    group_width = GROUP * head_size
    steps = HEADS // GROUP
    vector = whole((1, width))
    blocks = slot_total // (block_shape[0] * block_shape[1])

    def weight_spec(part):
        return pl.BlockSpec((width, group_width), lambda step: (0, part * steps + step))

    column_spec = pl.BlockSpec((tok_rows, group_width), lambda step: (0, step))
    return pl.pallas_call(
        functools.partial(front_kernel, slot_total, head_size),
        grid=(steps,),
        in_specs=[
            pl.BlockSpec(memory_space=pltpu.SMEM),
            whole((tok_rows, width)),
            whole((1, tok_rows)),
            vector,
            vector,
            weight_spec(0),
            weight_spec(1),
            weight_spec(2),
            pl.BlockSpec((group_width, width), lambda step: (step, 0)),
            vector,
            vector,
        ],
        out_specs=(
            whole((tok_rows, width)),
            column_spec,
            column_spec,
            column_spec,
            pl.BlockSpec((GROUP, tok_rows, tok_rows), lambda step: (step, 0, 0)),
            column_spec,
            whole((tok_rows, width)),
        )
        + (whole(block_shape),) * blocks,
        out_shape=(
            jax.ShapeDtypeStruct((tok_rows, width), BF16),
            jax.ShapeDtypeStruct((tok_rows, width), BF16),
            jax.ShapeDtypeStruct((tok_rows, width), BF16),
            jax.ShapeDtypeStruct((tok_rows, width), BF16),
            jax.ShapeDtypeStruct((HEADS, tok_rows, tok_rows), BF16),
            jax.ShapeDtypeStruct((tok_rows, width), BF16),
            jax.ShapeDtypeStruct((tok_rows, width), F32),
        )
        + (jax.ShapeDtypeStruct(block_shape, BF16),) * blocks,
        scratch_shapes=[pltpu.VMEM((tok_rows, tok_rows), F32)],
        cost_estimate=LIGHT,
        name="front",
    )(
        doc_lengths,
        tokens_in,
        slot_row,
        gain_one.reshape(1, width),
        shift_one.reshape(1, width),
        project_in,
        project_in,
        project_in,
        project_out,
        gain_two.reshape(1, width),
        shift_two.reshape(1, width),
    )


def spread_bits(index, layout):
    spot = 0
    for place, bit in enumerate(layout):
        spot = spot | (((index >> bit) & 1) << place)
    return spot


def store_rows(refs, first, column, values, tile, order, spot):
    keep_ref, send_ref = refs
    layout, roll = order
    top = len(layout) - 1
    even_kept = (spot >> top) == 0
    for index in range(0, values.shape[0] // tile, 2):
        place = (spread_bits(first + index, layout) ^ spot) & ((1 << top) - 1)
        if roll:
            place = place ^ (((place >> roll) & 1) << (roll - 1))
        even = values[index * tile : (index + 1) * tile]
        odd = values[(index + 1) * tile : (index + 2) * tile]
        rows = pl.ds(pl.multiple_of(place * tile, tile), tile)
        keep_ref[rows, column] = jnp.where(even_kept, even, odd).astype(BF16)
        send_ref[rows, column] = jnp.where(even_kept, odd, even).astype(BF16)


def back_kernel(
    head_size,
    tile,
    order,
    piece_count,
    spot_ref,
    slot_ref,
    hidden_ref,
    gain_two_ref,
    out_grad_ref,
    mixture_ref,
    out_weight_ref,
    query_ref,
    key_ref,
    value_ref,
    probs_ref,
    normed_ref,
    query_weight_ref,
    key_weight_ref,
    value_weight_ref,
    tokens_ref,
    gain_one_ref,
    *refs,
):
    piece_refs = refs[:piece_count]
    dense_refs = refs[piece_count : piece_count + 2]
    grad_in_ref, hidden_low_ref, normed_grad_ref, small_ref = refs[piece_count + 2 :]
    step = pl.program_id(0)
    width = tokens_ref.shape[1]
    group_width = query_ref.shape[1]

    @pl.when(step == 0)
    def _():
        buffer = stack_pieces(piece_refs)
        slot_hot = slot_matrix(slot_ref[...], buffer.shape[0])
        grad_routed = dot_tn(slot_hot, buffer)
        xhat, factor = norm_parts(hidden_ref[...])
        small_ref[0:1, :] = jnp.sum(grad_routed * xhat, 0, keepdims=True)
        small_ref[1:2, :] = jnp.sum(grad_routed, 0, keepdims=True)
        grad_hidden = out_grad_ref[...].astype(F32) + norm_back(
            grad_routed, gain_two_ref[...], xhat, factor
        )
        grad_in_ref[...] = grad_hidden
        hidden_low_ref[...] = grad_hidden.astype(BF16)
        normed_grad_ref[...] = jnp.zeros_like(normed_grad_ref)
        small_ref[4:, :] = jnp.zeros((LANES - 4, width), F32)

    hidden_low = hidden_low_ref[...]
    store_rows(
        dense_refs,
        step * (group_width // tile),
        slice(3 * width, 4 * width),
        dot_tn(mixture_ref[...], hidden_low),
        tile,
        order,
        spot_ref[0],
    )
    grad_mixture = dot_nt(hidden_low, out_weight_ref[...]).astype(BF16)
    query, key, value = query_ref[...], key_ref[...], value_ref[...]
    lane_head = iota((1, group_width), 1) // head_size
    scale = 1.0 / math.sqrt(head_size)
    grad_query = jnp.zeros(query.shape, F32)
    grad_key = jnp.zeros(query.shape, F32)
    grad_value = jnp.zeros(query.shape, F32)
    for head in range(GROUP):
        chosen = jnp.where(lane_head == head, 1.0, 0.0).astype(BF16)
        scaled = jnp.where(lane_head == head, scale, 0.0).astype(BF16)
        grad_part = grad_mixture * chosen
        weights_low = probs_ref[head]
        weights = weights_low.astype(F32)
        grad_weights = dot_nt(value, grad_part)
        inner = jnp.sum(weights * grad_weights, 0, keepdims=True)
        grad_scores = (weights * (grad_weights - inner)).astype(BF16)
        grad_query = grad_query + dot_tn(grad_scores, key * scaled)
        grad_key = grad_key + dot_nn(grad_scores, query * scaled)
        grad_value = grad_value + dot_nn(weights_low, grad_part)
    normed = normed_ref[...]
    for part, (grad, weight_ref) in enumerate(
        (
            (grad_query, query_weight_ref),
            (grad_key, key_weight_ref),
            (grad_value, value_weight_ref),
        )
    ):
        grad = grad.astype(BF16)
        column = pl.multiple_of(part * width + step * group_width, group_width)
        store_rows(
            dense_refs,
            0,
            pl.ds(column, group_width),
            dot_tn(normed, grad),
            tile,
            order,
            spot_ref[0],
        )
        normed_grad_ref[...] += dot_nt(grad, weight_ref[...])

    @pl.when(step == pl.num_programs(0) - 1)
    def _():
        grad_normed = normed_grad_ref[...]
        xhat, factor = norm_parts(tokens_ref[...].astype(F32))
        small_ref[2:3, :] = jnp.sum(grad_normed * xhat, 0, keepdims=True)
        small_ref[3:4, :] = jnp.sum(grad_normed, 0, keepdims=True)
        store_rows(
            dense_refs,
            0,
            slice(4 * width, 4 * width + LANES),
            small_ref[...].T,
            tile,
            order,
            spot_ref[0],
        )
        grad_in_ref[...] += norm_back(grad_normed, gain_one_ref[...], xhat, factor)


def back(
    tile,
    order,
    spot,
    pieces,
    slot_row,
    hidden,
    gain_two,
    out_grad,
    mixture,
    project_out,
    query,
    key,
    value,
    probs,
    normed,
    project_in,
    tokens_in,
    gain_one,
):
    tok_rows, width = tokens_in.shape
    head_size = width // HEADS
    group_width = GROUP * head_size
    steps = HEADS // GROUP
    vector = whole((1, width))
    tokens_spec = whole((tok_rows, width))

    def weight_spec(part):
        return pl.BlockSpec((width, group_width), lambda step: (0, part * steps + step))

    column_spec = pl.BlockSpec((tok_rows, group_width), lambda step: (0, step))
    return pl.pallas_call(
        functools.partial(back_kernel, head_size, tile, order, len(pieces)),
        grid=(steps,),
        in_specs=[
            pl.BlockSpec(memory_space=pltpu.SMEM),
            whole((1, tok_rows)),
            tokens_spec,
            vector,
            tokens_spec,
            column_spec,
            pl.BlockSpec((group_width, width), lambda step: (step, 0)),
            column_spec,
            column_spec,
            column_spec,
            pl.BlockSpec((GROUP, tok_rows, tok_rows), lambda step: (step, 0, 0)),
            tokens_spec,
            weight_spec(0),
            weight_spec(1),
            weight_spec(2),
            tokens_spec,
            vector,
        ]
        + piece_specs(pieces),
        out_specs=(
            whole((width // 2, 4 * width + LANES)),
            whole((width // 2, 4 * width + LANES)),
            tokens_spec,
        ),
        out_shape=(
            jax.ShapeDtypeStruct((width // 2, 4 * width + LANES), BF16),
            jax.ShapeDtypeStruct((width // 2, 4 * width + LANES), BF16),
            jax.ShapeDtypeStruct((tok_rows, width), F32),
        ),
        scratch_shapes=[
            pltpu.VMEM((tok_rows, width), BF16),
            pltpu.VMEM((tok_rows, width), F32),
            pltpu.VMEM((LANES, width), F32),
        ],
        cost_estimate=LIGHT,
        name="back",
    )(
        spot,
        slot_row,
        hidden,
        gain_two.reshape(1, width),
        out_grad,
        mixture,
        project_out,
        query,
        key,
        value,
        probs,
        normed,
        project_in,
        project_in,
        project_in,
        tokens_in,
        gain_one.reshape(1, width),
        *[array for array, _ in pieces],
    )


def finish_kernel(hidden_ref, slot_ref, *refs):
    buffer = stack_pieces(refs[:-1])
    slot_hot = slot_matrix(slot_ref[...], buffer.shape[0])
    refs[-1][...] = (hidden_ref[...] + dot_tn(slot_hot, buffer)).astype(BF16)


def finish(hidden, slot_row, pieces):
    return pl.pallas_call(
        finish_kernel,
        grid=(1,),
        in_specs=[whole(hidden.shape), whole(slot_row.shape)] + piece_specs(pieces),
        out_specs=whole(hidden.shape),
        out_shape=jax.ShapeDtypeStruct(hidden.shape, BF16),
        cost_estimate=LIGHT,
        name="finish",
    )(hidden, slot_row, *[array for array, _ in pieces])


def grad_act_kernel(weight_ref, *refs):
    rows_ref, out_ref = refs[-2:]

    @pl.when(pl.program_id(0) == 0)
    def _():
        rows_ref[...] = stack_pieces(refs[:-2])

    out_ref[...] = dot_nt(rows_ref[...], weight_ref[...]).astype(BF16)


def grad_act_of(weight, pieces, chunk=1024):
    hidden_units, width = weight.shape
    rows = sum(array.shape[1] for array, _ in pieces)
    return pl.pallas_call(
        grad_act_kernel,
        grid=(hidden_units // chunk,),
        in_specs=[pl.BlockSpec((chunk, width), lambda step: (step, 0))] + piece_specs(pieces),
        out_specs=(whole((rows, width)), pl.BlockSpec((rows, chunk), lambda step: (0, step))),
        out_shape=(
            jax.ShapeDtypeStruct((rows, width), BF16),
            jax.ShapeDtypeStruct((rows, hidden_units), BF16),
        ),
        cost_estimate=LIGHT,
        name="grad_act",
    )(weight, *[array for array, _ in pieces])


def result_kernel(act_a_ref, act_b_ref, weight_ref, *refs, places):
    step = pl.program_id(0)
    total_ref = refs[-1]
    half = act_a_ref.shape[0]

    @pl.when(step == 0)
    def _():
        total_ref[...] = jnp.zeros_like(total_ref)

    total_ref[:half] += dot_nn(act_a_ref[...], weight_ref[...])
    total_ref[half:] += dot_nn(act_b_ref[...], weight_ref[...])

    @pl.when(step == pl.num_programs(0) - 1)
    def _():
        store_places(refs[:-1], total_ref, places)


def store_places(refs, total_ref, places):
    for ref, firsts in zip(refs, places):
        for block, first in enumerate(firsts):
            ref[block] = total_ref[first : first + ref.shape[1]].astype(BF16)


def result_of(act_a, act_b, weight, places, block_rows, chunk=1024):
    half, hidden_units = act_a.shape
    width = weight.shape[1]
    shapes = [(len(firsts), block_rows, width) for firsts in places]
    act_spec = pl.BlockSpec((half, chunk), lambda step: (0, step))
    return pl.pallas_call(
        functools.partial(result_kernel, places=places),
        grid=(hidden_units // chunk,),
        in_specs=[act_spec, act_spec, pl.BlockSpec((chunk, width), lambda step: (step, 0))],
        out_specs=tuple(whole(shape) for shape in shapes),
        out_shape=tuple(jax.ShapeDtypeStruct(shape, BF16) for shape in shapes),
        scratch_shapes=[pltpu.VMEM((2 * half, width), F32)],
        cost_estimate=LIGHT,
        name="result",
    )(act_a, act_b, weight)


def gate_parts(pre):
    square = pre * pre
    curve = jnp.tanh(pre * (GATE_A + GATE_B * square))
    half = 0.5 * curve + 0.5
    slope = half + (0.5 * pre) * (1.0 - curve * curve) * (GATE_A + (3.0 * GATE_B) * square)
    return pre * half, slope


def expert_kernel(tile, places, piece_count, grad_act_ref, weight_ref, *refs):
    step = pl.program_id(0)
    act_ref, grad_pre_ref, rows_ref = refs[piece_count : piece_count + 3]
    out_refs, total_ref = refs[piece_count + 3 : -1], refs[-1]

    @pl.when(step == 0)
    def _():
        rows_ref[...] = stack_pieces(refs[:piece_count])
        total_ref[...] = jnp.zeros_like(total_ref)

    weight = weight_ref[...]
    for first in range(0, rows_ref.shape[0], tile):
        rows = slice(first, first + tile)
        act, slope = gate_parts(dot_nn(rows_ref[rows, :], weight))
        act_ref[rows, :] = act.astype(BF16)
        grad_pre = (grad_act_ref[rows, :].astype(F32) * slope).astype(BF16)
        grad_pre_ref[rows, :] = grad_pre
        total_ref[rows, :] += dot_nt(grad_pre, weight)

    @pl.when(step == pl.num_programs(0) - 1)
    def _():
        store_places(out_refs, total_ref, places)


def expert(half, grad_act, weight, pieces, places, block_rows, chunk=1024, tile=256):
    width, hidden_units = weight.shape
    rows = grad_act.shape[0] // 2
    column_spec = pl.BlockSpec((rows, chunk), lambda step: (0, step))
    shapes = [(len(firsts), block_rows, width) for firsts in places]
    return pl.pallas_call(
        functools.partial(expert_kernel, tile, places, len(pieces)),
        grid=(hidden_units // chunk,),
        in_specs=[
            pl.BlockSpec((rows, chunk), lambda step: (half, step)),
            pl.BlockSpec((width, chunk), lambda step: (0, step)),
        ]
        + piece_specs(pieces),
        out_specs=(column_spec, column_spec, whole((rows, width)))
        + tuple(whole(shape) for shape in shapes),
        out_shape=(
            jax.ShapeDtypeStruct((rows, hidden_units), BF16),
            jax.ShapeDtypeStruct((rows, hidden_units), BF16),
            jax.ShapeDtypeStruct((rows, width), BF16),
        )
        + tuple(jax.ShapeDtypeStruct(shape, BF16) for shape in shapes),
        scratch_shapes=[pltpu.VMEM((rows, width), F32)],
        cost_estimate=LIGHT,
        name="expert",
    )(grad_act, weight, *[array for array, _ in pieces])


def first_grad_kernel(flip_ref, rows_a_ref, rows_b_ref, grad_a_ref, grad_b_ref, *refs):
    step = pl.program_id(0)
    half_steps = pl.num_programs(0) // 2
    product_ref = refs[-1]
    product = dot_tn(rows_a_ref[...], grad_a_ref[...]) + dot_tn(rows_b_ref[...], grad_b_ref[...])
    product_ref[...] = product.astype(BF16)
    owned = product_ref.shape[0] // 4

    def piece(place):
        row = pl.multiple_of((place ^ flip_ref[0]) * owned, owned)
        return product_ref[pl.ds(row, owned), :]

    keep_a, send_a, keep_b, send_b = refs[:-1]

    @pl.when(step < half_steps)
    def _():
        for index, (kept, sent) in enumerate(((0, 1), (2, 3))):
            keep_a[index] = piece(kept)
            send_a[index] = piece(sent)

    @pl.when(step >= half_steps)
    def _():
        for index, (kept, sent) in enumerate(((0, 2), (1, 3))):
            keep_b[index] = piece(kept)
            send_b[index] = piece(sent)


def first_grad(flip, rows_a, rows_b, grad_a, grad_b, chunk=1024):
    rows, width = rows_a.shape
    columns = grad_a.shape[1]
    steps = columns // chunk
    shape = jax.ShapeDtypeStruct((2, width // 4, columns // 2), BF16)
    block = (2, width // 4, chunk)
    spec_a = pl.BlockSpec(block, lambda step: (0, 0, jnp.minimum(step, steps // 2 - 1)))
    spec_b = pl.BlockSpec(block, lambda step: (0, 0, jnp.maximum(step - steps // 2, 0)))
    return pl.pallas_call(
        first_grad_kernel,
        grid=(steps,),
        in_specs=[
            pl.BlockSpec(memory_space=pltpu.SMEM),
            whole((rows, width)),
            whole((rows, width)),
            pl.BlockSpec((rows, chunk), lambda step: (0, step)),
            pl.BlockSpec((rows, chunk), lambda step: (0, step)),
        ],
        out_specs=(spec_a, spec_a, spec_b, spec_b),
        out_shape=(shape,) * 4,
        scratch_shapes=[pltpu.VMEM((width, chunk), BF16)],
        cost_estimate=LIGHT,
        name="first_grad",
    )(flip, rows_a, rows_b, grad_a, grad_b)


def second_grad_kernel(
    flip_ref, act_a_ref, act_b_ref, grad_ref, keep_a, send_a, keep_b, send_b
):
    step = pl.program_id(0)
    rows = act_a_ref.shape[0]
    product = dot_tn(act_a_ref[...], grad_ref[:rows]) + dot_tn(act_b_ref[...], grad_ref[rows:])
    product = product.astype(BF16)
    half = product.shape[1] // 2

    @pl.when(step == 0)
    def _():
        send_a[0] = product[:, :half]
        send_b[0] = product[:, half:]

    @pl.when(step == 1)
    def _():
        send_a[0] = product[:, :half]
        keep_b[0] = product[:, half:]

    @pl.when(step == 2)
    def _():
        keep_a[0] = product[:, :half]
        send_b[0] = product[:, half:]

    @pl.when(step == 3)
    def _():
        keep_a[0] = product[:, :half]
        keep_b[0] = product[:, half:]


def second_grad(flip, act_a, act_b, grad):
    rows, width = grad.shape
    owned = act_a.shape[1] // 4
    act_spec = pl.BlockSpec(
        (rows // 2, owned), lambda step, flip_ref: (0, place_of(step) ^ flip_ref[0])
    )
    shape = jax.ShapeDtypeStruct((2, owned, width // 2), BF16)
    block = (1, owned, width // 2)

    def spec(first_step):
        return pl.BlockSpec(
            block, lambda step, flip_ref: (1 - (step >= first_step).astype(jnp.int32), 0, 0)
        )

    return pl.pallas_call(
        second_grad_kernel,
        grid_spec=pltpu.PrefetchScalarGridSpec(
            num_scalar_prefetch=1,
            grid=(4,),
            in_specs=[
                act_spec,
                act_spec,
                pl.BlockSpec((rows, width), lambda step, flip_ref: (0, 0)),
            ],
            out_specs=(spec(3), spec(1), spec(3), spec(2)),
        ),
        out_shape=(shape,) * 4,
        cost_estimate=LIGHT,
        name="second_grad",
    )(flip, act_a, act_b, grad)


def place_of(step):
    return jnp.where(step == 0, 3, jnp.where(step == 3, 0, step))


def swap(values, axis, bits):
    size = lax.axis_size(axis)
    return lax.ppermute(values, axis, [(index, index ^ bits) for index in range(size)])


def swap_copies(parts):
    return swap(parts[1], "rep", 1), swap(parts[3], "rep", 2)


def sum_over_copies(parts, got_a, got_b):
    keep_a, _, keep_b, _ = parts
    more_a = swap(add_low(keep_a[1], got_a[1]), "rep", 2)
    more_b = swap(add_low(keep_b[1], got_b[1]), "rep", 1)
    half_a = keep_a[0].astype(F32) + got_a[0].astype(F32) + more_a.astype(F32)
    half_b = keep_b[0].astype(F32) + got_b[0].astype(F32) + more_b.astype(F32)
    return jnp.concatenate([half_a, half_b], 1)


def sum_halves(keep, got, steps):
    for axis, _, bits in steps:
        values = add_low(keep, got)
        half = values.shape[0] // 2
        keep, got = values[:half], swap(values[half:], axis, bits)
    return keep.astype(F32) + got.astype(F32)


def add_low(left, right):
    return (left.astype(F32) + right.astype(F32)).astype(BF16)


def spread(blocks):
    return {bits: swap(block, "ep", bits) if bits else block for bits, block in blocks.items()}


def cross(blocks, members):
    return swap(jnp.concatenate([blocks[bits][1:] for bits in members], 0), "ep", 1)


def paired_pieces(blocks, members):
    crossed = cross(blocks, members)
    pieces = [((blocks[bits], 0), (crossed, place)) for place, bits in enumerate(members)]
    return [piece for pair in pieces for piece in pair]


def exchange(buffer):
    return lax.all_to_all(buffer, "ep", split_axis=0, concat_axis=0, tiled=True)


def local(
    tokens_in,
    token_ids,
    hash_table,
    doc_lengths,
    gain_one,
    shift_one,
    project_in,
    project_out,
    gain_two,
    shift_two,
    expert_in,
    expert_out,
    out_grad,
):
    tok_rows, width = tokens_in.shape
    rep_size, ep_size = lax.axis_size("rep"), lax.axis_size("ep")
    rep_bits, ep_bits = rep_size.bit_length() - 1, ep_size.bit_length() - 1
    expert_count = expert_in.shape[0] * ep_size
    capacity = 2 * tok_rows // expert_count
    slot_total = expert_count * capacity
    tile = width // (rep_size * ep_size)
    paired = expert_count <= 8
    first_weight, second_weight = expert_in[0], expert_out[0]
    rep_index, ep_index = lax.axis_index("rep"), lax.axis_index("ep")
    ep_flip = jnp.reshape(ep_index if paired else 0, (1,)).astype(jnp.int32)
    rep_flip = jnp.reshape(rep_index, (1,)).astype(jnp.int32)
    rep_steps = [("rep", bit, 1 << bit) for bit in range(rep_bits)]
    if paired:
        ep_steps = [("ep", 2, 6), ("ep", 1, 2)]
    else:
        ep_steps = [("ep", bit, 1 << bit) for bit in range(1, ep_bits)]
    steps = ep_steps + rep_steps
    places = [bit + (ep_bits if axis == "rep" else 0) for axis, bit, _ in reversed(steps)] + [0]
    dense_order = (tuple(places), rep_bits + 1 if paired else 0)
    spot = spread_bits(rep_index * ep_size + ep_index, places)
    spot = jnp.reshape(spot, (1,)).astype(jnp.int32)

    fronts = (
        doc_lengths,
        tokens_in,
        gain_one,
        shift_one,
        project_in,
        project_out,
        gain_two,
        shift_two,
    )
    half_rows = slot_total // 2
    if paired:
        members = tuple(range(0, expert_count, 2))
        order = members[::2] + members[1::2]
        halves = (members[::2], members[1::2])
        block_rows, block_shape = capacity, (2, capacity, width)
    else:
        block_rows, block_shape = half_rows, (expert_count, capacity, width)
    slot_row, *buffers = route(
        ep_flip, token_ids, hash_table, out_grad, expert_count, capacity, block_shape
    )
    grads = spread(dict(zip(members, buffers))) if paired else exchange(buffers[0])
    normed, query, key, value, probs, mixture, hidden, *buffers = front(
        *fronts[:2], slot_row, *fronts[2:], slot_total, block_shape
    )
    if paired:
        blocks, hidden = lax.optimization_barrier(([grads[bits] for bits in members], hidden))
        grads = dict(zip(members, blocks))
        crossed = cross(grads, order)
        grad_pieces = []
        for index, half in enumerate(halves):
            grad_pieces += [(grads[bits], 0) for bits in half]
            grad_pieces += [(crossed, index * len(half) + place) for place in range(len(half))]
    else:
        grads = grads.reshape(2, half_rows, width)
        grad_pieces = [(grads, 0), (grads, 1)]
    grad_rows, grad_act = grad_act_of(second_weight, grad_pieces)
    outs = []
    if paired:
        received = spread(dict(zip(members, buffers)))
        count = len(halves[0])
        places = [[place * capacity, (count + place) * capacity] for place in range(count)]
        sent = {}
        done = grad_rows
        for index, half in ((1, halves[1]), (0, halves[0])):
            blocks, done = lax.optimization_barrier(([received[bits] for bits in half], done))
            received.update(zip(half, blocks))
            if index:
                grad_rows = done
            else:
                outs[0][2] = done
            crossed = cross(received, half)
            pieces = [(received[bits], 0) for bits in half]
            pieces += [(crossed, place) for place in range(count)]
            *out, = expert(index, grad_act, first_weight, pieces, places, capacity)
            outs.append(out[:3])
            done = out[2]
            sent.update(spread(dict(zip(half, out[3:]))))
        places += [[first + half_rows for first in firsts] for firsts in places]
    else:
        received = exchange(buffers[0]).reshape(2, half_rows, width)
        places = [[0]]
        for index in range(2):
            *out, = expert(index, grad_act, first_weight, [(received, index)], places, half_rows)
            outs.append(out)
        sent = jnp.concatenate([outs[0][3], outs[1][3]], 0).reshape(buffers[0].shape)
        back_pieces = [(exchange(sent).reshape(1, slot_total, width), 0)]
        places = [[0, half_rows]]
    if paired:
        outs = outs[::-1]
    (act_a, grad_pre_a, rows_a), (act_b, grad_pre_b, rows_b) = outs[0][:3], outs[1][:3]
    second_parts = second_grad(rep_flip, act_a, act_b, grad_rows)
    act_a, second_parts = lax.optimization_barrier((act_a, second_parts))
    results = result_of(act_a, act_b, second_weight, places, block_rows)
    got_second = swap_copies(second_parts)
    if paired:
        blocks, results = lax.optimization_barrier(([sent[bits] for bits in members], results))
        back_pieces = paired_pieces(dict(zip(members, blocks)), members)
    returned = spread(dict(zip(order, results))) if paired else exchange(
        results[0].reshape(expert_count, capacity, width)
    )
    keep, send, grad_in = back(
        tile,
        dense_order,
        spot,
        back_pieces,
        slot_row,
        hidden,
        gain_two,
        out_grad,
        mixture,
        project_out,
        query,
        key,
        value,
        probs,
        normed,
        project_in,
        tokens_in,
        gain_one,
    )
    send, got_second, returned = lax.optimization_barrier((send, got_second, returned))
    got = swap(send, "ep", 1)
    rows_a, keep = lax.optimization_barrier((rows_a, keep))
    first_parts = first_grad(rep_flip, rows_a, rows_b, grad_pre_a, grad_pre_b)
    got_first = swap_copies(first_parts)
    keep_first, got = lax.optimization_barrier((first_parts[0], got))
    dense = sum_halves(keep, got, steps)
    summed_second = sum_over_copies(second_parts, *got_second)
    summed_first = sum_over_copies([keep_first, *first_parts[1:]], *got_first)
    if paired:
        pieces = paired_pieces(returned, members)
    else:
        pieces = [(returned.reshape(1, slot_total, width), 0)]
    block_out = finish(hidden, slot_row, pieces)
    return (
        block_out,
        grad_in,
        dense[:, : 3 * width],
        dense[:, 3 * width : 4 * width],
        dense[:, 4 * width + 2],
        dense[:, 4 * width + 3],
        dense[:, 4 * width],
        dense[:, 4 * width + 1],
        summed_first[None],
        summed_second[None],
    )


def solution(mesh):
    in_specs = (
        P(("rep", "ep"), None),
        P(("rep", "ep")),
        P(),
        P(("rep", "ep"), None),
        P(),
        P(),
        P(),
        P(),
        P(),
        P(),
        P("ep", None, None),
        P("ep", None, None),
        P(("rep", "ep"), None),
    )
    out_specs = (
        P(("rep", "ep"), None),
        P(("rep", "ep"), None),
        P(("rep", "ep"), None),
        P(("rep", "ep"), None),
        P(("rep", "ep")),
        P(("rep", "ep")),
        P(("rep", "ep")),
        P(("rep", "ep")),
        P("ep", "rep", None),
        P("ep", "rep", None),
    )
    return jax.shard_map(local, mesh=mesh, in_specs=in_specs, out_specs=out_specs, check_vma=False)
```

```python
import functools
import math

import jax
import jax.numpy as jnp
from jax import lax
from jax.experimental import pallas as pl
from jax.experimental.pallas import tpu as pltpu
from jax.sharding import PartitionSpec as P

HEADS = 16
GROUP = 4
LANES = 128
NEG_LARGE = -1e30
EPSILON = 1e-05
BF16 = jnp.bfloat16
F32 = jnp.float32
GATE_A = math.sqrt(2.0 / math.pi)
GATE_B = GATE_A * 0.044715
LIGHT = pl.CostEstimate(flops=1 << 20, bytes_accessed=1 << 16, transcendentals=0)


def dot_nn(a, b):
    return lax.dot_general(a, b, (((1,), (0,)), ((), ())), preferred_element_type=F32)


def dot_nt(a, b):
    return lax.dot_general(a, b, (((1,), (1,)), ((), ())), preferred_element_type=F32)


def dot_tn(a, b):
    return lax.dot_general(a, b, (((0,), (0,)), ((), ())), preferred_element_type=F32)


def iota(shape, axis):
    return lax.broadcasted_iota(jnp.int32, shape, axis)


def whole(shape):
    return pl.BlockSpec(shape, lambda *_: (0,) * len(shape))


def piece_specs(pieces):
    def spec(array, block):
        return pl.BlockSpec((None,) + array.shape[1:], lambda *_: (block, 0, 0))

    return [spec(array, block) for array, block in pieces]


def stack_pieces(refs):
    return jnp.concatenate([ref[...] for ref in refs], 0)


def store_blocks(refs, values):
    first = 0
    for ref in refs:
        for block in range(ref.shape[0]):
            ref[block] = values[first : first + ref.shape[1]]
            first += ref.shape[1]


def norm_parts(values):
    center = jnp.mean(values, -1, keepdims=True)
    centered = values - center
    spread = jnp.mean(centered * centered, -1, keepdims=True)
    factor = lax.rsqrt(spread + EPSILON)
    return centered * factor, factor


def norm_back(grad, gain, xhat, factor):
    scaled = grad * gain
    mean_scaled = jnp.mean(scaled, -1, keepdims=True)
    mean_cross = jnp.mean(scaled * xhat, -1, keepdims=True)
    return factor * (scaled - mean_scaled - xhat * mean_cross)


def slot_matrix(slot_row, slot_total):
    tok_rows = slot_row.shape[1]
    return (iota((slot_total, tok_rows), 0) == slot_row).astype(F32).astype(BF16)


def route_kernel(
    expert_count, capacity, flip_ref, ids_ref, table_ref, grad_ref, slot_ref, *buffer_refs
):
    tok_rows = ids_ref.shape[1]
    ids = ids_ref[...]
    table_rows = table_ref.shape[0]
    high = ids // LANES
    low = ids - high * LANES
    high_hot = (iota((table_rows, tok_rows), 0) == high).astype(F32).astype(BF16)
    picked = dot_tn(table_ref[...].astype(F32).astype(BF16), high_hot)
    low_hot = iota((LANES, tok_rows), 0) == low
    expert = jnp.sum(jnp.where(low_hot, picked, 0.0), 0, keepdims=True).astype(jnp.int32)
    expert_hot = (iota((expert_count, tok_rows), 0) == expert).astype(F32)
    before = (iota((tok_rows, tok_rows), 0) < iota((tok_rows, tok_rows), 1)).astype(F32)
    earlier = dot_nn(expert_hot.astype(BF16), before.astype(BF16))
    rank = jnp.sum(earlier * expert_hot, 0, keepdims=True).astype(jnp.int32)
    slot = (expert ^ flip_ref[0]) * capacity + rank
    slot_ref[...] = slot
    slot_hot = slot_matrix(slot, expert_count * capacity)
    store_blocks(buffer_refs, dot_nn(slot_hot, grad_ref[...]).astype(BF16))


def route(flip, token_ids, hash_table, out_grad, expert_count, capacity, block_shape):
    tok_rows, width = out_grad.shape
    slot_total = expert_count * capacity
    table_rows = hash_table.shape[0] // LANES
    blocks = slot_total // (block_shape[0] * block_shape[1])
    return pl.pallas_call(
        functools.partial(route_kernel, expert_count, capacity),
        in_specs=[
            pl.BlockSpec(memory_space=pltpu.SMEM),
            whole((1, tok_rows)),
            whole((table_rows, LANES)),
            whole((tok_rows, width)),
        ],
        out_specs=(whole((1, tok_rows)),) + (whole(block_shape),) * blocks,
        out_shape=(jax.ShapeDtypeStruct((1, tok_rows), jnp.int32),)
        + (jax.ShapeDtypeStruct(block_shape, BF16),) * blocks,
        cost_estimate=LIGHT,
        name="route",
    )(flip, token_ids.reshape(1, tok_rows), hash_table.reshape(table_rows, LANES), out_grad)


def front_kernel(
    slot_total,
    head_size,
    lengths_ref,
    tokens_ref,
    slot_ref,
    gain_one_ref,
    shift_one_ref,
    query_weight_ref,
    key_weight_ref,
    value_weight_ref,
    out_weight_ref,
    gain_two_ref,
    shift_two_ref,
    normed_ref,
    query_ref,
    key_ref,
    value_ref,
    probs_ref,
    mixture_ref,
    hidden_ref,
    *refs,
):
    buffer_refs, mask_ref = refs[:-1], refs[-1]
    step = pl.program_id(0)
    tok_rows = tokens_ref.shape[0]
    group_width = query_ref.shape[1]

    @pl.when(step == 0)
    def _():
        inputs = tokens_ref[...].astype(F32)
        xhat, _ = norm_parts(inputs)
        normed_ref[...] = (xhat * gain_one_ref[...] + shift_one_ref[...]).astype(BF16)
        position = iota((1, tok_rows), 1)
        start = jnp.zeros((1, tok_rows), jnp.int32)
        bound = jnp.int32(0)
        for index in range(lengths_ref.shape[1]):
            bound = bound + lengths_ref[0, index]
            start = jnp.where(position >= bound, bound, start)
        key_position = iota((tok_rows, tok_rows), 0)
        allowed = jnp.logical_and(key_position >= start, key_position <= position)
        mask_ref[...] = jnp.where(allowed, 0.0, NEG_LARGE)
        hidden_ref[...] = inputs

    normed = normed_ref[...]
    query = dot_nn(normed, query_weight_ref[...]).astype(BF16)
    key = dot_nn(normed, key_weight_ref[...]).astype(BF16)
    value = dot_nn(normed, value_weight_ref[...]).astype(BF16)
    query_ref[...] = query
    key_ref[...] = key
    value_ref[...] = value
    lane_head = iota((1, group_width), 1) // head_size
    scale = 1.0 / math.sqrt(head_size)
    total = jnp.zeros((tok_rows, group_width), F32)
    for head in range(GROUP):
        chosen = lane_head == head
        key_part = key * jnp.where(chosen, scale, 0.0).astype(BF16)
        value_part = value * jnp.where(chosen, 1.0, 0.0).astype(BF16)
        scores = dot_nt(key_part, query) + mask_ref[...]
        exponent = jnp.exp(scores - jnp.max(scores, 0, keepdims=True))
        inverse = 1.0 / jnp.sum(exponent, 0, keepdims=True)
        weights = (exponent * inverse).astype(BF16)
        probs_ref[head] = weights
        total = total + dot_tn(weights, value_part)
    mixture = total.astype(BF16)
    mixture_ref[...] = mixture
    hidden_ref[...] += dot_nn(mixture, out_weight_ref[...])

    @pl.when(step == pl.num_programs(0) - 1)
    def _():
        xhat, _ = norm_parts(hidden_ref[...])
        routed = (xhat * gain_two_ref[...] + shift_two_ref[...]).astype(BF16)
        slot_hot = slot_matrix(slot_ref[...], slot_total)
        store_blocks(buffer_refs, dot_nn(slot_hot, routed).astype(BF16))


def front(
    doc_lengths,
    tokens_in,
    slot_row,
    gain_one,
    shift_one,
    project_in,
    project_out,
    gain_two,
    shift_two,
    slot_total,
    block_shape,
):
    tok_rows, width = tokens_in.shape
    head_size = width // HEADS
    group_width = GROUP * head_size
    steps = HEADS // GROUP
    vector = whole((1, width))
    blocks = slot_total // (block_shape[0] * block_shape[1])

    def weight_spec(part):
        return pl.BlockSpec((width, group_width), lambda step: (0, part * steps + step))

    column_spec = pl.BlockSpec((tok_rows, group_width), lambda step: (0, step))
    return pl.pallas_call(
        functools.partial(front_kernel, slot_total, head_size),
        grid=(steps,),
        in_specs=[
            pl.BlockSpec(memory_space=pltpu.SMEM),
            whole((tok_rows, width)),
            whole((1, tok_rows)),
            vector,
            vector,
            weight_spec(0),
            weight_spec(1),
            weight_spec(2),
            pl.BlockSpec((group_width, width), lambda step: (step, 0)),
            vector,
            vector,
        ],
        out_specs=(
            whole((tok_rows, width)),
            column_spec,
            column_spec,
            column_spec,
            pl.BlockSpec((GROUP, tok_rows, tok_rows), lambda step: (step, 0, 0)),
            column_spec,
            whole((tok_rows, width)),
        )
        + (whole(block_shape),) * blocks,
        out_shape=(
            jax.ShapeDtypeStruct((tok_rows, width), BF16),
            jax.ShapeDtypeStruct((tok_rows, width), BF16),
            jax.ShapeDtypeStruct((tok_rows, width), BF16),
            jax.ShapeDtypeStruct((tok_rows, width), BF16),
            jax.ShapeDtypeStruct((HEADS, tok_rows, tok_rows), BF16),
            jax.ShapeDtypeStruct((tok_rows, width), BF16),
            jax.ShapeDtypeStruct((tok_rows, width), F32),
        )
        + (jax.ShapeDtypeStruct(block_shape, BF16),) * blocks,
        scratch_shapes=[pltpu.VMEM((tok_rows, tok_rows), F32)],
        cost_estimate=LIGHT,
        name="front",
    )(
        doc_lengths,
        tokens_in,
        slot_row,
        gain_one.reshape(1, width),
        shift_one.reshape(1, width),
        project_in,
        project_in,
        project_in,
        project_out,
        gain_two.reshape(1, width),
        shift_two.reshape(1, width),
    )


def spread_bits(index, layout):
    spot = 0
    for place, bit in enumerate(layout):
        spot = spot | (((index >> bit) & 1) << place)
    return spot


def store_rows(refs, first, column, values, tile, order, spot):
    keep_ref, send_ref = refs
    layout = order
    top = len(layout) - 1
    even_kept = (spot >> top) == 0
    for index in range(0, values.shape[0] // tile, 2):
        place = (spread_bits(first + index, layout) ^ spot) & ((1 << top) - 1)
        even = values[index * tile : (index + 1) * tile]
        odd = values[(index + 1) * tile : (index + 2) * tile]
        rows = pl.ds(pl.multiple_of(place * tile, tile), tile)
        keep_ref[rows, column] = jnp.where(even_kept, even, odd).astype(BF16)
        send_ref[rows, column] = jnp.where(even_kept, odd, even).astype(BF16)


def back_kernel(
    head_size,
    tile,
    orders,
    piece_count,
    spot_ref,
    slot_ref,
    hidden_ref,
    gain_two_ref,
    out_grad_ref,
    mixture_ref,
    out_weight_ref,
    query_ref,
    key_ref,
    value_ref,
    probs_ref,
    normed_ref,
    query_weight_ref,
    key_weight_ref,
    value_weight_ref,
    tokens_ref,
    gain_one_ref,
    *refs,
):
    piece_refs = refs[:piece_count]
    dense_a = refs[piece_count : piece_count + 2]
    dense_b = refs[piece_count + 2 : piece_count + 4]
    grad_in_ref, hidden_low_ref, normed_grad_ref, small_ref = refs[piece_count + 4 :]
    step = pl.program_id(0)
    width = tokens_ref.shape[1]
    group_width = query_ref.shape[1]

    @pl.when(step == 0)
    def _():
        buffer = stack_pieces(piece_refs)
        slot_hot = slot_matrix(slot_ref[...], buffer.shape[0])
        grad_routed = dot_tn(slot_hot, buffer)
        xhat, factor = norm_parts(hidden_ref[...])
        small_ref[0:1, :] = jnp.sum(grad_routed * xhat, 0, keepdims=True)
        small_ref[1:2, :] = jnp.sum(grad_routed, 0, keepdims=True)
        grad_hidden = out_grad_ref[...].astype(F32) + norm_back(
            grad_routed, gain_two_ref[...], xhat, factor
        )
        grad_in_ref[...] = grad_hidden
        hidden_low_ref[...] = grad_hidden.astype(BF16)
        normed_grad_ref[...] = jnp.zeros_like(normed_grad_ref)
        small_ref[4:, :] = jnp.zeros((LANES - 4, width), F32)

    hidden_low = hidden_low_ref[...]
    store_rows(
        dense_b,
        step * (group_width // tile),
        slice(width, 2 * width),
        dot_tn(mixture_ref[...], hidden_low),
        tile,
        orders[1],
        spot_ref[1],
    )
    grad_mixture = dot_nt(hidden_low, out_weight_ref[...]).astype(BF16)
    query, key, value = query_ref[...], key_ref[...], value_ref[...]
    lane_head = iota((1, group_width), 1) // head_size
    scale = 1.0 / math.sqrt(head_size)
    grad_query = jnp.zeros(query.shape, F32)
    grad_key = jnp.zeros(query.shape, F32)
    grad_value = jnp.zeros(query.shape, F32)
    for head in range(GROUP):
        chosen = jnp.where(lane_head == head, 1.0, 0.0).astype(BF16)
        scaled = jnp.where(lane_head == head, scale, 0.0).astype(BF16)
        grad_part = grad_mixture * chosen
        weights_low = probs_ref[head]
        weights = weights_low.astype(F32)
        grad_weights = dot_nt(value, grad_part)
        inner = jnp.sum(weights * grad_weights, 0, keepdims=True)
        grad_scores = (weights * (grad_weights - inner)).astype(BF16)
        grad_query = grad_query + dot_tn(grad_scores, key * scaled)
        grad_key = grad_key + dot_nn(grad_scores, query * scaled)
        grad_value = grad_value + dot_nn(weights_low, grad_part)
    normed = normed_ref[...]
    for part, (grad, weight_ref) in enumerate(
        (
            (grad_query, query_weight_ref),
            (grad_key, key_weight_ref),
            (grad_value, value_weight_ref),
        )
    ):
        grad = grad.astype(BF16)
        index = part // 2
        column = pl.multiple_of((part % 2) * width + step * group_width, group_width)
        store_rows(
            (dense_a, dense_b)[index],
            0,
            pl.ds(column, group_width),
            dot_tn(normed, grad),
            tile,
            orders[index],
            spot_ref[index],
        )
        normed_grad_ref[...] += dot_nt(grad, weight_ref[...])

    @pl.when(step == pl.num_programs(0) - 1)
    def _():
        grad_normed = normed_grad_ref[...]
        xhat, factor = norm_parts(tokens_ref[...].astype(F32))
        small_ref[2:3, :] = jnp.sum(grad_normed * xhat, 0, keepdims=True)
        small_ref[3:4, :] = jnp.sum(grad_normed, 0, keepdims=True)
        store_rows(
            dense_a,
            0,
            slice(2 * width, 2 * width + LANES),
            small_ref[...].T,
            tile,
            orders[0],
            spot_ref[0],
        )
        grad_in_ref[...] += norm_back(grad_normed, gain_one_ref[...], xhat, factor)


def back(
    tile,
    orders,
    spots,
    pieces,
    slot_row,
    hidden,
    gain_two,
    out_grad,
    mixture,
    project_out,
    query,
    key,
    value,
    probs,
    normed,
    project_in,
    tokens_in,
    gain_one,
):
    tok_rows, width = tokens_in.shape
    head_size = width // HEADS
    group_width = GROUP * head_size
    steps = HEADS // GROUP
    vector = whole((1, width))
    tokens_spec = whole((tok_rows, width))

    def weight_spec(part):
        return pl.BlockSpec((width, group_width), lambda step: (0, part * steps + step))

    column_spec = pl.BlockSpec((tok_rows, group_width), lambda step: (0, step))
    return pl.pallas_call(
        functools.partial(back_kernel, head_size, tile, orders, len(pieces)),
        grid=(steps,),
        in_specs=[
            pl.BlockSpec(memory_space=pltpu.SMEM),
            whole((1, tok_rows)),
            tokens_spec,
            vector,
            tokens_spec,
            column_spec,
            pl.BlockSpec((group_width, width), lambda step: (step, 0)),
            column_spec,
            column_spec,
            column_spec,
            pl.BlockSpec((GROUP, tok_rows, tok_rows), lambda step: (step, 0, 0)),
            tokens_spec,
            weight_spec(0),
            weight_spec(1),
            weight_spec(2),
            tokens_spec,
            vector,
        ]
        + piece_specs(pieces),
        out_specs=(
            whole((width // 2, 2 * width + LANES)),
            whole((width // 2, 2 * width + LANES)),
            whole((width // 2, 2 * width)),
            whole((width // 2, 2 * width)),
            tokens_spec,
        ),
        out_shape=(
            jax.ShapeDtypeStruct((width // 2, 2 * width + LANES), BF16),
            jax.ShapeDtypeStruct((width // 2, 2 * width + LANES), BF16),
            jax.ShapeDtypeStruct((width // 2, 2 * width), BF16),
            jax.ShapeDtypeStruct((width // 2, 2 * width), BF16),
            jax.ShapeDtypeStruct((tok_rows, width), F32),
        ),
        scratch_shapes=[
            pltpu.VMEM((tok_rows, width), BF16),
            pltpu.VMEM((tok_rows, width), F32),
            pltpu.VMEM((LANES, width), F32),
        ],
        cost_estimate=LIGHT,
        name="back",
    )(
        spots,
        slot_row,
        hidden,
        gain_two.reshape(1, width),
        out_grad,
        mixture,
        project_out,
        query,
        key,
        value,
        probs,
        normed,
        project_in,
        project_in,
        project_in,
        tokens_in,
        gain_one.reshape(1, width),
        *[array for array, _ in pieces],
    )


def finish_kernel(hidden_ref, slot_ref, *refs):
    buffer = stack_pieces(refs[:-1])
    slot_hot = slot_matrix(slot_ref[...], buffer.shape[0])
    refs[-1][...] = (hidden_ref[...] + dot_tn(slot_hot, buffer)).astype(BF16)


def finish(hidden, slot_row, pieces):
    return pl.pallas_call(
        finish_kernel,
        grid=(1,),
        in_specs=[whole(hidden.shape), whole(slot_row.shape)] + piece_specs(pieces),
        out_specs=whole(hidden.shape),
        out_shape=jax.ShapeDtypeStruct(hidden.shape, BF16),
        cost_estimate=LIGHT,
        name="finish",
    )(hidden, slot_row, *[array for array, _ in pieces])


def grad_act_kernel(weight_ref, *refs):
    rows_ref, out_ref = refs[-2:]

    @pl.when(pl.program_id(0) == 0)
    def _():
        rows_ref[...] = stack_pieces(refs[:-2])

    out_ref[...] = dot_nt(rows_ref[...], weight_ref[...]).astype(BF16)


def grad_act_of(weight, pieces, chunk=1024):
    hidden_units, width = weight.shape
    rows = sum(array.shape[1] for array, _ in pieces)
    return pl.pallas_call(
        grad_act_kernel,
        grid=(hidden_units // chunk,),
        in_specs=[pl.BlockSpec((chunk, width), lambda step: (step, 0))] + piece_specs(pieces),
        out_specs=(whole((rows, width)), pl.BlockSpec((rows, chunk), lambda step: (0, step))),
        out_shape=(
            jax.ShapeDtypeStruct((rows, width), BF16),
            jax.ShapeDtypeStruct((rows, hidden_units), BF16),
        ),
        cost_estimate=LIGHT,
        name="grad_act",
    )(weight, *[array for array, _ in pieces])


def result_kernel(act_a_ref, act_b_ref, weight_ref, *refs, places):
    step = pl.program_id(0)
    total_ref = refs[-1]
    half = act_a_ref.shape[0]

    @pl.when(step == 0)
    def _():
        total_ref[...] = jnp.zeros_like(total_ref)

    total_ref[:half] += dot_nn(act_a_ref[...], weight_ref[...])
    total_ref[half:] += dot_nn(act_b_ref[...], weight_ref[...])

    @pl.when(step == pl.num_programs(0) - 1)
    def _():
        store_places(refs[:-1], total_ref, places)


def store_places(refs, total_ref, places):
    for ref, firsts in zip(refs, places):
        for block, first in enumerate(firsts):
            ref[block] = total_ref[first : first + ref.shape[1]].astype(BF16)


def result_of(act_a, act_b, weight, places, block_rows, chunk=1024):
    half, hidden_units = act_a.shape
    width = weight.shape[1]
    shapes = [(len(firsts), block_rows, width) for firsts in places]
    act_spec = pl.BlockSpec((half, chunk), lambda step: (0, step))
    return pl.pallas_call(
        functools.partial(result_kernel, places=places),
        grid=(hidden_units // chunk,),
        in_specs=[act_spec, act_spec, pl.BlockSpec((chunk, width), lambda step: (step, 0))],
        out_specs=tuple(whole(shape) for shape in shapes),
        out_shape=tuple(jax.ShapeDtypeStruct(shape, BF16) for shape in shapes),
        scratch_shapes=[pltpu.VMEM((2 * half, width), F32)],
        cost_estimate=LIGHT,
        name="result",
    )(act_a, act_b, weight)


def gate_parts(pre):
    square = pre * pre
    curve = jnp.tanh(pre * (GATE_A + GATE_B * square))
    half = 0.5 * curve + 0.5
    slope = half + (0.5 * pre) * (1.0 - curve * curve) * (GATE_A + (3.0 * GATE_B) * square)
    return pre * half, slope


def expert_kernel(tile, places, piece_count, grad_act_ref, weight_ref, *refs):
    step = pl.program_id(0)
    act_ref, grad_pre_ref, rows_ref = refs[piece_count : piece_count + 3]
    out_refs, total_ref = refs[piece_count + 3 : -1], refs[-1]

    @pl.when(step == 0)
    def _():
        rows_ref[...] = stack_pieces(refs[:piece_count])
        total_ref[...] = jnp.zeros_like(total_ref)

    weight = weight_ref[...]
    for first in range(0, rows_ref.shape[0], tile):
        rows = slice(first, first + tile)
        act, slope = gate_parts(dot_nn(rows_ref[rows, :], weight))
        act_ref[rows, :] = act.astype(BF16)
        grad_pre = (grad_act_ref[rows, :].astype(F32) * slope).astype(BF16)
        grad_pre_ref[rows, :] = grad_pre
        total_ref[rows, :] += dot_nt(grad_pre, weight)

    @pl.when(step == pl.num_programs(0) - 1)
    def _():
        store_places(out_refs, total_ref, places)


def expert(half, grad_act, weight, pieces, places, block_rows, chunk=1024, tile=256):
    width, hidden_units = weight.shape
    rows = grad_act.shape[0] // 2
    column_spec = pl.BlockSpec((rows, chunk), lambda step: (0, step))
    shapes = [(len(firsts), block_rows, width) for firsts in places]
    return pl.pallas_call(
        functools.partial(expert_kernel, tile, places, len(pieces)),
        grid=(hidden_units // chunk,),
        in_specs=[
            pl.BlockSpec((rows, chunk), lambda step: (half, step)),
            pl.BlockSpec((width, chunk), lambda step: (0, step)),
        ]
        + piece_specs(pieces),
        out_specs=(column_spec, column_spec, whole((rows, width)))
        + tuple(whole(shape) for shape in shapes),
        out_shape=(
            jax.ShapeDtypeStruct((rows, hidden_units), BF16),
            jax.ShapeDtypeStruct((rows, hidden_units), BF16),
            jax.ShapeDtypeStruct((rows, width), BF16),
        )
        + tuple(jax.ShapeDtypeStruct(shape, BF16) for shape in shapes),
        scratch_shapes=[pltpu.VMEM((rows, width), F32)],
        cost_estimate=LIGHT,
        name="expert",
    )(grad_act, weight, *[array for array, _ in pieces])


def first_grad_kernel(flip_ref, rows_a_ref, rows_b_ref, grad_a_ref, grad_b_ref, *refs):
    step = pl.program_id(0)
    half_steps = pl.num_programs(0) // 2
    product_ref = refs[-1]
    product = dot_tn(rows_a_ref[...], grad_a_ref[...]) + dot_tn(rows_b_ref[...], grad_b_ref[...])
    product_ref[...] = product.astype(BF16)
    owned = product_ref.shape[0] // 4

    def piece(place):
        row = pl.multiple_of((place ^ flip_ref[0]) * owned, owned)
        return product_ref[pl.ds(row, owned), :]

    keep_a, send_a, keep_b, send_b = refs[:-1]

    @pl.when(step < half_steps)
    def _():
        for index, (kept, sent) in enumerate(((0, 1), (2, 3))):
            keep_a[index] = piece(kept)
            send_a[index] = piece(sent)

    @pl.when(step >= half_steps)
    def _():
        for index, (kept, sent) in enumerate(((0, 2), (1, 3))):
            keep_b[index] = piece(kept)
            send_b[index] = piece(sent)


def first_grad(flip, rows_a, rows_b, grad_a, grad_b, chunk=1024):
    rows, width = rows_a.shape
    columns = grad_a.shape[1]
    steps = columns // chunk
    shape = jax.ShapeDtypeStruct((2, width // 4, columns // 2), BF16)
    block = (2, width // 4, chunk)
    spec_a = pl.BlockSpec(block, lambda step: (0, 0, jnp.minimum(step, steps // 2 - 1)))
    spec_b = pl.BlockSpec(block, lambda step: (0, 0, jnp.maximum(step - steps // 2, 0)))
    return pl.pallas_call(
        first_grad_kernel,
        grid=(steps,),
        in_specs=[
            pl.BlockSpec(memory_space=pltpu.SMEM),
            whole((rows, width)),
            whole((rows, width)),
            pl.BlockSpec((rows, chunk), lambda step: (0, step)),
            pl.BlockSpec((rows, chunk), lambda step: (0, step)),
        ],
        out_specs=(spec_a, spec_a, spec_b, spec_b),
        out_shape=(shape,) * 4,
        scratch_shapes=[pltpu.VMEM((width, chunk), BF16)],
        cost_estimate=LIGHT,
        name="first_grad",
    )(flip, rows_a, rows_b, grad_a, grad_b)


def second_grad_kernel(
    flip_ref, act_a_ref, act_b_ref, grad_ref, keep_a, send_a, keep_b, send_b
):
    step = pl.program_id(0)
    rows = act_a_ref.shape[0]
    product = dot_tn(act_a_ref[...], grad_ref[:rows]) + dot_tn(act_b_ref[...], grad_ref[rows:])
    product = product.astype(BF16)
    half = product.shape[1] // 2

    @pl.when(step == 0)
    def _():
        send_a[0] = product[:, :half]
        send_b[0] = product[:, half:]

    @pl.when(step == 1)
    def _():
        send_a[0] = product[:, :half]
        keep_b[0] = product[:, half:]

    @pl.when(step == 2)
    def _():
        keep_a[0] = product[:, :half]
        send_b[0] = product[:, half:]

    @pl.when(step == 3)
    def _():
        keep_a[0] = product[:, :half]
        keep_b[0] = product[:, half:]


def second_grad(flip, act_a, act_b, grad):
    rows, width = grad.shape
    owned = act_a.shape[1] // 4
    act_spec = pl.BlockSpec(
        (rows // 2, owned), lambda step, flip_ref: (0, place_of(step) ^ flip_ref[0])
    )
    shape = jax.ShapeDtypeStruct((2, owned, width // 2), BF16)
    block = (1, owned, width // 2)

    def spec(first_step):
        return pl.BlockSpec(
            block, lambda step, flip_ref: (1 - (step >= first_step).astype(jnp.int32), 0, 0)
        )

    return pl.pallas_call(
        second_grad_kernel,
        grid_spec=pltpu.PrefetchScalarGridSpec(
            num_scalar_prefetch=1,
            grid=(4,),
            in_specs=[
                act_spec,
                act_spec,
                pl.BlockSpec((rows, width), lambda step, flip_ref: (0, 0)),
            ],
            out_specs=(spec(3), spec(1), spec(3), spec(2)),
        ),
        out_shape=(shape,) * 4,
        cost_estimate=LIGHT,
        name="second_grad",
    )(flip, act_a, act_b, grad)


def place_of(step):
    return jnp.where(step == 0, 3, jnp.where(step == 3, 0, step))


def swap(values, axis, bits):
    size = lax.axis_size(axis)
    return lax.ppermute(values, axis, [(index, index ^ bits) for index in range(size)])


def swap_copies(parts):
    return swap(parts[1], "rep", 1), swap(parts[3], "rep", 2)


def half_sum_kernel(keep_ref, got_ref, out_ref):
    out_ref[...] = add_low(keep_ref[...], got_ref[...])


def half_sum(keep, got, chunks=2):
    _, rows, width = keep.shape
    block = (None, rows // chunks, width)
    return pl.pallas_call(
        half_sum_kernel,
        grid=(chunks,),
        in_specs=[pl.BlockSpec(block, lambda step: (1, step, 0))] * 2,
        out_specs=pl.BlockSpec(block[1:], lambda step: (step, 0)),
        out_shape=jax.ShapeDtypeStruct((rows, width), BF16),
        cost_estimate=LIGHT,
        name="half_sum",
    )(keep, got)


def copy_sum_kernel(*refs):
    out_ref = refs[-1]
    half = out_ref.shape[1] // 2
    for index, columns in ((0, slice(0, half)), (3, slice(half, 2 * half))):
        keep, got, more = [ref[...].astype(F32) for ref in refs[index : index + 3]]
        out_ref[:, columns] = keep + got + more


def copy_sum(parts, got, more):
    keep_a, _, keep_b, _ = parts
    chunks = 4
    _, rows, width = keep_a.shape
    first = pl.BlockSpec((None, rows // chunks, width), lambda step: (0, step, 0))
    plain = pl.BlockSpec((rows // chunks, width), lambda step: (step, 0))
    return pl.pallas_call(
        copy_sum_kernel,
        grid=(chunks,),
        in_specs=[first, first, plain] * 2,
        out_specs=pl.BlockSpec((rows // chunks, 2 * width), lambda step: (step, 0)),
        out_shape=jax.ShapeDtypeStruct((rows, 2 * width), F32),
        cost_estimate=LIGHT,
        name="copy_sum",
    )(keep_a, got[0], more[0], keep_b, got[1], more[1])


def split_sum_kernel(keep_low, keep_high, got_low, got_high, low_ref, high_ref):
    low_ref[...] = add_low(keep_low[...], got_low[...])
    high_ref[...] = add_low(keep_high[...], got_high[...])


def split_sum(keep, got):
    half, width = keep.shape[0] // 2, keep.shape[1]
    chunks = 2 if half % 64 == 0 else 1
    block = (half // chunks, width)
    low = pl.BlockSpec(block, lambda step: (step, 0))
    high = pl.BlockSpec(block, lambda step: (step + chunks, 0))
    return pl.pallas_call(
        split_sum_kernel,
        grid=(chunks,),
        in_specs=[low, high, low, high],
        out_specs=(low, low),
        out_shape=(jax.ShapeDtypeStruct((half, width), BF16),) * 2,
        cost_estimate=LIGHT,
        name="split_sum",
    )(keep, keep, got, got)


def swap_halves(dense, steps):
    return [swap(send, axis, 1 << bit) for (_, send), (axis, bit) in zip(dense, steps)]


def swap_sums(sums):
    return swap(sums[0], "rep", 2), swap(sums[1], "rep", 1)


def add_low(left, right):
    return (left.astype(F32) + right.astype(F32)).astype(BF16)


def spread(blocks):
    return {bits: swap(block, "ep", bits) if bits else block for bits, block in blocks.items()}


def gather_kernel(*refs):
    for index, ref in enumerate(refs[:-1]):
        refs[-1][index] = ref[...]


def cross(blocks, members):
    pieces = [(blocks[bits], 1) for bits in members]
    shape = (len(pieces),) + blocks[members[0]].shape[1:]
    gathered = pl.pallas_call(
        gather_kernel,
        grid=(1,),
        in_specs=piece_specs(pieces),
        out_specs=whole(shape),
        out_shape=jax.ShapeDtypeStruct(shape, BF16),
        cost_estimate=LIGHT,
        name="gather_sum",
    )(*[array for array, _ in pieces])
    return swap(gathered, "ep", 1)


def paired_pieces(blocks, members):
    crossed = cross(blocks, members)
    pieces = [((blocks[bits], 0), (crossed, place)) for place, bits in enumerate(members)]
    return [piece for pair in pieces for piece in pair]


def exchange(buffer):
    return lax.all_to_all(buffer, "ep", split_axis=0, concat_axis=0, tiled=True)


def local(
    tokens_in,
    token_ids,
    hash_table,
    doc_lengths,
    gain_one,
    shift_one,
    project_in,
    project_out,
    gain_two,
    shift_two,
    expert_in,
    expert_out,
    out_grad,
):
    tok_rows, width = tokens_in.shape
    rep_size, ep_size = lax.axis_size("rep"), lax.axis_size("ep")
    rep_bits, ep_bits = rep_size.bit_length() - 1, ep_size.bit_length() - 1
    expert_count = expert_in.shape[0] * ep_size
    capacity = 2 * tok_rows // expert_count
    slot_total = expert_count * capacity
    tile = width // (rep_size * ep_size)
    paired = expert_count <= 8
    first_weight, second_weight = expert_in[0], expert_out[0]
    rep_index, ep_index = lax.axis_index("rep"), lax.axis_index("ep")
    ep_flip = jnp.reshape(ep_index if paired else 0, (1,)).astype(jnp.int32)
    rep_flip = jnp.reshape(rep_index, (1,)).astype(jnp.int32)
    ep_steps = [("ep", bit) for bit in range(1, ep_bits)]
    rep_steps = [("rep", bit) for bit in range(rep_bits)]
    steps_a, steps_b = ep_steps + rep_steps, ep_steps[::-1] + rep_steps[::-1]
    orders, spots = [], []
    for steps in (steps_a, steps_b):
        places = [bit + (ep_bits if axis == "rep" else 0) for axis, bit in reversed(steps)] + [0]
        orders.append(tuple(places))
        spots.append(spread_bits(rep_index * ep_size + ep_index, places))
    spots = jnp.stack(spots).astype(jnp.int32)

    fronts = (
        doc_lengths,
        tokens_in,
        gain_one,
        shift_one,
        project_in,
        project_out,
        gain_two,
        shift_two,
    )
    half_rows = slot_total // 2
    if paired:
        members = tuple(range(0, expert_count, 2))
        order = members[::2] + members[1::2]
        halves = (members[::2], members[1::2])
        block_rows, block_shape = capacity, (2, capacity, width)
    else:
        block_rows, block_shape = half_rows, (expert_count, capacity, width)
    slot_row, *buffers = route(
        ep_flip, token_ids, hash_table, out_grad, expert_count, capacity, block_shape
    )
    grads = spread(dict(zip(members, buffers))) if paired else exchange(buffers[0])
    normed, query, key, value, probs, mixture, hidden, *buffers = front(
        *fronts[:2], slot_row, *fronts[2:], slot_total, block_shape
    )
    if paired:
        blocks, hidden = lax.optimization_barrier(([grads[bits] for bits in members], hidden))
        grads = dict(zip(members, blocks))
        crossed = cross(grads, order)
        grad_pieces = []
        for index, half in enumerate(halves):
            grad_pieces += [(grads[bits], 0) for bits in half]
            grad_pieces += [(crossed, index * len(half) + place) for place in range(len(half))]
    else:
        grads = grads.reshape(2, half_rows, width)
        grad_pieces = [(grads, 0), (grads, 1)]
    grad_rows, grad_act = grad_act_of(second_weight, grad_pieces)
    outs = []
    if paired:
        received = spread(dict(zip(members, buffers)))
        count = len(halves[0])
        places = [[place * capacity, (count + place) * capacity] for place in range(count)]
        sent = {}
        done = grad_rows
        for index, half in ((1, halves[1]), (0, halves[0])):
            blocks, done = lax.optimization_barrier(([received[bits] for bits in half], done))
            received.update(zip(half, blocks))
            if index:
                grad_rows = done
            else:
                outs[0][2] = done
            crossed = cross(received, half)
            pieces = [(received[bits], 0) for bits in half]
            pieces += [(crossed, place) for place in range(count)]
            *out, = expert(index, grad_act, first_weight, pieces, places, capacity)
            outs.append(out[:3])
            done = out[2]
            sent.update(spread(dict(zip(half, out[3:]))))
        places += [[first + half_rows for first in firsts] for firsts in places]
    else:
        received = exchange(buffers[0]).reshape(2, half_rows, width)
        places = [[0]]
        for index in range(2):
            *out, = expert(index, grad_act, first_weight, [(received, index)], places, half_rows)
            outs.append(out)
        sent = jnp.concatenate([outs[0][3], outs[1][3]], 0).reshape(buffers[0].shape)
        back_pieces = [(exchange(sent).reshape(1, slot_total, width), 0)]
        places = [[0, half_rows]]
    if paired:
        outs = outs[::-1]
    (act_a, grad_pre_a, rows_a), (act_b, grad_pre_b, rows_b) = outs[0][:3], outs[1][:3]
    second_parts = second_grad(rep_flip, act_a, act_b, grad_rows)
    act_a, second_parts = lax.optimization_barrier((act_a, second_parts))
    results = result_of(act_a, act_b, second_weight, places, block_rows)
    got_second = swap_copies(second_parts)
    if paired:
        blocks, results = lax.optimization_barrier(([sent[bits] for bits in members], results))
        back_pieces = paired_pieces(dict(zip(members, blocks)), members)
    returned = spread(dict(zip(order, results))) if paired else exchange(
        results[0].reshape(expert_count, capacity, width)
    )
    keep_a, send_a, keep_b, send_b, grad_in = back(
        tile,
        orders,
        spots,
        back_pieces,
        slot_row,
        hidden,
        gain_two,
        out_grad,
        mixture,
        project_out,
        query,
        key,
        value,
        probs,
        normed,
        project_in,
        tokens_in,
        gain_one,
    )
    sends = (send_a, send_b)
    sends, got_second, returned = lax.optimization_barrier((sends, got_second, returned))
    got_a, got_b = swap(sends[0], "ep", 1), swap(sends[1], "ep", 1)
    sums_second = [half_sum(second_parts[2 * index], got_second[index]) for index in (0, 1)]
    dense = [split_sum(keep_a, got_a), split_sum(keep_b, got_b)]
    rows_a, dense, sums_second = lax.optimization_barrier((rows_a, dense, sums_second))
    got = swap_halves(dense, (steps_a[0], steps_b[0]))
    more_second = swap_sums(sums_second)
    first_parts = first_grad(rep_flip, rows_a, rows_b, grad_pre_a, grad_pre_b)
    first_parts, more_second = lax.optimization_barrier((first_parts, more_second))
    got_first = swap_copies(first_parts)
    summed_second = copy_sum(second_parts, got_second, more_second)
    keep_a, send_a, keep_b, send_b = first_parts
    for index, pair in enumerate(zip(steps_a, steps_b)):
        if index == 0:
            got, keep_b = lax.optimization_barrier((got, keep_b))
        else:
            got = swap_halves(dense, pair)
        if index == 1:
            got, got_first = lax.optimization_barrier((got, got_first))
        if index < len(steps_a) - 1:
            dense = [split_sum(keep, more) for (keep, _), more in zip(dense, got)]
    dense_a, dense_b = [keep.astype(F32) + more.astype(F32) for (keep, _), more in zip(dense, got)]
    first_parts = (keep_a, send_a, keep_b, send_b)
    sums_first = [half_sum(first_parts[2 * index], got_first[index]) for index in (0, 1)]
    summed_first = copy_sum(first_parts, got_first, swap_sums(sums_first))
    if paired:
        pieces = paired_pieces(returned, members)
    else:
        pieces = [(returned.reshape(1, slot_total, width), 0)]
    block_out = finish(hidden, slot_row, pieces)
    return (
        block_out,
        grad_in,
        jnp.concatenate([dense_a[:, : 2 * width], dense_b[:, :width]], 1),
        dense_b[:, width:],
        dense_a[:, 2 * width + 2],
        dense_a[:, 2 * width + 3],
        dense_a[:, 2 * width],
        dense_a[:, 2 * width + 1],
        summed_first[None],
        summed_second[None],
    )


def solution(mesh):
    in_specs = (
        P(("rep", "ep"), None),
        P(("rep", "ep")),
        P(),
        P(("rep", "ep"), None),
        P(),
        P(),
        P(),
        P(),
        P(),
        P(),
        P("ep", None, None),
        P("ep", None, None),
        P(("rep", "ep"), None),
    )
    out_specs = (
        P(("rep", "ep"), None),
        P(("rep", "ep"), None),
        P(("rep", "ep"), None),
        P(("rep", "ep"), None),
        P(("rep", "ep")),
        P(("rep", "ep")),
        P(("rep", "ep")),
        P(("rep", "ep")),
        P("ep", "rep", None),
        P("ep", "rep", None),
    )
    return jax.shard_map(local, mesh=mesh, in_specs=in_specs, out_specs=out_specs, check_vma=False)
```

```python
import functools
import math

import jax
import jax.numpy as jnp
from jax import lax
from jax.experimental import pallas as pl
from jax.experimental.pallas import tpu as pltpu
from jax.sharding import PartitionSpec as P

HEADS = 16
GROUP = 4
LANES = 128
NEG_LARGE = -1e30
EPSILON = 1e-05
BF16 = jnp.bfloat16
F32 = jnp.float32
GATE_A = math.sqrt(2.0 / math.pi)
GATE_B = GATE_A * 0.044715
LIGHT = pl.CostEstimate(flops=1 << 20, bytes_accessed=1 << 16, transcendentals=0)


def dot_nn(a, b):
    return lax.dot_general(a, b, (((1,), (0,)), ((), ())), preferred_element_type=F32)


def dot_nt(a, b):
    return lax.dot_general(a, b, (((1,), (1,)), ((), ())), preferred_element_type=F32)


def dot_tn(a, b):
    return lax.dot_general(a, b, (((0,), (0,)), ((), ())), preferred_element_type=F32)


def iota(shape, axis):
    return lax.broadcasted_iota(jnp.int32, shape, axis)


def whole(shape):
    return pl.BlockSpec(shape, lambda *_: (0,) * len(shape))


def piece_specs(pieces):
    def spec(array, block):
        return pl.BlockSpec((None,) + array.shape[1:], lambda *_: (block, 0, 0))

    return [spec(array, block) for array, block in pieces]


def stack_pieces(refs):
    return jnp.concatenate([ref[...] for ref in refs], 0)


def store_blocks(refs, values):
    first = 0
    for ref in refs:
        for block in range(ref.shape[0]):
            ref[block] = values[first : first + ref.shape[1]]
            first += ref.shape[1]


def norm_parts(values):
    center = jnp.mean(values, -1, keepdims=True)
    centered = values - center
    spread = jnp.mean(centered * centered, -1, keepdims=True)
    factor = lax.rsqrt(spread + EPSILON)
    return centered * factor, factor


def norm_back(grad, gain, xhat, factor):
    scaled = grad * gain
    mean_scaled = jnp.mean(scaled, -1, keepdims=True)
    mean_cross = jnp.mean(scaled * xhat, -1, keepdims=True)
    return factor * (scaled - mean_scaled - xhat * mean_cross)


def slot_matrix(slot_row, slot_total):
    tok_rows = slot_row.shape[1]
    return (iota((slot_total, tok_rows), 0) == slot_row).astype(F32).astype(BF16)


def route_kernel(
    expert_count, capacity, flip_ref, ids_ref, table_ref, grad_ref, slot_ref, *buffer_refs
):
    tok_rows = ids_ref.shape[1]
    ids = ids_ref[...]
    table_rows = table_ref.shape[0]
    high = ids // LANES
    low = ids - high * LANES
    high_hot = (iota((table_rows, tok_rows), 0) == high).astype(F32).astype(BF16)
    picked = dot_tn(table_ref[...].astype(F32).astype(BF16), high_hot)
    low_hot = iota((LANES, tok_rows), 0) == low
    expert = jnp.sum(jnp.where(low_hot, picked, 0.0), 0, keepdims=True).astype(jnp.int32)
    expert_hot = (iota((expert_count, tok_rows), 0) == expert).astype(F32)
    before = (iota((tok_rows, tok_rows), 0) < iota((tok_rows, tok_rows), 1)).astype(F32)
    earlier = dot_nn(expert_hot.astype(BF16), before.astype(BF16))
    rank = jnp.sum(earlier * expert_hot, 0, keepdims=True).astype(jnp.int32)
    slot = (expert ^ flip_ref[0]) * capacity + rank
    slot_ref[...] = slot
    slot_hot = slot_matrix(slot, expert_count * capacity)
    store_blocks(buffer_refs, dot_nn(slot_hot, grad_ref[...]).astype(BF16))


def route(flip, token_ids, hash_table, out_grad, expert_count, capacity, block_shape):
    tok_rows, width = out_grad.shape
    slot_total = expert_count * capacity
    table_rows = hash_table.shape[0] // LANES
    blocks = slot_total // (block_shape[0] * block_shape[1])
    return pl.pallas_call(
        functools.partial(route_kernel, expert_count, capacity),
        in_specs=[
            pl.BlockSpec(memory_space=pltpu.SMEM),
            whole((1, tok_rows)),
            whole((table_rows, LANES)),
            whole((tok_rows, width)),
        ],
        out_specs=(whole((1, tok_rows)),) + (whole(block_shape),) * blocks,
        out_shape=(jax.ShapeDtypeStruct((1, tok_rows), jnp.int32),)
        + (jax.ShapeDtypeStruct(block_shape, BF16),) * blocks,
        cost_estimate=LIGHT,
        name="route",
    )(flip, token_ids.reshape(1, tok_rows), hash_table.reshape(table_rows, LANES), out_grad)


def front_kernel(
    slot_total,
    head_size,
    lengths_ref,
    tokens_ref,
    slot_ref,
    gain_one_ref,
    shift_one_ref,
    query_weight_ref,
    key_weight_ref,
    value_weight_ref,
    out_weight_ref,
    gain_two_ref,
    shift_two_ref,
    normed_ref,
    query_ref,
    key_ref,
    value_ref,
    probs_ref,
    mixture_ref,
    hidden_ref,
    *refs,
):
    buffer_refs, mask_ref = refs[:-1], refs[-1]
    step = pl.program_id(0)
    tok_rows = tokens_ref.shape[0]
    group_width = query_ref.shape[1]

    @pl.when(step == 0)
    def _():
        inputs = tokens_ref[...].astype(F32)
        xhat, _ = norm_parts(inputs)
        normed_ref[...] = (xhat * gain_one_ref[...] + shift_one_ref[...]).astype(BF16)
        position = iota((1, tok_rows), 1)
        start = jnp.zeros((1, tok_rows), jnp.int32)
        bound = jnp.int32(0)
        for index in range(lengths_ref.shape[1]):
            bound = bound + lengths_ref[0, index]
            start = jnp.where(position >= bound, bound, start)
        key_position = iota((tok_rows, tok_rows), 0)
        allowed = jnp.logical_and(key_position >= start, key_position <= position)
        mask_ref[...] = jnp.where(allowed, 0.0, NEG_LARGE)
        hidden_ref[...] = inputs

    normed = normed_ref[...]
    query = dot_nn(normed, query_weight_ref[...]).astype(BF16)
    key = dot_nn(normed, key_weight_ref[...]).astype(BF16)
    value = dot_nn(normed, value_weight_ref[...]).astype(BF16)
    query_ref[...] = query
    key_ref[...] = key
    value_ref[...] = value
    lane_head = iota((1, group_width), 1) // head_size
    scale = 1.0 / math.sqrt(head_size)
    total = jnp.zeros((tok_rows, group_width), F32)
    for head in range(GROUP):
        chosen = lane_head == head
        key_part = key * jnp.where(chosen, scale, 0.0).astype(BF16)
        value_part = value * jnp.where(chosen, 1.0, 0.0).astype(BF16)
        scores = dot_nt(key_part, query) + mask_ref[...]
        exponent = jnp.exp(scores - jnp.max(scores, 0, keepdims=True))
        inverse = 1.0 / jnp.sum(exponent, 0, keepdims=True)
        weights = (exponent * inverse).astype(BF16)
        probs_ref[head] = weights
        total = total + dot_tn(weights, value_part)
    mixture = total.astype(BF16)
    mixture_ref[...] = mixture
    hidden_ref[...] += dot_nn(mixture, out_weight_ref[...])

    @pl.when(step == pl.num_programs(0) - 1)
    def _():
        xhat, _ = norm_parts(hidden_ref[...])
        routed = (xhat * gain_two_ref[...] + shift_two_ref[...]).astype(BF16)
        slot_hot = slot_matrix(slot_ref[...], slot_total)
        store_blocks(buffer_refs, dot_nn(slot_hot, routed).astype(BF16))


def front(
    doc_lengths,
    tokens_in,
    slot_row,
    gain_one,
    shift_one,
    project_in,
    project_out,
    gain_two,
    shift_two,
    slot_total,
    block_shape,
):
    tok_rows, width = tokens_in.shape
    head_size = width // HEADS
    group_width = GROUP * head_size
    steps = HEADS // GROUP
    vector = whole((1, width))
    blocks = slot_total // (block_shape[0] * block_shape[1])

    def weight_spec(part):
        return pl.BlockSpec((width, group_width), lambda step: (0, part * steps + step))

    column_spec = pl.BlockSpec((tok_rows, group_width), lambda step: (0, step))
    return pl.pallas_call(
        functools.partial(front_kernel, slot_total, head_size),
        grid=(steps,),
        in_specs=[
            pl.BlockSpec(memory_space=pltpu.SMEM),
            whole((tok_rows, width)),
            whole((1, tok_rows)),
            vector,
            vector,
            weight_spec(0),
            weight_spec(1),
            weight_spec(2),
            pl.BlockSpec((group_width, width), lambda step: (step, 0)),
            vector,
            vector,
        ],
        out_specs=(
            whole((tok_rows, width)),
            column_spec,
            column_spec,
            column_spec,
            pl.BlockSpec((GROUP, tok_rows, tok_rows), lambda step: (step, 0, 0)),
            column_spec,
            whole((tok_rows, width)),
        )
        + (whole(block_shape),) * blocks,
        out_shape=(
            jax.ShapeDtypeStruct((tok_rows, width), BF16),
            jax.ShapeDtypeStruct((tok_rows, width), BF16),
            jax.ShapeDtypeStruct((tok_rows, width), BF16),
            jax.ShapeDtypeStruct((tok_rows, width), BF16),
            jax.ShapeDtypeStruct((HEADS, tok_rows, tok_rows), BF16),
            jax.ShapeDtypeStruct((tok_rows, width), BF16),
            jax.ShapeDtypeStruct((tok_rows, width), F32),
        )
        + (jax.ShapeDtypeStruct(block_shape, BF16),) * blocks,
        scratch_shapes=[pltpu.VMEM((tok_rows, tok_rows), F32)],
        cost_estimate=LIGHT,
        name="front",
    )(
        doc_lengths,
        tokens_in,
        slot_row,
        gain_one.reshape(1, width),
        shift_one.reshape(1, width),
        project_in,
        project_in,
        project_in,
        project_out,
        gain_two.reshape(1, width),
        shift_two.reshape(1, width),
    )


def spread_bits(index, layout):
    spot = 0
    for place, bit in enumerate(layout):
        spot = spot | (((index >> bit) & 1) << place)
    return spot


def store_rows(refs, first, column, values, tile, order, spot):
    keep_ref, send_ref = refs
    layout = order
    top = len(layout) - 1
    even_kept = (spot >> top) == 0
    for index in range(0, values.shape[0] // tile, 2):
        place = (spread_bits(first + index, layout) ^ spot) & ((1 << top) - 1)
        even = values[index * tile : (index + 1) * tile]
        odd = values[(index + 1) * tile : (index + 2) * tile]
        rows = pl.ds(pl.multiple_of(place * tile, tile), tile)
        keep_ref[rows, column] = jnp.where(even_kept, even, odd).astype(BF16)
        send_ref[rows, column] = jnp.where(even_kept, odd, even).astype(BF16)


def back_kernel(
    head_size,
    tile,
    orders,
    piece_count,
    spot_ref,
    slot_ref,
    hidden_ref,
    gain_two_ref,
    out_grad_ref,
    mixture_ref,
    out_weight_ref,
    query_ref,
    key_ref,
    value_ref,
    probs_ref,
    normed_ref,
    query_weight_ref,
    key_weight_ref,
    value_weight_ref,
    tokens_ref,
    gain_one_ref,
    *refs,
):
    piece_refs = refs[:piece_count]
    dense_a = refs[piece_count : piece_count + 2]
    dense_b = refs[piece_count + 2 : piece_count + 4]
    grad_in_ref, hidden_low_ref, normed_grad_ref, small_ref = refs[piece_count + 4 :]
    step = pl.program_id(0)
    width = tokens_ref.shape[1]
    group_width = query_ref.shape[1]

    @pl.when(step == 0)
    def _():
        buffer = stack_pieces(piece_refs)
        slot_hot = slot_matrix(slot_ref[...], buffer.shape[0])
        grad_routed = dot_tn(slot_hot, buffer)
        xhat, factor = norm_parts(hidden_ref[...])
        small_ref[0:1, :] = jnp.sum(grad_routed * xhat, 0, keepdims=True)
        small_ref[1:2, :] = jnp.sum(grad_routed, 0, keepdims=True)
        grad_hidden = out_grad_ref[...].astype(F32) + norm_back(
            grad_routed, gain_two_ref[...], xhat, factor
        )
        grad_in_ref[...] = grad_hidden
        hidden_low_ref[...] = grad_hidden.astype(BF16)
        normed_grad_ref[...] = jnp.zeros_like(normed_grad_ref)
        small_ref[4:, :] = jnp.zeros((LANES - 4, width), F32)

    hidden_low = hidden_low_ref[...]
    store_rows(
        dense_b,
        step * (group_width // tile),
        slice(width, 2 * width),
        dot_tn(mixture_ref[...], hidden_low),
        tile,
        orders[1],
        spot_ref[1],
    )
    grad_mixture = dot_nt(hidden_low, out_weight_ref[...]).astype(BF16)
    query, key, value = query_ref[...], key_ref[...], value_ref[...]
    lane_head = iota((1, group_width), 1) // head_size
    scale = 1.0 / math.sqrt(head_size)
    grad_query = jnp.zeros(query.shape, F32)
    grad_key = jnp.zeros(query.shape, F32)
    grad_value = jnp.zeros(query.shape, F32)
    for head in range(GROUP):
        chosen = jnp.where(lane_head == head, 1.0, 0.0).astype(BF16)
        scaled = jnp.where(lane_head == head, scale, 0.0).astype(BF16)
        grad_part = grad_mixture * chosen
        weights_low = probs_ref[head]
        weights = weights_low.astype(F32)
        grad_weights = dot_nt(value, grad_part)
        inner = jnp.sum(weights * grad_weights, 0, keepdims=True)
        grad_scores = (weights * (grad_weights - inner)).astype(BF16)
        grad_query = grad_query + dot_tn(grad_scores, key * scaled)
        grad_key = grad_key + dot_nn(grad_scores, query * scaled)
        grad_value = grad_value + dot_nn(weights_low, grad_part)
    normed = normed_ref[...]
    for part, (grad, weight_ref) in enumerate(
        (
            (grad_query, query_weight_ref),
            (grad_key, key_weight_ref),
            (grad_value, value_weight_ref),
        )
    ):
        grad = grad.astype(BF16)
        index = part // 2
        column = pl.multiple_of((part % 2) * width + step * group_width, group_width)
        store_rows(
            (dense_a, dense_b)[index],
            0,
            pl.ds(column, group_width),
            dot_tn(normed, grad),
            tile,
            orders[index],
            spot_ref[index],
        )
        normed_grad_ref[...] += dot_nt(grad, weight_ref[...])

    @pl.when(step == pl.num_programs(0) - 1)
    def _():
        grad_normed = normed_grad_ref[...]
        xhat, factor = norm_parts(tokens_ref[...].astype(F32))
        small_ref[2:3, :] = jnp.sum(grad_normed * xhat, 0, keepdims=True)
        small_ref[3:4, :] = jnp.sum(grad_normed, 0, keepdims=True)
        store_rows(
            dense_a,
            0,
            slice(2 * width, 2 * width + LANES),
            small_ref[...].T,
            tile,
            orders[0],
            spot_ref[0],
        )
        grad_in_ref[...] += norm_back(grad_normed, gain_one_ref[...], xhat, factor)


def back(
    tile,
    orders,
    spots,
    pieces,
    slot_row,
    hidden,
    gain_two,
    out_grad,
    mixture,
    project_out,
    query,
    key,
    value,
    probs,
    normed,
    project_in,
    tokens_in,
    gain_one,
):
    tok_rows, width = tokens_in.shape
    head_size = width // HEADS
    group_width = GROUP * head_size
    steps = HEADS // GROUP
    vector = whole((1, width))
    tokens_spec = whole((tok_rows, width))

    def weight_spec(part):
        return pl.BlockSpec((width, group_width), lambda step: (0, part * steps + step))

    column_spec = pl.BlockSpec((tok_rows, group_width), lambda step: (0, step))
    return pl.pallas_call(
        functools.partial(back_kernel, head_size, tile, orders, len(pieces)),
        grid=(steps,),
        in_specs=[
            pl.BlockSpec(memory_space=pltpu.SMEM),
            whole((1, tok_rows)),
            tokens_spec,
            vector,
            tokens_spec,
            column_spec,
            pl.BlockSpec((group_width, width), lambda step: (step, 0)),
            column_spec,
            column_spec,
            column_spec,
            pl.BlockSpec((GROUP, tok_rows, tok_rows), lambda step: (step, 0, 0)),
            tokens_spec,
            weight_spec(0),
            weight_spec(1),
            weight_spec(2),
            tokens_spec,
            vector,
        ]
        + piece_specs(pieces),
        out_specs=(
            whole((width // 2, 2 * width + LANES)),
            whole((width // 2, 2 * width + LANES)),
            whole((width // 2, 2 * width)),
            whole((width // 2, 2 * width)),
            tokens_spec,
        ),
        out_shape=(
            jax.ShapeDtypeStruct((width // 2, 2 * width + LANES), BF16),
            jax.ShapeDtypeStruct((width // 2, 2 * width + LANES), BF16),
            jax.ShapeDtypeStruct((width // 2, 2 * width), BF16),
            jax.ShapeDtypeStruct((width // 2, 2 * width), BF16),
            jax.ShapeDtypeStruct((tok_rows, width), F32),
        ),
        scratch_shapes=[
            pltpu.VMEM((tok_rows, width), BF16),
            pltpu.VMEM((tok_rows, width), F32),
            pltpu.VMEM((LANES, width), F32),
        ],
        cost_estimate=LIGHT,
        name="back",
    )(
        spots,
        slot_row,
        hidden,
        gain_two.reshape(1, width),
        out_grad,
        mixture,
        project_out,
        query,
        key,
        value,
        probs,
        normed,
        project_in,
        project_in,
        project_in,
        tokens_in,
        gain_one.reshape(1, width),
        *[array for array, _ in pieces],
    )


def finish_kernel(hidden_ref, slot_ref, *refs):
    buffer = stack_pieces(refs[:-1])
    slot_hot = slot_matrix(slot_ref[...], buffer.shape[0])
    refs[-1][...] = (hidden_ref[...] + dot_tn(slot_hot, buffer)).astype(BF16)


def finish(hidden, slot_row, pieces):
    return pl.pallas_call(
        finish_kernel,
        grid=(1,),
        in_specs=[whole(hidden.shape), whole(slot_row.shape)] + piece_specs(pieces),
        out_specs=whole(hidden.shape),
        out_shape=jax.ShapeDtypeStruct(hidden.shape, BF16),
        cost_estimate=LIGHT,
        name="finish",
    )(hidden, slot_row, *[array for array, _ in pieces])


def grad_act_kernel(weight_ref, *refs):
    rows_ref, out_ref = refs[-2:]

    @pl.when(pl.program_id(0) == 0)
    def _():
        rows_ref[...] = stack_pieces(refs[:-2])

    out_ref[...] = dot_nt(rows_ref[...], weight_ref[...]).astype(BF16)


def grad_act_of(weight, pieces, chunk=1024):
    hidden_units, width = weight.shape
    rows = sum(array.shape[1] for array, _ in pieces)
    return pl.pallas_call(
        grad_act_kernel,
        grid=(hidden_units // chunk,),
        in_specs=[pl.BlockSpec((chunk, width), lambda step: (step, 0))] + piece_specs(pieces),
        out_specs=(whole((rows, width)), pl.BlockSpec((rows, chunk), lambda step: (0, step))),
        out_shape=(
            jax.ShapeDtypeStruct((rows, width), BF16),
            jax.ShapeDtypeStruct((rows, hidden_units), BF16),
        ),
        cost_estimate=LIGHT,
        name="grad_act",
    )(weight, *[array for array, _ in pieces])


def result_kernel(act_a_ref, act_b_ref, weight_ref, *refs, places):
    step = pl.program_id(0)
    total_ref = refs[-1]
    half = act_a_ref.shape[0]

    @pl.when(step == 0)
    def _():
        total_ref[...] = jnp.zeros_like(total_ref)

    total_ref[:half] += dot_nn(act_a_ref[...], weight_ref[...])
    total_ref[half:] += dot_nn(act_b_ref[...], weight_ref[...])

    @pl.when(step == pl.num_programs(0) - 1)
    def _():
        store_places(refs[:-1], total_ref, places)


def store_places(refs, total_ref, places):
    for ref, firsts in zip(refs, places):
        for block, first in enumerate(firsts):
            ref[block] = total_ref[first : first + ref.shape[1]].astype(BF16)


def result_of(act_a, act_b, weight, places, block_rows, chunk=1024):
    half, hidden_units = act_a.shape
    width = weight.shape[1]
    shapes = [(len(firsts), block_rows, width) for firsts in places]
    act_spec = pl.BlockSpec((half, chunk), lambda step: (0, step))
    return pl.pallas_call(
        functools.partial(result_kernel, places=places),
        grid=(hidden_units // chunk,),
        in_specs=[act_spec, act_spec, pl.BlockSpec((chunk, width), lambda step: (step, 0))],
        out_specs=tuple(whole(shape) for shape in shapes),
        out_shape=tuple(jax.ShapeDtypeStruct(shape, BF16) for shape in shapes),
        scratch_shapes=[pltpu.VMEM((2 * half, width), F32)],
        cost_estimate=LIGHT,
        name="result",
    )(act_a, act_b, weight)


def gate_parts(pre):
    square = pre * pre
    curve = jnp.tanh(pre * (GATE_A + GATE_B * square))
    half = 0.5 * curve + 0.5
    slope = half + (0.5 * pre) * (1.0 - curve * curve) * (GATE_A + (3.0 * GATE_B) * square)
    return pre * half, slope


def expert_kernel(tile, places, piece_count, grad_act_ref, weight_ref, *refs):
    step = pl.program_id(0)
    act_ref, grad_pre_ref, rows_ref = refs[piece_count : piece_count + 3]
    out_refs, total_ref = refs[piece_count + 3 : -1], refs[-1]

    @pl.when(step == 0)
    def _():
        rows_ref[...] = stack_pieces(refs[:piece_count])
        total_ref[...] = jnp.zeros_like(total_ref)

    weight = weight_ref[...]
    for first in range(0, rows_ref.shape[0], tile):
        rows = slice(first, first + tile)
        act, slope = gate_parts(dot_nn(rows_ref[rows, :], weight))
        act_ref[rows, :] = act.astype(BF16)
        grad_pre = (grad_act_ref[rows, :].astype(F32) * slope).astype(BF16)
        grad_pre_ref[rows, :] = grad_pre
        total_ref[rows, :] += dot_nt(grad_pre, weight)

    @pl.when(step == pl.num_programs(0) - 1)
    def _():
        store_places(out_refs, total_ref, places)


def expert(half, grad_act, weight, pieces, places, block_rows, chunk=1024, tile=256):
    width, hidden_units = weight.shape
    rows = grad_act.shape[0] // 2
    column_spec = pl.BlockSpec((rows, chunk), lambda step: (0, step))
    shapes = [(len(firsts), block_rows, width) for firsts in places]
    return pl.pallas_call(
        functools.partial(expert_kernel, tile, places, len(pieces)),
        grid=(hidden_units // chunk,),
        in_specs=[
            pl.BlockSpec((rows, chunk), lambda step: (half, step)),
            pl.BlockSpec((width, chunk), lambda step: (0, step)),
        ]
        + piece_specs(pieces),
        out_specs=(column_spec, column_spec, whole((rows, width)))
        + tuple(whole(shape) for shape in shapes),
        out_shape=(
            jax.ShapeDtypeStruct((rows, hidden_units), BF16),
            jax.ShapeDtypeStruct((rows, hidden_units), BF16),
            jax.ShapeDtypeStruct((rows, width), BF16),
        )
        + tuple(jax.ShapeDtypeStruct(shape, BF16) for shape in shapes),
        scratch_shapes=[pltpu.VMEM((rows, width), F32)],
        cost_estimate=LIGHT,
        name="expert",
    )(grad_act, weight, *[array for array, _ in pieces])


def first_grad_kernel(flip_ref, rows_a_ref, rows_b_ref, grad_a_ref, grad_b_ref, *refs):
    step = pl.program_id(0)
    half_steps = pl.num_programs(0) // 2
    product_ref = refs[-1]
    product = dot_tn(rows_a_ref[...], grad_a_ref[...]) + dot_tn(rows_b_ref[...], grad_b_ref[...])
    product_ref[...] = product.astype(BF16)
    owned = product_ref.shape[0] // 4

    def piece(place):
        row = pl.multiple_of((place ^ flip_ref[0]) * owned, owned)
        return product_ref[pl.ds(row, owned), :]

    keep_a, send_a, keep_b, send_b = refs[:-1]

    @pl.when(step < half_steps)
    def _():
        for index, (kept, sent) in enumerate(((0, 1), (2, 3))):
            keep_a[index] = piece(kept)
            send_a[index] = piece(sent)

    @pl.when(step >= half_steps)
    def _():
        for index, (kept, sent) in enumerate(((0, 2), (1, 3))):
            keep_b[index] = piece(kept)
            send_b[index] = piece(sent)


def first_grad(flip, rows_a, rows_b, grad_a, grad_b, chunk=1024):
    rows, width = rows_a.shape
    columns = grad_a.shape[1]
    steps = columns // chunk
    shape = jax.ShapeDtypeStruct((2, width // 4, columns // 2), BF16)
    block = (2, width // 4, chunk)
    spec_a = pl.BlockSpec(block, lambda step: (0, 0, jnp.minimum(step, steps // 2 - 1)))
    spec_b = pl.BlockSpec(block, lambda step: (0, 0, jnp.maximum(step - steps // 2, 0)))
    return pl.pallas_call(
        first_grad_kernel,
        grid=(steps,),
        in_specs=[
            pl.BlockSpec(memory_space=pltpu.SMEM),
            whole((rows, width)),
            whole((rows, width)),
            pl.BlockSpec((rows, chunk), lambda step: (0, step)),
            pl.BlockSpec((rows, chunk), lambda step: (0, step)),
        ],
        out_specs=(spec_a, spec_a, spec_b, spec_b),
        out_shape=(shape,) * 4,
        scratch_shapes=[pltpu.VMEM((width, chunk), BF16)],
        cost_estimate=LIGHT,
        name="first_grad",
    )(flip, rows_a, rows_b, grad_a, grad_b)


def second_grad_kernel(
    flip_ref, act_a_ref, act_b_ref, grad_ref, keep_a, send_a, keep_b, send_b
):
    step = pl.program_id(0)
    rows = act_a_ref.shape[0]
    product = dot_tn(act_a_ref[...], grad_ref[:rows]) + dot_tn(act_b_ref[...], grad_ref[rows:])
    product = product.astype(BF16)
    half = product.shape[1] // 2

    @pl.when(step == 0)
    def _():
        send_a[0] = product[:, :half]
        send_b[0] = product[:, half:]

    @pl.when(step == 1)
    def _():
        send_a[0] = product[:, :half]
        keep_b[0] = product[:, half:]

    @pl.when(step == 2)
    def _():
        keep_a[0] = product[:, :half]
        send_b[0] = product[:, half:]

    @pl.when(step == 3)
    def _():
        keep_a[0] = product[:, :half]
        keep_b[0] = product[:, half:]


def second_grad(flip, act_a, act_b, grad):
    rows, width = grad.shape
    owned = act_a.shape[1] // 4
    act_spec = pl.BlockSpec(
        (rows // 2, owned), lambda step, flip_ref: (0, place_of(step) ^ flip_ref[0])
    )
    shape = jax.ShapeDtypeStruct((2, owned, width // 2), BF16)
    block = (1, owned, width // 2)

    def spec(first_step):
        return pl.BlockSpec(
            block, lambda step, flip_ref: (1 - (step >= first_step).astype(jnp.int32), 0, 0)
        )

    return pl.pallas_call(
        second_grad_kernel,
        grid_spec=pltpu.PrefetchScalarGridSpec(
            num_scalar_prefetch=1,
            grid=(4,),
            in_specs=[
                act_spec,
                act_spec,
                pl.BlockSpec((rows, width), lambda step, flip_ref: (0, 0)),
            ],
            out_specs=(spec(3), spec(1), spec(3), spec(2)),
        ),
        out_shape=(shape,) * 4,
        cost_estimate=LIGHT,
        name="second_grad",
    )(flip, act_a, act_b, grad)


def place_of(step):
    return jnp.where(step == 0, 3, jnp.where(step == 3, 0, step))


def swap(values, axis, bits):
    size = lax.axis_size(axis)
    return lax.ppermute(values, axis, [(index, index ^ bits) for index in range(size)])


def swap_copies(parts):
    return swap(parts[1], "rep", 1), swap(parts[3], "rep", 2)


def half_sum_kernel(keep_a, got_a, keep_b, got_b, out_a, out_b):
    out_a[...] = add_low(keep_a[...], got_a[...])
    out_b[...] = add_low(keep_b[...], got_b[...])


def half_sums(parts, got, chunks=4):
    _, rows, width = got[0].shape
    block = (None, rows // chunks, width)
    out_spec = pl.BlockSpec(block[1:], lambda step: (step, 0))
    return pl.pallas_call(
        half_sum_kernel,
        grid=(chunks,),
        in_specs=[pl.BlockSpec(block, lambda step: (1, step, 0))] * 4,
        out_specs=(out_spec,) * 2,
        out_shape=(jax.ShapeDtypeStruct((rows, width), BF16),) * 2,
        cost_estimate=LIGHT,
        name="half_sum",
    )(parts[0], got[0], parts[2], got[1])


def copy_sum_kernel(*refs):
    out_ref = refs[-1]
    half = out_ref.shape[1] // 2
    for index, columns in ((0, slice(0, half)), (3, slice(half, 2 * half))):
        keep, got, more = [ref[...].astype(F32) for ref in refs[index : index + 3]]
        out_ref[:, columns] = keep + got + more


def copy_sum(parts, got, more):
    keep_a, _, keep_b, _ = parts
    chunks = 8
    _, rows, width = keep_a.shape
    first = pl.BlockSpec((None, rows // chunks, width), lambda step: (0, step, 0))
    plain = pl.BlockSpec((rows // chunks, width), lambda step: (step, 0))
    return pl.pallas_call(
        copy_sum_kernel,
        grid=(chunks,),
        in_specs=[first, first, plain] * 2,
        out_specs=pl.BlockSpec((rows // chunks, 2 * width), lambda step: (step, 0)),
        out_shape=jax.ShapeDtypeStruct((rows, 2 * width), F32),
        cost_estimate=LIGHT,
        name="copy_sum",
    )(keep_a, got[0], more[0], keep_b, got[1], more[1])


def split_sum_kernel(keep_low, keep_high, got_low, got_high, low_ref, high_ref):
    low_ref[...] = add_low(keep_low[...], got_low[...])
    high_ref[...] = add_low(keep_high[...], got_high[...])


def split_sum(keep, got):
    half, width = keep.shape[0] // 2, keep.shape[1]
    chunks = 4 if half % 128 == 0 else 1
    block = (half // chunks, width)
    low = pl.BlockSpec(block, lambda step: (step, 0))
    high = pl.BlockSpec(block, lambda step: (step + chunks, 0))
    return pl.pallas_call(
        split_sum_kernel,
        grid=(chunks,),
        in_specs=[low, high, low, high],
        out_specs=(low, low),
        out_shape=(jax.ShapeDtypeStruct((half, width), BF16),) * 2,
        cost_estimate=LIGHT,
        name="split_sum",
    )(keep, keep, got, got)


def swap_halves(dense, steps):
    return [swap(send, axis, 1 << bit) for (_, send), (axis, bit) in zip(dense, steps)]


def swap_sums(sums):
    return swap(sums[0], "rep", 2), swap(sums[1], "rep", 1)


def add_low(left, right):
    return (left.astype(F32) + right.astype(F32)).astype(BF16)


def spread(blocks):
    return {bits: swap(block, "ep", bits) if bits else block for bits, block in blocks.items()}


def gather_kernel(*refs):
    for index, ref in enumerate(refs[:-1]):
        refs[-1][index] = ref[...]


def cross(blocks, members):
    return swap(jnp.concatenate([blocks[bits][1:] for bits in members], 0), "ep", 1)


def cross_late(blocks, members):
    pieces = [(blocks[bits], 1) for bits in members]
    shape = (len(pieces),) + blocks[members[0]].shape[1:]
    gathered = pl.pallas_call(
        gather_kernel,
        grid=(1,),
        in_specs=piece_specs(pieces),
        out_specs=whole(shape),
        out_shape=jax.ShapeDtypeStruct(shape, BF16),
        cost_estimate=LIGHT,
        name="gather_sum",
    )(*[array for array, _ in pieces])
    return swap(gathered, "ep", 1)


def paired_pieces(blocks, members, cross):
    crossed = cross(blocks, members)
    pieces = [((blocks[bits], 0), (crossed, place)) for place, bits in enumerate(members)]
    return [piece for pair in pieces for piece in pair]


def exchange(buffer):
    return lax.all_to_all(buffer, "ep", split_axis=0, concat_axis=0, tiled=True)


def local(
    tokens_in,
    token_ids,
    hash_table,
    doc_lengths,
    gain_one,
    shift_one,
    project_in,
    project_out,
    gain_two,
    shift_two,
    expert_in,
    expert_out,
    out_grad,
):
    tok_rows, width = tokens_in.shape
    rep_size, ep_size = lax.axis_size("rep"), lax.axis_size("ep")
    rep_bits, ep_bits = rep_size.bit_length() - 1, ep_size.bit_length() - 1
    expert_count = expert_in.shape[0] * ep_size
    capacity = 2 * tok_rows // expert_count
    slot_total = expert_count * capacity
    tile = width // (rep_size * ep_size)
    paired = expert_count <= 8
    first_weight, second_weight = expert_in[0], expert_out[0]
    rep_index, ep_index = lax.axis_index("rep"), lax.axis_index("ep")
    ep_flip = jnp.reshape(ep_index if paired else 0, (1,)).astype(jnp.int32)
    rep_flip = jnp.reshape(rep_index, (1,)).astype(jnp.int32)
    ep_steps = [("ep", bit) for bit in range(1, ep_bits)]
    rep_steps = [("rep", bit) for bit in range(rep_bits)]
    steps_a, steps_b = ep_steps + rep_steps, ep_steps[::-1] + rep_steps[::-1]
    orders, spots = [], []
    for steps in (steps_a, steps_b):
        places = [bit + (ep_bits if axis == "rep" else 0) for axis, bit in reversed(steps)] + [0]
        orders.append(tuple(places))
        spots.append(spread_bits(rep_index * ep_size + ep_index, places))
    spots = jnp.stack(spots).astype(jnp.int32)

    fronts = (
        doc_lengths,
        tokens_in,
        gain_one,
        shift_one,
        project_in,
        project_out,
        gain_two,
        shift_two,
    )
    half_rows = slot_total // 2
    if paired:
        members = tuple(range(0, expert_count, 2))
        order = members[::2] + members[1::2]
        halves = (members[::2], members[1::2])
        block_rows, block_shape = capacity, (2, capacity, width)
    else:
        block_rows, block_shape = half_rows, (expert_count, capacity, width)
    slot_row, *buffers = route(
        ep_flip, token_ids, hash_table, out_grad, expert_count, capacity, block_shape
    )
    grads = spread(dict(zip(members, buffers))) if paired else exchange(buffers[0])
    normed, query, key, value, probs, mixture, hidden, *buffers = front(
        *fronts[:2], slot_row, *fronts[2:], slot_total, block_shape
    )
    if paired:
        blocks, hidden = lax.optimization_barrier(([grads[bits] for bits in members], hidden))
        grads = dict(zip(members, blocks))
        crossed = cross(grads, order)
        grad_pieces = []
        for index, half in enumerate(halves):
            grad_pieces += [(grads[bits], 0) for bits in half]
            grad_pieces += [(crossed, index * len(half) + place) for place in range(len(half))]
    else:
        grads = grads.reshape(2, half_rows, width)
        grad_pieces = [(grads, 0), (grads, 1)]
    grad_rows, grad_act = grad_act_of(second_weight, grad_pieces)
    outs = []
    if paired:
        received = spread(dict(zip(members, buffers)))
        count = len(halves[0])
        places = [[place * capacity, (count + place) * capacity] for place in range(count)]
        sent = {}
        done = grad_rows
        for index, half in ((1, halves[1]), (0, halves[0])):
            blocks, done = lax.optimization_barrier(([received[bits] for bits in half], done))
            received.update(zip(half, blocks))
            if index:
                grad_rows = done
            else:
                outs[0][2] = done
            crossed = cross(received, half)
            pieces = [(received[bits], 0) for bits in half]
            pieces += [(crossed, place) for place in range(count)]
            *out, = expert(index, grad_act, first_weight, pieces, places, capacity)
            outs.append(out[:3])
            done = out[2]
            sent.update(spread(dict(zip(half, out[3:]))))
        places += [[first + half_rows for first in firsts] for firsts in places]
    else:
        received = exchange(buffers[0]).reshape(2, half_rows, width)
        places = [[0]]
        for index in range(2):
            *out, = expert(index, grad_act, first_weight, [(received, index)], places, half_rows)
            outs.append(out)
        sent = jnp.concatenate([outs[0][3], outs[1][3]], 0).reshape(buffers[0].shape)
        back_pieces = [(exchange(sent).reshape(1, slot_total, width), 0)]
        places = [[0, half_rows]]
    if paired:
        outs = outs[::-1]
    (act_a, grad_pre_a, rows_a), (act_b, grad_pre_b, rows_b) = outs[0][:3], outs[1][:3]
    second_parts = second_grad(rep_flip, act_a, act_b, grad_rows)
    act_a, second_parts = lax.optimization_barrier((act_a, second_parts))
    results = result_of(act_a, act_b, second_weight, places, block_rows)
    got_second = swap_copies(second_parts)
    if paired:
        blocks, results = lax.optimization_barrier(([sent[bits] for bits in members], results))
        back_pieces = paired_pieces(dict(zip(members, blocks)), members, cross)
    returned = spread(dict(zip(order, results))) if paired else exchange(
        results[0].reshape(expert_count, capacity, width)
    )
    keep_a, send_a, keep_b, send_b, grad_in = back(
        tile,
        orders,
        spots,
        back_pieces,
        slot_row,
        hidden,
        gain_two,
        out_grad,
        mixture,
        project_out,
        query,
        key,
        value,
        probs,
        normed,
        project_in,
        tokens_in,
        gain_one,
    )
    sends = (send_a, send_b)
    sends, got_second, returned = lax.optimization_barrier((sends, got_second, returned))
    got_a, got_b = swap(sends[0], "ep", 1), swap(sends[1], "ep", 1)
    sums_second = half_sums(second_parts, got_second)
    rows_a, sums_second = lax.optimization_barrier((rows_a, sums_second))
    more_second = swap_sums(sums_second)
    first_parts = first_grad(rep_flip, rows_a, rows_b, grad_pre_a, grad_pre_b)
    got_a, got_b, first_parts = lax.optimization_barrier((got_a, got_b, first_parts))
    dense = [split_sum(keep_a, got_a), split_sum(keep_b, got_b)]
    dense, first_parts, more_second = lax.optimization_barrier((dense, first_parts, more_second))
    got_first = swap_copies(first_parts)
    summed_second = copy_sum(second_parts, got_second, more_second)
    if paired:
        pieces = paired_pieces(returned, members, cross_late)
    else:
        pieces = [(returned.reshape(1, slot_total, width), 0)]
    block_out = finish(hidden, slot_row, pieces)
    for index, pair in enumerate(zip(steps_a, steps_b)):
        got = swap_halves(dense, pair)
        if index == 0:
            got, got_first, summed_second, block_out = lax.optimization_barrier(
                (got, got_first, summed_second, block_out)
            )
            sums_first, got = lax.optimization_barrier((half_sums(first_parts, got_first), got))
            more_first = swap_sums(sums_first)
        if index == 1:
            got, more_first = lax.optimization_barrier((got, more_first))
            summed_first = copy_sum(first_parts, got_first, more_first)
        if index == 2:
            got, summed_first = lax.optimization_barrier((got, summed_first))
        if index < len(steps_a) - 1:
            dense = [split_sum(keep, more) for (keep, _), more in zip(dense, got)]
    dense_a, dense_b = [keep.astype(F32) + more.astype(F32) for (keep, _), more in zip(dense, got)]
    return (
        block_out,
        grad_in,
        jnp.concatenate([dense_a[:, : 2 * width], dense_b[:, :width]], 1),
        dense_b[:, width:],
        dense_a[:, 2 * width + 2],
        dense_a[:, 2 * width + 3],
        dense_a[:, 2 * width],
        dense_a[:, 2 * width + 1],
        summed_first[None],
        summed_second[None],
    )


def solution(mesh):
    in_specs = (
        P(("rep", "ep"), None),
        P(("rep", "ep")),
        P(),
        P(("rep", "ep"), None),
        P(),
        P(),
        P(),
        P(),
        P(),
        P(),
        P("ep", None, None),
        P("ep", None, None),
        P(("rep", "ep"), None),
    )
    out_specs = (
        P(("rep", "ep"), None),
        P(("rep", "ep"), None),
        P(("rep", "ep"), None),
        P(("rep", "ep"), None),
        P(("rep", "ep")),
        P(("rep", "ep")),
        P(("rep", "ep")),
        P(("rep", "ep")),
        P("ep", "rep", None),
        P("ep", "rep", None),
    )
    return jax.shard_map(local, mesh=mesh, in_specs=in_specs, out_specs=out_specs, check_vma=False)
```

```python
import functools
import math

import jax
import jax.numpy as jnp
from jax import lax
from jax.experimental import pallas as pl
from jax.experimental.pallas import tpu as pltpu
from jax.sharding import PartitionSpec as P

HEADS = 16
GROUP = 4
LANES = 128
NEG_LARGE = -1e30
EPSILON = 1e-05
BF16 = jnp.bfloat16
F32 = jnp.float32
GATE_A = math.sqrt(2.0 / math.pi)
GATE_B = GATE_A * 0.044715
LIGHT = pl.CostEstimate(flops=1 << 20, bytes_accessed=1 << 16, transcendentals=0)


def dot_nn(a, b):
    return lax.dot_general(a, b, (((1,), (0,)), ((), ())), preferred_element_type=F32)


def dot_nt(a, b):
    return lax.dot_general(a, b, (((1,), (1,)), ((), ())), preferred_element_type=F32)


def dot_tn(a, b):
    return lax.dot_general(a, b, (((0,), (0,)), ((), ())), preferred_element_type=F32)


def iota(shape, axis):
    return lax.broadcasted_iota(jnp.int32, shape, axis)


def whole(shape):
    return pl.BlockSpec(shape, lambda *_: (0,) * len(shape))


def piece_specs(pieces):
    def spec(array, block):
        return pl.BlockSpec((None,) + array.shape[1:], lambda *_: (block, 0, 0))

    return [spec(array, block) for array, block in pieces]


def stack_pieces(refs):
    return jnp.concatenate([ref[...] for ref in refs], 0)


def store_blocks(refs, values):
    first = 0
    for ref in refs:
        for block in range(ref.shape[0]):
            ref[block] = values[first : first + ref.shape[1]]
            first += ref.shape[1]


def norm_parts(values):
    center = jnp.mean(values, -1, keepdims=True)
    centered = values - center
    spread = jnp.mean(centered * centered, -1, keepdims=True)
    factor = lax.rsqrt(spread + EPSILON)
    return centered * factor, factor


def norm_back(grad, gain, xhat, factor):
    scaled = grad * gain
    mean_scaled = jnp.mean(scaled, -1, keepdims=True)
    mean_cross = jnp.mean(scaled * xhat, -1, keepdims=True)
    return factor * (scaled - mean_scaled - xhat * mean_cross)


def slot_matrix(slot_row, slot_total):
    tok_rows = slot_row.shape[1]
    return (iota((slot_total, tok_rows), 0) == slot_row).astype(F32).astype(BF16)


def route_kernel(
    expert_count, capacity, flip_ref, ids_ref, table_ref, grad_ref, slot_ref, *buffer_refs
):
    tok_rows = ids_ref.shape[1]
    ids = ids_ref[...]
    table_rows = table_ref.shape[0]
    high = ids // LANES
    low = ids - high * LANES
    high_hot = (iota((table_rows, tok_rows), 0) == high).astype(F32).astype(BF16)
    picked = dot_tn(table_ref[...].astype(F32).astype(BF16), high_hot)
    low_hot = iota((LANES, tok_rows), 0) == low
    expert = jnp.sum(jnp.where(low_hot, picked, 0.0), 0, keepdims=True).astype(jnp.int32)
    expert_hot = (iota((expert_count, tok_rows), 0) == expert).astype(F32)
    before = (iota((tok_rows, tok_rows), 0) < iota((tok_rows, tok_rows), 1)).astype(F32)
    earlier = dot_nn(expert_hot.astype(BF16), before.astype(BF16))
    rank = jnp.sum(earlier * expert_hot, 0, keepdims=True).astype(jnp.int32)
    slot = (expert ^ flip_ref[0]) * capacity + rank
    slot_ref[...] = slot
    slot_hot = slot_matrix(slot, expert_count * capacity)
    store_blocks(buffer_refs, dot_nn(slot_hot, grad_ref[...]).astype(BF16))


def route(flip, token_ids, hash_table, out_grad, expert_count, capacity, block_shape):
    tok_rows, width = out_grad.shape
    slot_total = expert_count * capacity
    table_rows = hash_table.shape[0] // LANES
    blocks = slot_total // (block_shape[0] * block_shape[1])
    return pl.pallas_call(
        functools.partial(route_kernel, expert_count, capacity),
        in_specs=[
            pl.BlockSpec(memory_space=pltpu.SMEM),
            whole((1, tok_rows)),
            whole((table_rows, LANES)),
            whole((tok_rows, width)),
        ],
        out_specs=(whole((1, tok_rows)),) + (whole(block_shape),) * blocks,
        out_shape=(jax.ShapeDtypeStruct((1, tok_rows), jnp.int32),)
        + (jax.ShapeDtypeStruct(block_shape, BF16),) * blocks,
        cost_estimate=LIGHT,
        name="route",
    )(flip, token_ids.reshape(1, tok_rows), hash_table.reshape(table_rows, LANES), out_grad)


def front_kernel(
    slot_total,
    head_size,
    lengths_ref,
    tokens_ref,
    slot_ref,
    gain_one_ref,
    shift_one_ref,
    query_weight_ref,
    key_weight_ref,
    value_weight_ref,
    out_weight_ref,
    gain_two_ref,
    shift_two_ref,
    normed_ref,
    query_ref,
    key_ref,
    value_ref,
    probs_ref,
    mixture_ref,
    hidden_ref,
    *refs,
):
    buffer_refs, mask_ref = refs[:-1], refs[-1]
    step = pl.program_id(0)
    tok_rows = tokens_ref.shape[0]
    group_width = query_ref.shape[1]

    @pl.when(step == 0)
    def _():
        inputs = tokens_ref[...].astype(F32)
        xhat, _ = norm_parts(inputs)
        normed_ref[...] = (xhat * gain_one_ref[...] + shift_one_ref[...]).astype(BF16)
        position = iota((1, tok_rows), 1)
        start = jnp.zeros((1, tok_rows), jnp.int32)
        bound = jnp.int32(0)
        for index in range(lengths_ref.shape[1]):
            bound = bound + lengths_ref[0, index]
            start = jnp.where(position >= bound, bound, start)
        key_position = iota((tok_rows, tok_rows), 0)
        allowed = jnp.logical_and(key_position >= start, key_position <= position)
        mask_ref[...] = jnp.where(allowed, 0.0, NEG_LARGE)
        hidden_ref[...] = inputs

    normed = normed_ref[...]
    query = dot_nn(normed, query_weight_ref[...]).astype(BF16)
    key = dot_nn(normed, key_weight_ref[...]).astype(BF16)
    value = dot_nn(normed, value_weight_ref[...]).astype(BF16)
    query_ref[...] = query
    key_ref[...] = key
    value_ref[...] = value
    lane_head = iota((1, group_width), 1) // head_size
    scale = 1.0 / math.sqrt(head_size)
    total = jnp.zeros((tok_rows, group_width), F32)
    for head in range(GROUP):
        chosen = lane_head == head
        key_part = key * jnp.where(chosen, scale, 0.0).astype(BF16)
        value_part = value * jnp.where(chosen, 1.0, 0.0).astype(BF16)
        scores = dot_nt(key_part, query) + mask_ref[...]
        exponent = jnp.exp(scores - jnp.max(scores, 0, keepdims=True))
        inverse = 1.0 / jnp.sum(exponent, 0, keepdims=True)
        weights = (exponent * inverse).astype(BF16)
        probs_ref[head] = weights
        total = total + dot_tn(weights, value_part)
    mixture = total.astype(BF16)
    mixture_ref[...] = mixture
    hidden_ref[...] += dot_nn(mixture, out_weight_ref[...])

    @pl.when(step == pl.num_programs(0) - 1)
    def _():
        xhat, _ = norm_parts(hidden_ref[...])
        routed = (xhat * gain_two_ref[...] + shift_two_ref[...]).astype(BF16)
        slot_hot = slot_matrix(slot_ref[...], slot_total)
        store_blocks(buffer_refs, dot_nn(slot_hot, routed).astype(BF16))


def front(
    doc_lengths,
    tokens_in,
    slot_row,
    gain_one,
    shift_one,
    project_in,
    project_out,
    gain_two,
    shift_two,
    slot_total,
    block_shape,
):
    tok_rows, width = tokens_in.shape
    head_size = width // HEADS
    group_width = GROUP * head_size
    steps = HEADS // GROUP
    vector = whole((1, width))
    blocks = slot_total // (block_shape[0] * block_shape[1])

    def weight_spec(part):
        return pl.BlockSpec((width, group_width), lambda step: (0, part * steps + step))

    column_spec = pl.BlockSpec((tok_rows, group_width), lambda step: (0, step))
    return pl.pallas_call(
        functools.partial(front_kernel, slot_total, head_size),
        grid=(steps,),
        in_specs=[
            pl.BlockSpec(memory_space=pltpu.SMEM),
            whole((tok_rows, width)),
            whole((1, tok_rows)),
            vector,
            vector,
            weight_spec(0),
            weight_spec(1),
            weight_spec(2),
            pl.BlockSpec((group_width, width), lambda step: (step, 0)),
            vector,
            vector,
        ],
        out_specs=(
            whole((tok_rows, width)),
            column_spec,
            column_spec,
            column_spec,
            pl.BlockSpec((GROUP, tok_rows, tok_rows), lambda step: (step, 0, 0)),
            column_spec,
            whole((tok_rows, width)),
        )
        + (whole(block_shape),) * blocks,
        out_shape=(
            jax.ShapeDtypeStruct((tok_rows, width), BF16),
            jax.ShapeDtypeStruct((tok_rows, width), BF16),
            jax.ShapeDtypeStruct((tok_rows, width), BF16),
            jax.ShapeDtypeStruct((tok_rows, width), BF16),
            jax.ShapeDtypeStruct((HEADS, tok_rows, tok_rows), BF16),
            jax.ShapeDtypeStruct((tok_rows, width), BF16),
            jax.ShapeDtypeStruct((tok_rows, width), F32),
        )
        + (jax.ShapeDtypeStruct(block_shape, BF16),) * blocks,
        scratch_shapes=[pltpu.VMEM((tok_rows, tok_rows), F32)],
        cost_estimate=LIGHT,
        name="front",
    )(
        doc_lengths,
        tokens_in,
        slot_row,
        gain_one.reshape(1, width),
        shift_one.reshape(1, width),
        project_in,
        project_in,
        project_in,
        project_out,
        gain_two.reshape(1, width),
        shift_two.reshape(1, width),
    )


def spread_bits(index, layout):
    spot = 0
    for place, bit in enumerate(layout):
        spot = spot | (((index >> bit) & 1) << place)
    return spot


def store_rows(refs, first, column, values, tile, order, spot):
    keep_ref, send_ref = refs
    layout = order
    top = len(layout) - 1
    even_kept = (spot >> top) == 0
    for index in range(0, values.shape[0] // tile, 2):
        place = (spread_bits(first + index, layout) ^ spot) & ((1 << top) - 1)
        even = values[index * tile : (index + 1) * tile]
        odd = values[(index + 1) * tile : (index + 2) * tile]
        rows = pl.ds(pl.multiple_of(place * tile, tile), tile)
        keep_ref[rows, column] = jnp.where(even_kept, even, odd).astype(BF16)
        send_ref[rows, column] = jnp.where(even_kept, odd, even).astype(BF16)


def back_kernel(
    head_size,
    tile,
    orders,
    piece_count,
    spot_ref,
    slot_ref,
    hidden_ref,
    gain_two_ref,
    out_grad_ref,
    mixture_ref,
    out_weight_ref,
    query_ref,
    key_ref,
    value_ref,
    probs_ref,
    normed_ref,
    query_weight_ref,
    key_weight_ref,
    value_weight_ref,
    tokens_ref,
    gain_one_ref,
    *refs,
):
    piece_refs = refs[:piece_count]
    dense_a = refs[piece_count : piece_count + 2]
    dense_b = refs[piece_count + 2 : piece_count + 4]
    grad_in_ref, hidden_low_ref, normed_grad_ref, small_ref = refs[piece_count + 4 :]
    step = pl.program_id(0)
    width = tokens_ref.shape[1]
    group_width = query_ref.shape[1]

    @pl.when(step == 0)
    def _():
        buffer = stack_pieces(piece_refs)
        slot_hot = slot_matrix(slot_ref[...], buffer.shape[0])
        grad_routed = dot_tn(slot_hot, buffer)
        xhat, factor = norm_parts(hidden_ref[...])
        small_ref[0:1, :] = jnp.sum(grad_routed * xhat, 0, keepdims=True)
        small_ref[1:2, :] = jnp.sum(grad_routed, 0, keepdims=True)
        grad_hidden = out_grad_ref[...].astype(F32) + norm_back(
            grad_routed, gain_two_ref[...], xhat, factor
        )
        grad_in_ref[...] = grad_hidden
        hidden_low_ref[...] = grad_hidden.astype(BF16)
        normed_grad_ref[...] = jnp.zeros_like(normed_grad_ref)
        small_ref[4:, :] = jnp.zeros((LANES - 4, width), F32)

    hidden_low = hidden_low_ref[...]
    store_rows(
        dense_b,
        step * (group_width // tile),
        slice(width, 2 * width),
        dot_tn(mixture_ref[...], hidden_low),
        tile,
        orders[1],
        spot_ref[1],
    )
    grad_mixture = dot_nt(hidden_low, out_weight_ref[...]).astype(BF16)
    query, key, value = query_ref[...], key_ref[...], value_ref[...]
    lane_head = iota((1, group_width), 1) // head_size
    scale = 1.0 / math.sqrt(head_size)
    grad_query = jnp.zeros(query.shape, F32)
    grad_key = jnp.zeros(query.shape, F32)
    grad_value = jnp.zeros(query.shape, F32)
    for head in range(GROUP):
        chosen = jnp.where(lane_head == head, 1.0, 0.0).astype(BF16)
        scaled = jnp.where(lane_head == head, scale, 0.0).astype(BF16)
        grad_part = grad_mixture * chosen
        weights_low = probs_ref[head]
        weights = weights_low.astype(F32)
        grad_weights = dot_nt(value, grad_part)
        inner = jnp.sum(weights * grad_weights, 0, keepdims=True)
        grad_scores = (weights * (grad_weights - inner)).astype(BF16)
        grad_query = grad_query + dot_tn(grad_scores, key * scaled)
        grad_key = grad_key + dot_nn(grad_scores, query * scaled)
        grad_value = grad_value + dot_nn(weights_low, grad_part)
    normed = normed_ref[...]
    for part, (grad, weight_ref) in enumerate(
        (
            (grad_query, query_weight_ref),
            (grad_key, key_weight_ref),
            (grad_value, value_weight_ref),
        )
    ):
        grad = grad.astype(BF16)
        index = part // 2
        column = pl.multiple_of((part % 2) * width + step * group_width, group_width)
        store_rows(
            (dense_a, dense_b)[index],
            0,
            pl.ds(column, group_width),
            dot_tn(normed, grad),
            tile,
            orders[index],
            spot_ref[index],
        )
        normed_grad_ref[...] += dot_nt(grad, weight_ref[...])

    @pl.when(step == pl.num_programs(0) - 1)
    def _():
        grad_normed = normed_grad_ref[...]
        xhat, factor = norm_parts(tokens_ref[...].astype(F32))
        small_ref[2:3, :] = jnp.sum(grad_normed * xhat, 0, keepdims=True)
        small_ref[3:4, :] = jnp.sum(grad_normed, 0, keepdims=True)
        store_rows(
            dense_a,
            0,
            slice(2 * width, 2 * width + LANES),
            small_ref[...].T,
            tile,
            orders[0],
            spot_ref[0],
        )
        grad_in_ref[...] += norm_back(grad_normed, gain_one_ref[...], xhat, factor)


def back(
    tile,
    orders,
    spots,
    pieces,
    slot_row,
    hidden,
    gain_two,
    out_grad,
    mixture,
    project_out,
    query,
    key,
    value,
    probs,
    normed,
    project_in,
    tokens_in,
    gain_one,
):
    tok_rows, width = tokens_in.shape
    head_size = width // HEADS
    group_width = GROUP * head_size
    steps = HEADS // GROUP
    vector = whole((1, width))
    tokens_spec = whole((tok_rows, width))

    def weight_spec(part):
        return pl.BlockSpec((width, group_width), lambda step: (0, part * steps + step))

    column_spec = pl.BlockSpec((tok_rows, group_width), lambda step: (0, step))
    return pl.pallas_call(
        functools.partial(back_kernel, head_size, tile, orders, len(pieces)),
        grid=(steps,),
        in_specs=[
            pl.BlockSpec(memory_space=pltpu.SMEM),
            whole((1, tok_rows)),
            tokens_spec,
            vector,
            tokens_spec,
            column_spec,
            pl.BlockSpec((group_width, width), lambda step: (step, 0)),
            column_spec,
            column_spec,
            column_spec,
            pl.BlockSpec((GROUP, tok_rows, tok_rows), lambda step: (step, 0, 0)),
            tokens_spec,
            weight_spec(0),
            weight_spec(1),
            weight_spec(2),
            tokens_spec,
            vector,
        ]
        + piece_specs(pieces),
        out_specs=(
            whole((width // 2, 2 * width + LANES)),
            whole((width // 2, 2 * width + LANES)),
            whole((width // 2, 2 * width)),
            whole((width // 2, 2 * width)),
            tokens_spec,
        ),
        out_shape=(
            jax.ShapeDtypeStruct((width // 2, 2 * width + LANES), BF16),
            jax.ShapeDtypeStruct((width // 2, 2 * width + LANES), BF16),
            jax.ShapeDtypeStruct((width // 2, 2 * width), BF16),
            jax.ShapeDtypeStruct((width // 2, 2 * width), BF16),
            jax.ShapeDtypeStruct((tok_rows, width), F32),
        ),
        scratch_shapes=[
            pltpu.VMEM((tok_rows, width), BF16),
            pltpu.VMEM((tok_rows, width), F32),
            pltpu.VMEM((LANES, width), F32),
        ],
        cost_estimate=LIGHT,
        name="back",
    )(
        spots,
        slot_row,
        hidden,
        gain_two.reshape(1, width),
        out_grad,
        mixture,
        project_out,
        query,
        key,
        value,
        probs,
        normed,
        project_in,
        project_in,
        project_in,
        tokens_in,
        gain_one.reshape(1, width),
        *[array for array, _ in pieces],
    )


def finish_kernel(hidden_ref, slot_ref, *refs):
    buffer = stack_pieces(refs[:-1])
    slot_hot = slot_matrix(slot_ref[...], buffer.shape[0])
    refs[-1][...] = (hidden_ref[...] + dot_tn(slot_hot, buffer)).astype(BF16)


def finish(hidden, slot_row, pieces):
    return pl.pallas_call(
        finish_kernel,
        grid=(1,),
        in_specs=[whole(hidden.shape), whole(slot_row.shape)] + piece_specs(pieces),
        out_specs=whole(hidden.shape),
        out_shape=jax.ShapeDtypeStruct(hidden.shape, BF16),
        cost_estimate=LIGHT,
        name="finish",
    )(hidden, slot_row, *[array for array, _ in pieces])


def grad_act_kernel(weight_ref, *refs):
    rows_ref, out_ref = refs[-2:]

    @pl.when(pl.program_id(0) == 0)
    def _():
        rows_ref[...] = stack_pieces(refs[:-2])

    out_ref[...] = dot_nt(rows_ref[...], weight_ref[...]).astype(BF16)


def grad_act_of(weight, pieces, chunk=1024):
    hidden_units, width = weight.shape
    rows = sum(array.shape[1] for array, _ in pieces)
    return pl.pallas_call(
        grad_act_kernel,
        grid=(hidden_units // chunk,),
        in_specs=[pl.BlockSpec((chunk, width), lambda step: (step, 0))] + piece_specs(pieces),
        out_specs=(whole((rows, width)), pl.BlockSpec((rows, chunk), lambda step: (0, step))),
        out_shape=(
            jax.ShapeDtypeStruct((rows, width), BF16),
            jax.ShapeDtypeStruct((rows, hidden_units), BF16),
        ),
        cost_estimate=LIGHT,
        name="grad_act",
    )(weight, *[array for array, _ in pieces])


def result_kernel(act_a_ref, act_b_ref, weight_ref, *refs, places):
    step = pl.program_id(0)
    total_ref = refs[-1]
    half = act_a_ref.shape[0]

    @pl.when(step == 0)
    def _():
        total_ref[...] = jnp.zeros_like(total_ref)

    total_ref[:half] += dot_nn(act_a_ref[...], weight_ref[...])
    total_ref[half:] += dot_nn(act_b_ref[...], weight_ref[...])

    @pl.when(step == pl.num_programs(0) - 1)
    def _():
        store_places(refs[:-1], total_ref, places)


def store_places(refs, total_ref, places):
    for ref, firsts in zip(refs, places):
        for block, first in enumerate(firsts):
            ref[block] = total_ref[first : first + ref.shape[1]].astype(BF16)


def result_of(act_a, act_b, weight, places, block_rows, chunk=1024):
    half, hidden_units = act_a.shape
    width = weight.shape[1]
    shapes = [(len(firsts), block_rows, width) for firsts in places]
    act_spec = pl.BlockSpec((half, chunk), lambda step: (0, step))
    return pl.pallas_call(
        functools.partial(result_kernel, places=places),
        grid=(hidden_units // chunk,),
        in_specs=[act_spec, act_spec, pl.BlockSpec((chunk, width), lambda step: (step, 0))],
        out_specs=tuple(whole(shape) for shape in shapes),
        out_shape=tuple(jax.ShapeDtypeStruct(shape, BF16) for shape in shapes),
        scratch_shapes=[pltpu.VMEM((2 * half, width), F32)],
        cost_estimate=LIGHT,
        name="result",
    )(act_a, act_b, weight)


def gate_parts(pre):
    square = pre * pre
    curve = jnp.tanh(pre * (GATE_A + GATE_B * square))
    half = 0.5 * curve + 0.5
    slope = half + (0.5 * pre) * (1.0 - curve * curve) * (GATE_A + (3.0 * GATE_B) * square)
    return pre * half, slope


def expert_kernel(tile, places, piece_count, grad_act_ref, weight_ref, *refs):
    step = pl.program_id(0)
    act_ref, grad_pre_ref, rows_ref = refs[piece_count : piece_count + 3]
    out_refs, total_ref = refs[piece_count + 3 : -1], refs[-1]

    @pl.when(step == 0)
    def _():
        rows_ref[...] = stack_pieces(refs[:piece_count])
        total_ref[...] = jnp.zeros_like(total_ref)

    weight = weight_ref[...]
    for first in range(0, rows_ref.shape[0], tile):
        rows = slice(first, first + tile)
        act, slope = gate_parts(dot_nn(rows_ref[rows, :], weight))
        act_ref[rows, :] = act.astype(BF16)
        grad_pre = (grad_act_ref[rows, :].astype(F32) * slope).astype(BF16)
        grad_pre_ref[rows, :] = grad_pre
        total_ref[rows, :] += dot_nt(grad_pre, weight)

    @pl.when(step == pl.num_programs(0) - 1)
    def _():
        store_places(out_refs, total_ref, places)


def expert(half, grad_act, weight, pieces, places, block_rows, chunk=1024, tile=256):
    width, hidden_units = weight.shape
    rows = grad_act.shape[0] // 2
    column_spec = pl.BlockSpec((rows, chunk), lambda step: (0, step))
    shapes = [(len(firsts), block_rows, width) for firsts in places]
    return pl.pallas_call(
        functools.partial(expert_kernel, tile, places, len(pieces)),
        grid=(hidden_units // chunk,),
        in_specs=[
            pl.BlockSpec((rows, chunk), lambda step: (half, step)),
            pl.BlockSpec((width, chunk), lambda step: (0, step)),
        ]
        + piece_specs(pieces),
        out_specs=(column_spec, column_spec, whole((rows, width)))
        + tuple(whole(shape) for shape in shapes),
        out_shape=(
            jax.ShapeDtypeStruct((rows, hidden_units), BF16),
            jax.ShapeDtypeStruct((rows, hidden_units), BF16),
            jax.ShapeDtypeStruct((rows, width), BF16),
        )
        + tuple(jax.ShapeDtypeStruct(shape, BF16) for shape in shapes),
        scratch_shapes=[pltpu.VMEM((rows, width), F32)],
        cost_estimate=LIGHT,
        name="expert",
    )(grad_act, weight, *[array for array, _ in pieces])


def first_grad_kernel(flip_ref, rows_a_ref, rows_b_ref, grad_a_ref, grad_b_ref, *refs):
    step = pl.program_id(0)
    half_steps = pl.num_programs(0) // 2
    product_ref = refs[-1]
    product = dot_tn(rows_a_ref[...], grad_a_ref[...]) + dot_tn(rows_b_ref[...], grad_b_ref[...])
    product_ref[...] = product.astype(BF16)
    owned = product_ref.shape[0] // 4

    def piece(place):
        row = pl.multiple_of((place ^ flip_ref[0]) * owned, owned)
        return product_ref[pl.ds(row, owned), :]

    keep_a, send_a, keep_b, send_b = refs[:-1]

    @pl.when(step < half_steps)
    def _():
        for index, (kept, sent) in enumerate(((0, 1), (2, 3))):
            keep_a[index] = piece(kept)
            send_a[index] = piece(sent)

    @pl.when(step >= half_steps)
    def _():
        for index, (kept, sent) in enumerate(((0, 2), (1, 3))):
            keep_b[index] = piece(kept)
            send_b[index] = piece(sent)


def first_grad(flip, rows_a, rows_b, grad_a, grad_b, chunk=1024):
    rows, width = rows_a.shape
    columns = grad_a.shape[1]
    steps = columns // chunk
    shape = jax.ShapeDtypeStruct((2, width // 4, columns // 2), BF16)
    block = (2, width // 4, chunk)
    spec_a = pl.BlockSpec(block, lambda step: (0, 0, jnp.minimum(step, steps // 2 - 1)))
    spec_b = pl.BlockSpec(block, lambda step: (0, 0, jnp.maximum(step - steps // 2, 0)))
    return pl.pallas_call(
        first_grad_kernel,
        grid=(steps,),
        in_specs=[
            pl.BlockSpec(memory_space=pltpu.SMEM),
            whole((rows, width)),
            whole((rows, width)),
            pl.BlockSpec((rows, chunk), lambda step: (0, step)),
            pl.BlockSpec((rows, chunk), lambda step: (0, step)),
        ],
        out_specs=(spec_a, spec_a, spec_b, spec_b),
        out_shape=(shape,) * 4,
        scratch_shapes=[pltpu.VMEM((width, chunk), BF16)],
        cost_estimate=LIGHT,
        name="first_grad",
    )(flip, rows_a, rows_b, grad_a, grad_b)


def second_grad_kernel(
    flip_ref, act_a_ref, act_b_ref, grad_ref, keep_a, send_a, keep_b, send_b
):
    step = pl.program_id(0)
    rows = act_a_ref.shape[0]
    product = dot_tn(act_a_ref[...], grad_ref[:rows]) + dot_tn(act_b_ref[...], grad_ref[rows:])
    product = product.astype(BF16)
    half = product.shape[1] // 2

    @pl.when(step == 0)
    def _():
        send_a[0] = product[:, :half]
        send_b[0] = product[:, half:]

    @pl.when(step == 1)
    def _():
        send_a[0] = product[:, :half]
        keep_b[0] = product[:, half:]

    @pl.when(step == 2)
    def _():
        keep_a[0] = product[:, :half]
        send_b[0] = product[:, half:]

    @pl.when(step == 3)
    def _():
        keep_a[0] = product[:, :half]
        keep_b[0] = product[:, half:]


def second_grad(flip, act_a, act_b, grad):
    rows, width = grad.shape
    owned = act_a.shape[1] // 4
    act_spec = pl.BlockSpec(
        (rows // 2, owned), lambda step, flip_ref: (0, place_of(step) ^ flip_ref[0])
    )
    shape = jax.ShapeDtypeStruct((2, owned, width // 2), BF16)
    block = (1, owned, width // 2)

    def spec(first_step):
        return pl.BlockSpec(
            block, lambda step, flip_ref: (1 - (step >= first_step).astype(jnp.int32), 0, 0)
        )

    return pl.pallas_call(
        second_grad_kernel,
        grid_spec=pltpu.PrefetchScalarGridSpec(
            num_scalar_prefetch=1,
            grid=(4,),
            in_specs=[
                act_spec,
                act_spec,
                pl.BlockSpec((rows, width), lambda step, flip_ref: (0, 0)),
            ],
            out_specs=(spec(3), spec(1), spec(3), spec(2)),
        ),
        out_shape=(shape,) * 4,
        cost_estimate=LIGHT,
        name="second_grad",
    )(flip, act_a, act_b, grad)


def place_of(step):
    return jnp.where(step == 0, 3, jnp.where(step == 3, 0, step))


def swap(values, axis, bits):
    size = lax.axis_size(axis)
    return lax.ppermute(values, axis, [(index, index ^ bits) for index in range(size)])


def swap_copies(parts):
    return swap(parts[1], "rep", 1), swap(parts[3], "rep", 2)


def half_sum_kernel(keep_a, got_a, keep_b, got_b, out_a, out_b):
    out_a[...] = add_low(keep_a[...], got_a[...])
    out_b[...] = add_low(keep_b[...], got_b[...])


def half_sums(parts, got, chunks=2):
    _, rows, width = got[0].shape
    block = (None, rows // chunks, width)
    out_spec = pl.BlockSpec(block[1:], lambda step: (step, 0))
    return pl.pallas_call(
        half_sum_kernel,
        grid=(chunks,),
        in_specs=[pl.BlockSpec(block, lambda step: (1, step, 0))] * 4,
        out_specs=(out_spec,) * 2,
        out_shape=(jax.ShapeDtypeStruct((rows, width), BF16),) * 2,
        cost_estimate=LIGHT,
        name="half_sum",
    )(parts[0], got[0], parts[2], got[1])


def copy_sum_kernel(*refs):
    out_ref = refs[-1]
    half = out_ref.shape[1] // 2
    for index, columns in ((0, slice(0, half)), (3, slice(half, 2 * half))):
        keep, got, more = [ref[...].astype(F32) for ref in refs[index : index + 3]]
        out_ref[:, columns] = keep + got + more


def copy_sum(parts, got, more):
    keep_a, _, keep_b, _ = parts
    chunks = 4
    _, rows, width = keep_a.shape
    first = pl.BlockSpec((None, rows // chunks, width), lambda step: (0, step, 0))
    plain = pl.BlockSpec((rows // chunks, width), lambda step: (step, 0))
    return pl.pallas_call(
        copy_sum_kernel,
        grid=(chunks,),
        in_specs=[first, first, plain] * 2,
        out_specs=pl.BlockSpec((rows // chunks, 2 * width), lambda step: (step, 0)),
        out_shape=jax.ShapeDtypeStruct((rows, 2 * width), F32),
        cost_estimate=LIGHT,
        name="copy_sum",
    )(keep_a, got[0], more[0], keep_b, got[1], more[1])


def split_sum_kernel(keep_low, keep_high, got_low, got_high, low_ref, high_ref):
    low_ref[...] = add_low(keep_low[...], got_low[...])
    high_ref[...] = add_low(keep_high[...], got_high[...])


def split_sum(keep, got):
    half, width = keep.shape[0] // 2, keep.shape[1]
    if half < 128:
        total = add_low(keep, got)
        return total[:half], total[half:]
    chunks = 2 if half % 128 == 0 else 1
    block = (half // chunks, width)
    low = pl.BlockSpec(block, lambda step: (step, 0))
    high = pl.BlockSpec(block, lambda step: (step + chunks, 0))
    return pl.pallas_call(
        split_sum_kernel,
        grid=(chunks,),
        in_specs=[low, high, low, high],
        out_specs=(low, low),
        out_shape=(jax.ShapeDtypeStruct((half, width), BF16),) * 2,
        cost_estimate=LIGHT,
        name="split_sum",
    )(keep, keep, got, got)


def swap_halves(dense, steps):
    return [swap(send, axis, 1 << bit) for (_, send), (axis, bit) in zip(dense, steps)]


def swap_sums(sums):
    return swap(sums[0], "rep", 2), swap(sums[1], "rep", 1)


def add_low(left, right):
    return (left.astype(F32) + right.astype(F32)).astype(BF16)


def spread(blocks):
    return {bits: swap(block, "ep", bits) if bits else block for bits, block in blocks.items()}


def gather_kernel(*refs):
    for index, ref in enumerate(refs[:-1]):
        refs[-1][index] = ref[...]


def cross(blocks, members):
    return swap(jnp.concatenate([blocks[bits][1:] for bits in members], 0), "ep", 1)


def cross_late(blocks, members):
    pieces = [(blocks[bits], 1) for bits in members]
    shape = (len(pieces),) + blocks[members[0]].shape[1:]
    gathered = pl.pallas_call(
        gather_kernel,
        grid=(1,),
        in_specs=piece_specs(pieces),
        out_specs=whole(shape),
        out_shape=jax.ShapeDtypeStruct(shape, BF16),
        cost_estimate=LIGHT,
        name="gather_sum",
    )(*[array for array, _ in pieces])
    return swap(gathered, "ep", 1)


def paired_pieces(blocks, members, cross):
    crossed = cross(blocks, members)
    pieces = [((blocks[bits], 0), (crossed, place)) for place, bits in enumerate(members)]
    return [piece for pair in pieces for piece in pair]


def exchange(buffer):
    return lax.all_to_all(buffer, "ep", split_axis=0, concat_axis=0, tiled=True)


def local(
    tokens_in,
    token_ids,
    hash_table,
    doc_lengths,
    gain_one,
    shift_one,
    project_in,
    project_out,
    gain_two,
    shift_two,
    expert_in,
    expert_out,
    out_grad,
):
    tok_rows, width = tokens_in.shape
    rep_size, ep_size = lax.axis_size("rep"), lax.axis_size("ep")
    rep_bits, ep_bits = rep_size.bit_length() - 1, ep_size.bit_length() - 1
    expert_count = expert_in.shape[0] * ep_size
    capacity = 2 * tok_rows // expert_count
    slot_total = expert_count * capacity
    tile = width // (rep_size * ep_size)
    paired = expert_count <= 8
    first_weight, second_weight = expert_in[0], expert_out[0]
    rep_index, ep_index = lax.axis_index("rep"), lax.axis_index("ep")
    ep_flip = jnp.reshape(ep_index if paired else 0, (1,)).astype(jnp.int32)
    rep_flip = jnp.reshape(rep_index, (1,)).astype(jnp.int32)
    ep_steps = [("ep", bit) for bit in range(1, ep_bits)]
    rep_steps = [("rep", bit) for bit in range(rep_bits)]
    steps_a, steps_b = ep_steps + rep_steps, ep_steps[::-1] + rep_steps[::-1]
    orders, spots = [], []
    for steps in (steps_a, steps_b):
        places = [bit + (ep_bits if axis == "rep" else 0) for axis, bit in reversed(steps)] + [0]
        orders.append(tuple(places))
        spots.append(spread_bits(rep_index * ep_size + ep_index, places))
    spots = jnp.stack(spots).astype(jnp.int32)

    fronts = (
        doc_lengths,
        tokens_in,
        gain_one,
        shift_one,
        project_in,
        project_out,
        gain_two,
        shift_two,
    )
    half_rows = slot_total // 2
    if paired:
        members = tuple(range(0, expert_count, 2))
        order = members[::2] + members[1::2]
        halves = (members[::2], members[1::2])
        block_rows, block_shape = capacity, (2, capacity, width)
    else:
        block_rows, block_shape = half_rows, (expert_count, capacity, width)
    slot_row, *buffers = route(
        ep_flip, token_ids, hash_table, out_grad, expert_count, capacity, block_shape
    )
    grads = spread(dict(zip(members, buffers))) if paired else exchange(buffers[0])
    normed, query, key, value, probs, mixture, hidden, *buffers = front(
        *fronts[:2], slot_row, *fronts[2:], slot_total, block_shape
    )
    if paired:
        blocks, hidden = lax.optimization_barrier(([grads[bits] for bits in members], hidden))
        grads = dict(zip(members, blocks))
        crossed = cross(grads, order)
        grad_pieces = []
        for index, half in enumerate(halves):
            grad_pieces += [(grads[bits], 0) for bits in half]
            grad_pieces += [(crossed, index * len(half) + place) for place in range(len(half))]
    else:
        grads = grads.reshape(2, half_rows, width)
        grad_pieces = [(grads, 0), (grads, 1)]
    grad_rows, grad_act = grad_act_of(second_weight, grad_pieces)
    outs = []
    if paired:
        received = spread(dict(zip(members, buffers)))
        count = len(halves[0])
        places = [[place * capacity, (count + place) * capacity] for place in range(count)]
        sent = {}
        done = grad_rows
        for index, half in ((1, halves[1]), (0, halves[0])):
            blocks, done = lax.optimization_barrier(([received[bits] for bits in half], done))
            received.update(zip(half, blocks))
            if index:
                grad_rows = done
            else:
                outs[0][2] = done
            crossed = cross(received, half)
            pieces = [(received[bits], 0) for bits in half]
            pieces += [(crossed, place) for place in range(count)]
            *out, = expert(index, grad_act, first_weight, pieces, places, capacity)
            outs.append(out[:3])
            done = out[2]
            sent.update(spread(dict(zip(half, out[3:]))))
        places += [[first + half_rows for first in firsts] for firsts in places]
    else:
        received = exchange(buffers[0]).reshape(2, half_rows, width)
        places = [[0]]
        for index in range(2):
            *out, = expert(index, grad_act, first_weight, [(received, index)], places, half_rows)
            outs.append(out)
        sent = jnp.concatenate([outs[0][3], outs[1][3]], 0).reshape(buffers[0].shape)
        back_pieces = [(exchange(sent).reshape(1, slot_total, width), 0)]
        places = [[0, half_rows]]
    if paired:
        outs = outs[::-1]
    (act_a, grad_pre_a, rows_a), (act_b, grad_pre_b, rows_b) = outs[0][:3], outs[1][:3]
    second_parts = second_grad(rep_flip, act_a, act_b, grad_rows)
    act_a, second_parts = lax.optimization_barrier((act_a, second_parts))
    results = result_of(act_a, act_b, second_weight, places, block_rows)
    got_second = swap_copies(second_parts)
    if paired:
        blocks, results = lax.optimization_barrier(([sent[bits] for bits in members], results))
        back_pieces = paired_pieces(dict(zip(members, blocks)), members, cross)
    returned = spread(dict(zip(order, results))) if paired else exchange(
        results[0].reshape(expert_count, capacity, width)
    )
    keep_a, send_a, keep_b, send_b, grad_in = back(
        tile,
        orders,
        spots,
        back_pieces,
        slot_row,
        hidden,
        gain_two,
        out_grad,
        mixture,
        project_out,
        query,
        key,
        value,
        probs,
        normed,
        project_in,
        tokens_in,
        gain_one,
    )
    sends = (send_a, send_b)
    sends, got_second, returned = lax.optimization_barrier((sends, got_second, returned))
    got_a, got_b = swap(sends[0], "ep", 1), swap(sends[1], "ep", 1)
    sums_second = half_sums(second_parts, got_second)
    rows_a, sums_second = lax.optimization_barrier((rows_a, sums_second))
    more_second = swap_sums(sums_second)
    first_parts = first_grad(rep_flip, rows_a, rows_b, grad_pre_a, grad_pre_b)
    got_a, got_b, first_parts = lax.optimization_barrier((got_a, got_b, first_parts))
    dense = [split_sum(keep_a, got_a), split_sum(keep_b, got_b)]
    dense, first_parts, more_second = lax.optimization_barrier((dense, first_parts, more_second))
    got_first = swap_copies(first_parts)
    summed_second = copy_sum(second_parts, got_second, more_second)
    if paired:
        pieces = paired_pieces(returned, members, cross_late)
    else:
        pieces = [(returned.reshape(1, slot_total, width), 0)]
    block_out = finish(hidden, slot_row, pieces)
    for index, pair in enumerate(zip(steps_a, steps_b)):
        got = swap_halves(dense, pair)
        if index == 0:
            got_first, summed_second, block_out = lax.optimization_barrier(
                (got_first, summed_second, block_out)
            )
            sums_first, got = lax.optimization_barrier((half_sums(first_parts, got_first), got))
            more_first = swap_sums(sums_first)
        if index == 1:
            got, more_first = lax.optimization_barrier((got, more_first))
            summed_first = copy_sum(first_parts, got_first, more_first)
        if index == 2:
            got, summed_first = lax.optimization_barrier((got, summed_first))
        if index < len(steps_a) - 1:
            dense = [split_sum(keep, more) for (keep, _), more in zip(dense, got)]
    dense_a, dense_b = [keep.astype(F32) + more.astype(F32) for (keep, _), more in zip(dense, got)]
    return (
        block_out,
        grad_in,
        jnp.concatenate([dense_a[:, : 2 * width], dense_b[:, :width]], 1),
        dense_b[:, width:],
        dense_a[:, 2 * width + 2],
        dense_a[:, 2 * width + 3],
        dense_a[:, 2 * width],
        dense_a[:, 2 * width + 1],
        summed_first[None],
        summed_second[None],
    )


def solution(mesh):
    in_specs = (
        P(("rep", "ep"), None),
        P(("rep", "ep")),
        P(),
        P(("rep", "ep"), None),
        P(),
        P(),
        P(),
        P(),
        P(),
        P(),
        P("ep", None, None),
        P("ep", None, None),
        P(("rep", "ep"), None),
    )
    out_specs = (
        P(("rep", "ep"), None),
        P(("rep", "ep"), None),
        P(("rep", "ep"), None),
        P(("rep", "ep"), None),
        P(("rep", "ep")),
        P(("rep", "ep")),
        P(("rep", "ep")),
        P(("rep", "ep")),
        P("ep", "rep", None),
        P("ep", "rep", None),
    )
    return jax.shard_map(local, mesh=mesh, in_specs=in_specs, out_specs=out_specs, check_vma=False)
```

```python
import functools
import math

import jax
import jax.numpy as jnp
from jax import lax
from jax.experimental import pallas as pl
from jax.experimental.pallas import tpu as pltpu
from jax.sharding import PartitionSpec as P

HEADS = 16
GROUP = 4
LANES = 128
NEG_LARGE = -1e30
EPSILON = 1e-05
BF16 = jnp.bfloat16
F32 = jnp.float32
GATE_A = math.sqrt(2.0 / math.pi)
GATE_B = GATE_A * 0.044715
HEAVY = pl.CostEstimate(flops=10000000000, bytes_accessed=1 << 16, transcendentals=0)
LIGHT = pl.CostEstimate(flops=1 << 20, bytes_accessed=1 << 16, transcendentals=0)


def dot_nn(a, b):
    return lax.dot_general(a, b, (((1,), (0,)), ((), ())), preferred_element_type=F32)


def dot_nt(a, b):
    return lax.dot_general(a, b, (((1,), (1,)), ((), ())), preferred_element_type=F32)


def dot_tn(a, b):
    return lax.dot_general(a, b, (((0,), (0,)), ((), ())), preferred_element_type=F32)


def iota(shape, axis):
    return lax.broadcasted_iota(jnp.int32, shape, axis)


def whole(shape):
    return pl.BlockSpec(shape, lambda *_: (0,) * len(shape))


def piece_specs(pieces):
    def spec(array, block):
        return pl.BlockSpec((None,) + array.shape[1:], lambda *_: (block, 0, 0))

    return [spec(array, block) for array, block in pieces]


def stack_pieces(refs):
    return jnp.concatenate([ref[...] for ref in refs], 0)


def store_blocks(refs, values):
    first = 0
    for ref in refs:
        for block in range(ref.shape[0]):
            ref[block] = values[first : first + ref.shape[1]]
            first += ref.shape[1]


def norm_parts(values):
    center = jnp.mean(values, -1, keepdims=True)
    centered = values - center
    spread = jnp.mean(centered * centered, -1, keepdims=True)
    factor = lax.rsqrt(spread + EPSILON)
    return centered * factor, factor


def norm_back(grad, gain, xhat, factor):
    scaled = grad * gain
    mean_scaled = jnp.mean(scaled, -1, keepdims=True)
    mean_cross = jnp.mean(scaled * xhat, -1, keepdims=True)
    return factor * (scaled - mean_scaled - xhat * mean_cross)


def slot_matrix(slot_row, slot_total):
    tok_rows = slot_row.shape[1]
    return (iota((slot_total, tok_rows), 0) == slot_row).astype(F32).astype(BF16)


def route_kernel(
    expert_count, capacity, flip_ref, ids_ref, table_ref, grad_ref, slot_ref, *buffer_refs
):
    tok_rows = ids_ref.shape[1]
    ids = ids_ref[...]
    table_rows = table_ref.shape[0]
    high = ids // LANES
    low = ids - high * LANES
    high_hot = (iota((table_rows, tok_rows), 0) == high).astype(F32).astype(BF16)
    picked = dot_tn(table_ref[...].astype(F32).astype(BF16), high_hot)
    low_hot = iota((LANES, tok_rows), 0) == low
    expert = jnp.sum(jnp.where(low_hot, picked, 0.0), 0, keepdims=True).astype(jnp.int32)
    expert_hot = (iota((expert_count, tok_rows), 0) == expert).astype(F32)
    before = (iota((tok_rows, tok_rows), 0) < iota((tok_rows, tok_rows), 1)).astype(F32)
    earlier = dot_nn(expert_hot.astype(BF16), before.astype(BF16))
    rank = jnp.sum(earlier * expert_hot, 0, keepdims=True).astype(jnp.int32)
    slot = (expert ^ flip_ref[0]) * capacity + rank
    slot_ref[...] = slot
    slot_hot = slot_matrix(slot, expert_count * capacity)
    store_blocks(buffer_refs, dot_nn(slot_hot, grad_ref[...]).astype(BF16))


def route(flip, token_ids, hash_table, out_grad, expert_count, capacity, block_shape):
    tok_rows, width = out_grad.shape
    slot_total = expert_count * capacity
    table_rows = hash_table.shape[0] // LANES
    blocks = slot_total // (block_shape[0] * block_shape[1])
    return pl.pallas_call(
        functools.partial(route_kernel, expert_count, capacity),
        in_specs=[
            pl.BlockSpec(memory_space=pltpu.SMEM),
            whole((1, tok_rows)),
            whole((table_rows, LANES)),
            whole((tok_rows, width)),
        ],
        out_specs=(whole((1, tok_rows)),) + (whole(block_shape),) * blocks,
        out_shape=(jax.ShapeDtypeStruct((1, tok_rows), jnp.int32),)
        + (jax.ShapeDtypeStruct(block_shape, BF16),) * blocks,
        cost_estimate=LIGHT,
        name="route",
    )(flip, token_ids.reshape(1, tok_rows), hash_table.reshape(table_rows, LANES), out_grad)


def front_kernel(
    slot_total,
    head_size,
    lengths_ref,
    tokens_ref,
    slot_ref,
    gain_one_ref,
    shift_one_ref,
    query_weight_ref,
    key_weight_ref,
    value_weight_ref,
    out_weight_ref,
    gain_two_ref,
    shift_two_ref,
    normed_ref,
    query_ref,
    key_ref,
    value_ref,
    probs_ref,
    mixture_ref,
    hidden_ref,
    *refs,
):
    buffer_refs, mask_ref = refs[:-1], refs[-1]
    step = pl.program_id(0)
    tok_rows = tokens_ref.shape[0]
    group_width = query_ref.shape[1]

    @pl.when(step == 0)
    def _():
        inputs = tokens_ref[...].astype(F32)
        xhat, _ = norm_parts(inputs)
        normed_ref[...] = (xhat * gain_one_ref[...] + shift_one_ref[...]).astype(BF16)
        position = iota((1, tok_rows), 1)
        start = jnp.zeros((1, tok_rows), jnp.int32)
        bound = jnp.int32(0)
        for index in range(lengths_ref.shape[1]):
            bound = bound + lengths_ref[0, index]
            start = jnp.where(position >= bound, bound, start)
        key_position = iota((tok_rows, tok_rows), 0)
        allowed = jnp.logical_and(key_position >= start, key_position <= position)
        mask_ref[...] = jnp.where(allowed, 0.0, NEG_LARGE)
        hidden_ref[...] = inputs

    normed = normed_ref[...]
    query = dot_nn(normed, query_weight_ref[...]).astype(BF16)
    key = dot_nn(normed, key_weight_ref[...]).astype(BF16)
    value = dot_nn(normed, value_weight_ref[...]).astype(BF16)
    query_ref[...] = query
    key_ref[...] = key
    value_ref[...] = value
    lane_head = iota((1, group_width), 1) // head_size
    scale = 1.0 / math.sqrt(head_size)
    total = jnp.zeros((tok_rows, group_width), F32)
    for head in range(GROUP):
        chosen = lane_head == head
        key_part = key * jnp.where(chosen, scale, 0.0).astype(BF16)
        value_part = value * jnp.where(chosen, 1.0, 0.0).astype(BF16)
        scores = dot_nt(key_part, query) + mask_ref[...]
        exponent = jnp.exp(scores - jnp.max(scores, 0, keepdims=True))
        inverse = 1.0 / jnp.sum(exponent, 0, keepdims=True)
        weights = (exponent * inverse).astype(BF16)
        probs_ref[head] = weights
        total = total + dot_tn(weights, value_part)
    mixture = total.astype(BF16)
    mixture_ref[...] = mixture
    hidden_ref[...] += dot_nn(mixture, out_weight_ref[...])

    @pl.when(step == pl.num_programs(0) - 1)
    def _():
        xhat, _ = norm_parts(hidden_ref[...])
        routed = (xhat * gain_two_ref[...] + shift_two_ref[...]).astype(BF16)
        slot_hot = slot_matrix(slot_ref[...], slot_total)
        store_blocks(buffer_refs, dot_nn(slot_hot, routed).astype(BF16))


def front(
    doc_lengths,
    tokens_in,
    slot_row,
    gain_one,
    shift_one,
    project_in,
    project_out,
    gain_two,
    shift_two,
    slot_total,
    block_shape,
):
    tok_rows, width = tokens_in.shape
    head_size = width // HEADS
    group_width = GROUP * head_size
    steps = HEADS // GROUP
    vector = whole((1, width))
    blocks = slot_total // (block_shape[0] * block_shape[1])

    def weight_spec(part):
        return pl.BlockSpec((width, group_width), lambda step: (0, part * steps + step))

    column_spec = pl.BlockSpec((tok_rows, group_width), lambda step: (0, step))
    return pl.pallas_call(
        functools.partial(front_kernel, slot_total, head_size),
        grid=(steps,),
        in_specs=[
            pl.BlockSpec(memory_space=pltpu.SMEM),
            whole((tok_rows, width)),
            whole((1, tok_rows)),
            vector,
            vector,
            weight_spec(0),
            weight_spec(1),
            weight_spec(2),
            pl.BlockSpec((group_width, width), lambda step: (step, 0)),
            vector,
            vector,
        ],
        out_specs=(
            whole((tok_rows, width)),
            column_spec,
            column_spec,
            column_spec,
            pl.BlockSpec((GROUP, tok_rows, tok_rows), lambda step: (step, 0, 0)),
            column_spec,
            whole((tok_rows, width)),
        )
        + (whole(block_shape),) * blocks,
        out_shape=(
            jax.ShapeDtypeStruct((tok_rows, width), BF16),
            jax.ShapeDtypeStruct((tok_rows, width), BF16),
            jax.ShapeDtypeStruct((tok_rows, width), BF16),
            jax.ShapeDtypeStruct((tok_rows, width), BF16),
            jax.ShapeDtypeStruct((HEADS, tok_rows, tok_rows), BF16),
            jax.ShapeDtypeStruct((tok_rows, width), BF16),
            jax.ShapeDtypeStruct((tok_rows, width), F32),
        )
        + (jax.ShapeDtypeStruct(block_shape, BF16),) * blocks,
        scratch_shapes=[pltpu.VMEM((tok_rows, tok_rows), F32)],
        cost_estimate=LIGHT,
        name="front",
    )(
        doc_lengths,
        tokens_in,
        slot_row,
        gain_one.reshape(1, width),
        shift_one.reshape(1, width),
        project_in,
        project_in,
        project_in,
        project_out,
        gain_two.reshape(1, width),
        shift_two.reshape(1, width),
    )


def spread_bits(index, layout):
    spot = 0
    for place, bit in enumerate(layout):
        spot = spot | (((index >> bit) & 1) << place)
    return spot


def store_rows(refs, first, column, values, tile, order, spot):
    keep_ref, send_ref = refs
    layout = order
    top = len(layout) - 1
    even_kept = (spot >> top) == 0
    for index in range(0, values.shape[0] // tile, 2):
        place = (spread_bits(first + index, layout) ^ spot) & ((1 << top) - 1)
        even = values[index * tile : (index + 1) * tile]
        odd = values[(index + 1) * tile : (index + 2) * tile]
        rows = pl.ds(pl.multiple_of(place * tile, tile), tile)
        keep_ref[rows, column] = jnp.where(even_kept, even, odd).astype(BF16)
        send_ref[rows, column] = jnp.where(even_kept, odd, even).astype(BF16)


def back_kernel(
    head_size,
    tile,
    orders,
    piece_count,
    spot_ref,
    slot_ref,
    hidden_ref,
    gain_two_ref,
    out_grad_ref,
    mixture_ref,
    out_weight_ref,
    query_ref,
    key_ref,
    value_ref,
    probs_ref,
    normed_ref,
    query_weight_ref,
    key_weight_ref,
    value_weight_ref,
    tokens_ref,
    gain_one_ref,
    *refs,
):
    piece_refs = refs[:piece_count]
    dense_a = refs[piece_count : piece_count + 2]
    dense_b = refs[piece_count + 2 : piece_count + 4]
    grad_in_ref, hidden_low_ref, normed_grad_ref, small_ref = refs[piece_count + 4 :]
    step = pl.program_id(0)
    width = tokens_ref.shape[1]
    group_width = query_ref.shape[1]

    @pl.when(step == 0)
    def _():
        buffer = stack_pieces(piece_refs)
        slot_hot = slot_matrix(slot_ref[...], buffer.shape[0])
        grad_routed = dot_tn(slot_hot, buffer)
        xhat, factor = norm_parts(hidden_ref[...])
        small_ref[0:1, :] = jnp.sum(grad_routed * xhat, 0, keepdims=True)
        small_ref[1:2, :] = jnp.sum(grad_routed, 0, keepdims=True)
        grad_hidden = out_grad_ref[...].astype(F32) + norm_back(
            grad_routed, gain_two_ref[...], xhat, factor
        )
        grad_in_ref[...] = grad_hidden
        hidden_low_ref[...] = grad_hidden.astype(BF16)
        normed_grad_ref[...] = jnp.zeros_like(normed_grad_ref)
        small_ref[4:, :] = jnp.zeros((LANES - 4, width), F32)

    hidden_low = hidden_low_ref[...]
    store_rows(
        dense_b,
        step * (group_width // tile),
        slice(width, 2 * width),
        dot_tn(mixture_ref[...], hidden_low),
        tile,
        orders[1],
        spot_ref[1],
    )
    grad_mixture = dot_nt(hidden_low, out_weight_ref[...]).astype(BF16)
    query, key, value = query_ref[...], key_ref[...], value_ref[...]
    lane_head = iota((1, group_width), 1) // head_size
    scale = 1.0 / math.sqrt(head_size)
    grad_query = jnp.zeros(query.shape, F32)
    grad_key = jnp.zeros(query.shape, F32)
    grad_value = jnp.zeros(query.shape, F32)
    for head in range(GROUP):
        chosen = jnp.where(lane_head == head, 1.0, 0.0).astype(BF16)
        scaled = jnp.where(lane_head == head, scale, 0.0).astype(BF16)
        grad_part = grad_mixture * chosen
        weights_low = probs_ref[head]
        weights = weights_low.astype(F32)
        grad_weights = dot_nt(value, grad_part)
        inner = jnp.sum(weights * grad_weights, 0, keepdims=True)
        grad_scores = (weights * (grad_weights - inner)).astype(BF16)
        grad_query = grad_query + dot_tn(grad_scores, key * scaled)
        grad_key = grad_key + dot_nn(grad_scores, query * scaled)
        grad_value = grad_value + dot_nn(weights_low, grad_part)
    normed = normed_ref[...]
    for part, (grad, weight_ref) in enumerate(
        (
            (grad_query, query_weight_ref),
            (grad_key, key_weight_ref),
            (grad_value, value_weight_ref),
        )
    ):
        grad = grad.astype(BF16)
        index = part // 2
        column = pl.multiple_of((part % 2) * width + step * group_width, group_width)
        store_rows(
            (dense_a, dense_b)[index],
            0,
            pl.ds(column, group_width),
            dot_tn(normed, grad),
            tile,
            orders[index],
            spot_ref[index],
        )
        normed_grad_ref[...] += dot_nt(grad, weight_ref[...])

    @pl.when(step == pl.num_programs(0) - 1)
    def _():
        grad_normed = normed_grad_ref[...]
        xhat, factor = norm_parts(tokens_ref[...].astype(F32))
        small_ref[2:3, :] = jnp.sum(grad_normed * xhat, 0, keepdims=True)
        small_ref[3:4, :] = jnp.sum(grad_normed, 0, keepdims=True)
        store_rows(
            dense_a,
            0,
            slice(2 * width, 2 * width + LANES),
            small_ref[...].T,
            tile,
            orders[0],
            spot_ref[0],
        )
        grad_in_ref[...] += norm_back(grad_normed, gain_one_ref[...], xhat, factor)


def back(
    tile,
    orders,
    spots,
    pieces,
    slot_row,
    hidden,
    gain_two,
    out_grad,
    mixture,
    project_out,
    query,
    key,
    value,
    probs,
    normed,
    project_in,
    tokens_in,
    gain_one,
):
    tok_rows, width = tokens_in.shape
    head_size = width // HEADS
    group_width = GROUP * head_size
    steps = HEADS // GROUP
    vector = whole((1, width))
    tokens_spec = whole((tok_rows, width))

    def weight_spec(part):
        return pl.BlockSpec((width, group_width), lambda step: (0, part * steps + step))

    column_spec = pl.BlockSpec((tok_rows, group_width), lambda step: (0, step))
    return pl.pallas_call(
        functools.partial(back_kernel, head_size, tile, orders, len(pieces)),
        grid=(steps,),
        in_specs=[
            pl.BlockSpec(memory_space=pltpu.SMEM),
            whole((1, tok_rows)),
            tokens_spec,
            vector,
            tokens_spec,
            column_spec,
            pl.BlockSpec((group_width, width), lambda step: (step, 0)),
            column_spec,
            column_spec,
            column_spec,
            pl.BlockSpec((GROUP, tok_rows, tok_rows), lambda step: (step, 0, 0)),
            tokens_spec,
            weight_spec(0),
            weight_spec(1),
            weight_spec(2),
            tokens_spec,
            vector,
        ]
        + piece_specs(pieces),
        out_specs=(
            whole((width // 2, 2 * width + LANES)),
            whole((width // 2, 2 * width + LANES)),
            whole((width // 2, 2 * width)),
            whole((width // 2, 2 * width)),
            tokens_spec,
        ),
        out_shape=(
            jax.ShapeDtypeStruct((width // 2, 2 * width + LANES), BF16),
            jax.ShapeDtypeStruct((width // 2, 2 * width + LANES), BF16),
            jax.ShapeDtypeStruct((width // 2, 2 * width), BF16),
            jax.ShapeDtypeStruct((width // 2, 2 * width), BF16),
            jax.ShapeDtypeStruct((tok_rows, width), F32),
        ),
        scratch_shapes=[
            pltpu.VMEM((tok_rows, width), BF16),
            pltpu.VMEM((tok_rows, width), F32),
            pltpu.VMEM((LANES, width), F32),
        ],
        cost_estimate=LIGHT,
        name="back",
    )(
        spots,
        slot_row,
        hidden,
        gain_two.reshape(1, width),
        out_grad,
        mixture,
        project_out,
        query,
        key,
        value,
        probs,
        normed,
        project_in,
        project_in,
        project_in,
        tokens_in,
        gain_one.reshape(1, width),
        *[array for array, _ in pieces],
    )


def finish_kernel(hidden_ref, slot_ref, *refs):
    buffer = stack_pieces(refs[:-1])
    slot_hot = slot_matrix(slot_ref[...], buffer.shape[0])
    refs[-1][...] = (hidden_ref[...] + dot_tn(slot_hot, buffer)).astype(BF16)


def finish(hidden, slot_row, pieces):
    return pl.pallas_call(
        finish_kernel,
        grid=(1,),
        in_specs=[whole(hidden.shape), whole(slot_row.shape)] + piece_specs(pieces),
        out_specs=whole(hidden.shape),
        out_shape=jax.ShapeDtypeStruct(hidden.shape, BF16),
        cost_estimate=LIGHT,
        name="finish",
    )(hidden, slot_row, *[array for array, _ in pieces])


def grad_act_kernel(weight_ref, *refs):
    rows_ref, out_ref = refs[-2:]

    @pl.when(pl.program_id(0) == 0)
    def _():
        rows_ref[...] = stack_pieces(refs[:-2])

    out_ref[...] = dot_nt(rows_ref[...], weight_ref[...]).astype(BF16)


def grad_act_of(weight, pieces, chunk=1024):
    hidden_units, width = weight.shape
    rows = sum(array.shape[1] for array, _ in pieces)
    return pl.pallas_call(
        grad_act_kernel,
        grid=(hidden_units // chunk,),
        in_specs=[pl.BlockSpec((chunk, width), lambda step: (step, 0))] + piece_specs(pieces),
        out_specs=(whole((rows, width)), pl.BlockSpec((rows, chunk), lambda step: (0, step))),
        out_shape=(
            jax.ShapeDtypeStruct((rows, width), BF16),
            jax.ShapeDtypeStruct((rows, hidden_units), BF16),
        ),
        cost_estimate=LIGHT,
        name="grad_act",
    )(weight, *[array for array, _ in pieces])


def result_kernel(act_a_ref, act_b_ref, weight_ref, *refs, places):
    step = pl.program_id(0)
    total_ref = refs[-1]
    half = act_a_ref.shape[0]

    @pl.when(step == 0)
    def _():
        total_ref[...] = jnp.zeros_like(total_ref)

    total_ref[:half] += dot_nn(act_a_ref[...], weight_ref[...])
    total_ref[half:] += dot_nn(act_b_ref[...], weight_ref[...])

    @pl.when(step == pl.num_programs(0) - 1)
    def _():
        store_places(refs[:-1], total_ref, places)


def store_places(refs, total_ref, places):
    for ref, firsts in zip(refs, places):
        for block, first in enumerate(firsts):
            ref[block] = total_ref[first : first + ref.shape[1]].astype(BF16)


def result_of(act_a, act_b, weight, places, block_rows, chunk=1024):
    half, hidden_units = act_a.shape
    width = weight.shape[1]
    shapes = [(len(firsts), block_rows, width) for firsts in places]
    act_spec = pl.BlockSpec((half, chunk), lambda step: (0, step))
    return pl.pallas_call(
        functools.partial(result_kernel, places=places),
        grid=(hidden_units // chunk,),
        in_specs=[act_spec, act_spec, pl.BlockSpec((chunk, width), lambda step: (step, 0))],
        out_specs=tuple(whole(shape) for shape in shapes),
        out_shape=tuple(jax.ShapeDtypeStruct(shape, BF16) for shape in shapes),
        scratch_shapes=[pltpu.VMEM((2 * half, width), F32)],
        cost_estimate=LIGHT,
        name="result",
    )(act_a, act_b, weight)


def gate_parts(pre):
    square = pre * pre
    curve = jnp.tanh(pre * (GATE_A + GATE_B * square))
    half = 0.5 * curve + 0.5
    slope = half + (0.5 * pre) * (1.0 - curve * curve) * (GATE_A + (3.0 * GATE_B) * square)
    return pre * half, slope


def expert_kernel(tile, places, piece_count, grad_act_ref, weight_ref, *refs):
    step = pl.program_id(0)
    act_ref, grad_pre_ref, rows_ref = refs[piece_count : piece_count + 3]
    out_refs, total_ref = refs[piece_count + 3 : -1], refs[-1]

    @pl.when(step == 0)
    def _():
        rows_ref[...] = stack_pieces(refs[:piece_count])
        total_ref[...] = jnp.zeros_like(total_ref)

    weight = weight_ref[...]
    for first in range(0, rows_ref.shape[0], tile):
        rows = slice(first, first + tile)
        act, slope = gate_parts(dot_nn(rows_ref[rows, :], weight))
        act_ref[rows, :] = act.astype(BF16)
        grad_pre = (grad_act_ref[rows, :].astype(F32) * slope).astype(BF16)
        grad_pre_ref[rows, :] = grad_pre
        total_ref[rows, :] += dot_nt(grad_pre, weight)

    @pl.when(step == pl.num_programs(0) - 1)
    def _():
        store_places(out_refs, total_ref, places)


def expert(half, grad_act, weight, pieces, places, block_rows, chunk=1024, tile=256):
    width, hidden_units = weight.shape
    rows = grad_act.shape[0] // 2
    column_spec = pl.BlockSpec((rows, chunk), lambda step: (0, step))
    shapes = [(len(firsts), block_rows, width) for firsts in places]
    return pl.pallas_call(
        functools.partial(expert_kernel, tile, places, len(pieces)),
        grid=(hidden_units // chunk,),
        in_specs=[
            pl.BlockSpec((rows, chunk), lambda step: (half, step)),
            pl.BlockSpec((width, chunk), lambda step: (0, step)),
        ]
        + piece_specs(pieces),
        out_specs=(column_spec, column_spec, whole((rows, width)))
        + tuple(whole(shape) for shape in shapes),
        out_shape=(
            jax.ShapeDtypeStruct((rows, hidden_units), BF16),
            jax.ShapeDtypeStruct((rows, hidden_units), BF16),
            jax.ShapeDtypeStruct((rows, width), BF16),
        )
        + tuple(jax.ShapeDtypeStruct(shape, BF16) for shape in shapes),
        scratch_shapes=[pltpu.VMEM((rows, width), F32)],
        cost_estimate=LIGHT,
        name="expert",
    )(grad_act, weight, *[array for array, _ in pieces])


def first_grad_kernel(flip_ref, rows_a_ref, rows_b_ref, grad_a_ref, grad_b_ref, *refs):
    step = pl.program_id(0)
    half_steps = pl.num_programs(0) // 2
    product_ref = refs[-1]
    product = dot_tn(rows_a_ref[...], grad_a_ref[...]) + dot_tn(rows_b_ref[...], grad_b_ref[...])
    product_ref[...] = product.astype(BF16)
    owned = product_ref.shape[0] // 4

    def piece(place):
        row = pl.multiple_of((place ^ flip_ref[0]) * owned, owned)
        return product_ref[pl.ds(row, owned), :]

    keep_a, send_a, keep_b, send_b = refs[:-1]

    @pl.when(step < half_steps)
    def _():
        for index, (kept, sent) in enumerate(((0, 1), (2, 3))):
            keep_a[index] = piece(kept)
            send_a[index] = piece(sent)

    @pl.when(step >= half_steps)
    def _():
        for index, (kept, sent) in enumerate(((0, 2), (1, 3))):
            keep_b[index] = piece(kept)
            send_b[index] = piece(sent)


def first_grad(flip, rows_a, rows_b, grad_a, grad_b, chunk=1024):
    rows, width = rows_a.shape
    columns = grad_a.shape[1]
    steps = columns // chunk
    shape = jax.ShapeDtypeStruct((2, width // 4, columns // 2), BF16)
    block = (2, width // 4, chunk)
    spec_a = pl.BlockSpec(block, lambda step: (0, 0, jnp.minimum(step, steps // 2 - 1)))
    spec_b = pl.BlockSpec(block, lambda step: (0, 0, jnp.maximum(step - steps // 2, 0)))
    return pl.pallas_call(
        first_grad_kernel,
        grid=(steps,),
        in_specs=[
            pl.BlockSpec(memory_space=pltpu.SMEM),
            whole((rows, width)),
            whole((rows, width)),
            pl.BlockSpec((rows, chunk), lambda step: (0, step)),
            pl.BlockSpec((rows, chunk), lambda step: (0, step)),
        ],
        out_specs=(spec_a, spec_a, spec_b, spec_b),
        out_shape=(shape,) * 4,
        scratch_shapes=[pltpu.VMEM((width, chunk), BF16)],
        cost_estimate=LIGHT,
        name="first_grad",
    )(flip, rows_a, rows_b, grad_a, grad_b)


def second_grad_kernel(
    flip_ref, act_a_ref, act_b_ref, grad_ref, keep_a, send_a, keep_b, send_b
):
    step = pl.program_id(0)
    rows = act_a_ref.shape[0]
    product = dot_tn(act_a_ref[...], grad_ref[:rows]) + dot_tn(act_b_ref[...], grad_ref[rows:])
    product = product.astype(BF16)
    half = product.shape[1] // 2

    @pl.when(step == 0)
    def _():
        send_a[0] = product[:, :half]
        send_b[0] = product[:, half:]

    @pl.when(step == 1)
    def _():
        send_a[0] = product[:, :half]
        keep_b[0] = product[:, half:]

    @pl.when(step == 2)
    def _():
        keep_a[0] = product[:, :half]
        send_b[0] = product[:, half:]

    @pl.when(step == 3)
    def _():
        keep_a[0] = product[:, :half]
        keep_b[0] = product[:, half:]


def second_grad(flip, act_a, act_b, grad):
    rows, width = grad.shape
    owned = act_a.shape[1] // 4
    act_spec = pl.BlockSpec(
        (rows // 2, owned), lambda step, flip_ref: (0, place_of(step) ^ flip_ref[0])
    )
    shape = jax.ShapeDtypeStruct((2, owned, width // 2), BF16)
    block = (1, owned, width // 2)

    def spec(first_step):
        return pl.BlockSpec(
            block, lambda step, flip_ref: (1 - (step >= first_step).astype(jnp.int32), 0, 0)
        )

    return pl.pallas_call(
        second_grad_kernel,
        grid_spec=pltpu.PrefetchScalarGridSpec(
            num_scalar_prefetch=1,
            grid=(4,),
            in_specs=[
                act_spec,
                act_spec,
                pl.BlockSpec((rows, width), lambda step, flip_ref: (0, 0)),
            ],
            out_specs=(spec(3), spec(1), spec(3), spec(2)),
        ),
        out_shape=(shape,) * 4,
        cost_estimate=LIGHT,
        name="second_grad",
    )(flip, act_a, act_b, grad)


def place_of(step):
    return jnp.where(step == 0, 3, jnp.where(step == 3, 0, step))


def swap(values, axis, bits):
    size = lax.axis_size(axis)
    return lax.ppermute(values, axis, [(index, index ^ bits) for index in range(size)])


def swap_copies(parts):
    return swap(parts[1], "rep", 1), swap(parts[3], "rep", 2)


def half_sum_kernel(keep_a, got_a, keep_b, got_b, out_a, out_b):
    out_a[...] = add_low(keep_a[...], got_a[...])
    out_b[...] = add_low(keep_b[...], got_b[...])


def half_sums(parts, got, chunks=2):
    _, rows, width = got[0].shape
    block = (None, rows // chunks, width)
    out_spec = pl.BlockSpec(block[1:], lambda step: (step, 0))
    return pl.pallas_call(
        half_sum_kernel,
        grid=(chunks,),
        in_specs=[pl.BlockSpec(block, lambda step: (1, step, 0))] * 4,
        out_specs=(out_spec,) * 2,
        out_shape=(jax.ShapeDtypeStruct((rows, width), BF16),) * 2,
        cost_estimate=LIGHT,
        name="half_sum",
    )(parts[0], got[0], parts[2], got[1])


def copy_sum_kernel(*refs):
    out_ref = refs[-1]
    half = out_ref.shape[1] // 2
    for index, columns in ((0, slice(0, half)), (3, slice(half, 2 * half))):
        keep, got, more = [ref[...].astype(F32) for ref in refs[index : index + 3]]
        out_ref[:, columns] = keep + got + more


def copy_sum(parts, got, more):
    keep_a, _, keep_b, _ = parts
    chunks = 4
    _, rows, width = keep_a.shape
    first = pl.BlockSpec((None, rows // chunks, width), lambda step: (0, step, 0))
    plain = pl.BlockSpec((rows // chunks, width), lambda step: (step, 0))
    return pl.pallas_call(
        copy_sum_kernel,
        grid=(chunks,),
        in_specs=[first, first, plain] * 2,
        out_specs=pl.BlockSpec((rows // chunks, 2 * width), lambda step: (step, 0)),
        out_shape=jax.ShapeDtypeStruct((rows, 2 * width), F32),
        cost_estimate=LIGHT,
        name="copy_sum",
    )(keep_a, got[0], more[0], keep_b, got[1], more[1])


def split_sum_kernel(keep_low, keep_high, got_low, got_high, low_ref, high_ref):
    low_ref[...] = add_low(keep_low[...], got_low[...])
    high_ref[...] = add_low(keep_high[...], got_high[...])


def split_sum(keep, got, cost=LIGHT):
    half, width = keep.shape[0] // 2, keep.shape[1]
    if half < 64:
        total = add_low(keep, got)
        return total[:half], total[half:]
    chunks = 2 if half % 128 == 0 else 1
    block = (half // chunks, width)
    low = pl.BlockSpec(block, lambda step: (step, 0))
    high = pl.BlockSpec(block, lambda step: (step + chunks, 0))
    return pl.pallas_call(
        split_sum_kernel,
        grid=(chunks,),
        in_specs=[low, high, low, high],
        out_specs=(low, low),
        out_shape=(jax.ShapeDtypeStruct((half, width), BF16),) * 2,
        cost_estimate=cost,
        name="split_sum",
    )(keep, keep, got, got)


def swap_halves(dense, steps):
    return [swap(send, axis, 1 << bit) for (_, send), (axis, bit) in zip(dense, steps)]


def swap_sums(sums):
    return swap(sums[0], "rep", 2), swap(sums[1], "rep", 1)


def add_low(left, right):
    return (left.astype(F32) + right.astype(F32)).astype(BF16)


def spread(blocks):
    return {bits: swap(block, "ep", bits) if bits else block for bits, block in blocks.items()}


def gather_kernel(*refs):
    for index, ref in enumerate(refs[:-1]):
        refs[-1][index] = ref[...]


def cross(blocks, members):
    return swap(jnp.concatenate([blocks[bits][1:] for bits in members], 0), "ep", 1)


def cross_late(blocks, members):
    pieces = [(blocks[bits], 1) for bits in members]
    shape = (len(pieces),) + blocks[members[0]].shape[1:]
    gathered = pl.pallas_call(
        gather_kernel,
        grid=(1,),
        in_specs=piece_specs(pieces),
        out_specs=whole(shape),
        out_shape=jax.ShapeDtypeStruct(shape, BF16),
        cost_estimate=LIGHT,
        name="gather_sum",
    )(*[array for array, _ in pieces])
    return swap(gathered, "ep", 1)


def paired_pieces(blocks, members, cross):
    crossed = cross(blocks, members)
    pieces = [((blocks[bits], 0), (crossed, place)) for place, bits in enumerate(members)]
    return [piece for pair in pieces for piece in pair]


def exchange(buffer):
    return lax.all_to_all(buffer, "ep", split_axis=0, concat_axis=0, tiled=True)


def local(
    tokens_in,
    token_ids,
    hash_table,
    doc_lengths,
    gain_one,
    shift_one,
    project_in,
    project_out,
    gain_two,
    shift_two,
    expert_in,
    expert_out,
    out_grad,
):
    tok_rows, width = tokens_in.shape
    rep_size, ep_size = lax.axis_size("rep"), lax.axis_size("ep")
    rep_bits, ep_bits = rep_size.bit_length() - 1, ep_size.bit_length() - 1
    expert_count = expert_in.shape[0] * ep_size
    capacity = 2 * tok_rows // expert_count
    slot_total = expert_count * capacity
    tile = width // (rep_size * ep_size)
    paired = expert_count <= 8
    first_weight, second_weight = expert_in[0], expert_out[0]
    rep_index, ep_index = lax.axis_index("rep"), lax.axis_index("ep")
    ep_flip = jnp.reshape(ep_index if paired else 0, (1,)).astype(jnp.int32)
    rep_flip = jnp.reshape(rep_index, (1,)).astype(jnp.int32)
    ep_steps = [("ep", bit) for bit in range(1, ep_bits)]
    rep_steps = [("rep", bit) for bit in range(rep_bits)]
    steps_a, steps_b = ep_steps + rep_steps, ep_steps[::-1] + rep_steps[::-1]
    orders, spots = [], []
    for steps in (steps_a, steps_b):
        places = [bit + (ep_bits if axis == "rep" else 0) for axis, bit in reversed(steps)] + [0]
        orders.append(tuple(places))
        spots.append(spread_bits(rep_index * ep_size + ep_index, places))
    spots = jnp.stack(spots).astype(jnp.int32)

    fronts = (
        doc_lengths,
        tokens_in,
        gain_one,
        shift_one,
        project_in,
        project_out,
        gain_two,
        shift_two,
    )
    half_rows = slot_total // 2
    if paired:
        members = tuple(range(0, expert_count, 2))
        order = members[::2] + members[1::2]
        halves = (members[::2], members[1::2])
        block_rows, block_shape = capacity, (2, capacity, width)
    else:
        block_rows, block_shape = half_rows, (expert_count, capacity, width)
    slot_row, *buffers = route(
        ep_flip, token_ids, hash_table, out_grad, expert_count, capacity, block_shape
    )
    grads = spread(dict(zip(members, buffers))) if paired else exchange(buffers[0])
    normed, query, key, value, probs, mixture, hidden, *buffers = front(
        *fronts[:2], slot_row, *fronts[2:], slot_total, block_shape
    )
    if paired:
        blocks, hidden = lax.optimization_barrier(([grads[bits] for bits in members], hidden))
        grads = dict(zip(members, blocks))
        crossed = cross(grads, order)
        grad_pieces = []
        for index, half in enumerate(halves):
            grad_pieces += [(grads[bits], 0) for bits in half]
            grad_pieces += [(crossed, index * len(half) + place) for place in range(len(half))]
    else:
        grads = grads.reshape(2, half_rows, width)
        grad_pieces = [(grads, 0), (grads, 1)]
    grad_rows, grad_act = grad_act_of(second_weight, grad_pieces)
    outs = []
    if paired:
        received = spread(dict(zip(members, buffers)))
        count = len(halves[0])
        places = [[place * capacity, (count + place) * capacity] for place in range(count)]
        sent = {}
        done = grad_rows
        for index, half in ((1, halves[1]), (0, halves[0])):
            blocks, done = lax.optimization_barrier(([received[bits] for bits in half], done))
            received.update(zip(half, blocks))
            if index:
                grad_rows = done
            else:
                outs[0][2] = done
            crossed = cross(received, half)
            pieces = [(received[bits], 0) for bits in half]
            pieces += [(crossed, place) for place in range(count)]
            *out, = expert(index, grad_act, first_weight, pieces, places, capacity)
            outs.append(out[:3])
            done = out[2]
            sent.update(spread(dict(zip(half, out[3:]))))
        places += [[first + half_rows for first in firsts] for firsts in places]
    else:
        received = exchange(buffers[0]).reshape(2, half_rows, width)
        places = [[0]]
        for index in range(2):
            *out, = expert(index, grad_act, first_weight, [(received, index)], places, half_rows)
            outs.append(out)
        sent = jnp.concatenate([outs[0][3], outs[1][3]], 0).reshape(buffers[0].shape)
        back_pieces = [(exchange(sent).reshape(1, slot_total, width), 0)]
        places = [[0, half_rows]]
    if paired:
        outs = outs[::-1]
    (act_a, grad_pre_a, rows_a), (act_b, grad_pre_b, rows_b) = outs[0][:3], outs[1][:3]
    second_parts = second_grad(rep_flip, act_a, act_b, grad_rows)
    act_a, second_parts = lax.optimization_barrier((act_a, second_parts))
    results = result_of(act_a, act_b, second_weight, places, block_rows)
    got_second = swap_copies(second_parts)
    if paired:
        blocks, results = lax.optimization_barrier(([sent[bits] for bits in members], results))
        back_pieces = paired_pieces(dict(zip(members, blocks)), members, cross)
    returned = spread(dict(zip(order, results))) if paired else exchange(
        results[0].reshape(expert_count, capacity, width)
    )
    keep_a, send_a, keep_b, send_b, grad_in = back(
        tile,
        orders,
        spots,
        back_pieces,
        slot_row,
        hidden,
        gain_two,
        out_grad,
        mixture,
        project_out,
        query,
        key,
        value,
        probs,
        normed,
        project_in,
        tokens_in,
        gain_one,
    )
    sends = (send_a, send_b)
    sends, got_second, returned = lax.optimization_barrier((sends, got_second, returned))
    got_a, got_b = swap(sends[0], "ep", 1), swap(sends[1], "ep", 1)
    sums_second = half_sums(second_parts, got_second)
    dense = [split_sum(keep_a, got_a), split_sum(keep_b, got_b)]
    rows_a, sums_second, dense = lax.optimization_barrier((rows_a, sums_second, dense))
    more_second = swap_sums(sums_second)
    first_parts = first_grad(rep_flip, rows_a, rows_b, grad_pre_a, grad_pre_b)
    first_parts, more_second = lax.optimization_barrier((first_parts, more_second))
    got_first = swap_copies(first_parts)
    summed_second = copy_sum(second_parts, got_second, more_second)
    if paired:
        pieces = paired_pieces(returned, members, cross_late)
    else:
        pieces = [(returned.reshape(1, slot_total, width), 0)]
    block_out = finish(hidden, slot_row, pieces)
    for index, pair in enumerate(zip(steps_a, steps_b)):
        got = swap_halves(dense, pair)
        if index == 0:
            got, summed_second, block_out = lax.optimization_barrier(
                (got, summed_second, block_out)
            )
        if index == 2:
            got, more_first = lax.optimization_barrier((got, more_first))
            summed_first = copy_sum(first_parts, got_first, more_first)
        if index < len(steps_a) - 1:
            cost = LIGHT if index > 1 else HEAVY
            dense = [split_sum(keep, more, cost) for (keep, _), more in zip(dense, got)]
        if index == 0:
            got_first, dense = lax.optimization_barrier((got_first, dense))
            more_first = swap_sums(half_sums(first_parts, got_first))
    dense_a, dense_b = [keep.astype(F32) + more.astype(F32) for (keep, _), more in zip(dense, got)]
    return (
        block_out,
        grad_in,
        jnp.concatenate([dense_a[:, : 2 * width], dense_b[:, :width]], 1),
        dense_b[:, width:],
        dense_a[:, 2 * width + 2],
        dense_a[:, 2 * width + 3],
        dense_a[:, 2 * width],
        dense_a[:, 2 * width + 1],
        summed_first[None],
        summed_second[None],
    )


def solution(mesh):
    in_specs = (
        P(("rep", "ep"), None),
        P(("rep", "ep")),
        P(),
        P(("rep", "ep"), None),
        P(),
        P(),
        P(),
        P(),
        P(),
        P(),
        P("ep", None, None),
        P("ep", None, None),
        P(("rep", "ep"), None),
    )
    out_specs = (
        P(("rep", "ep"), None),
        P(("rep", "ep"), None),
        P(("rep", "ep"), None),
        P(("rep", "ep"), None),
        P(("rep", "ep")),
        P(("rep", "ep")),
        P(("rep", "ep")),
        P(("rep", "ep")),
        P("ep", "rep", None),
        P("ep", "rep", None),
    )
    return jax.shard_map(local, mesh=mesh, in_specs=in_specs, out_specs=out_specs, check_vma=False)
```

```python
import functools
import math

import jax
import jax.numpy as jnp
from jax import lax
from jax.experimental import pallas as pl
from jax.experimental.pallas import tpu as pltpu
from jax.sharding import PartitionSpec as P

HEADS = 16
GROUP = 4
LANES = 128
NEG_LARGE = -1e30
EPSILON = 1e-05
BF16 = jnp.bfloat16
F32 = jnp.float32
GATE_A = math.sqrt(2.0 / math.pi)
GATE_B = GATE_A * 0.044715
HEAVY = pl.CostEstimate(flops=10000000000, bytes_accessed=1 << 16, transcendentals=0)
LIGHT = pl.CostEstimate(flops=1 << 20, bytes_accessed=1 << 16, transcendentals=0)


def dot_nn(a, b):
    return lax.dot_general(a, b, (((1,), (0,)), ((), ())), preferred_element_type=F32)


def dot_nt(a, b):
    return lax.dot_general(a, b, (((1,), (1,)), ((), ())), preferred_element_type=F32)


def dot_tn(a, b):
    return lax.dot_general(a, b, (((0,), (0,)), ((), ())), preferred_element_type=F32)


def iota(shape, axis):
    return lax.broadcasted_iota(jnp.int32, shape, axis)


def whole(shape):
    return pl.BlockSpec(shape, lambda *_: (0,) * len(shape))


def piece_specs(pieces):
    def spec(array, block):
        return pl.BlockSpec((None,) + array.shape[1:], lambda *_: (block, 0, 0))

    return [spec(array, block) for array, block in pieces]


def stack_pieces(refs):
    return jnp.concatenate([ref[...] for ref in refs], 0)


def store_blocks(refs, values):
    first = 0
    for ref in refs:
        for block in range(ref.shape[0]):
            ref[block] = values[first : first + ref.shape[1]]
            first += ref.shape[1]


def norm_parts(values):
    center = jnp.mean(values, -1, keepdims=True)
    centered = values - center
    spread = jnp.mean(centered * centered, -1, keepdims=True)
    factor = lax.rsqrt(spread + EPSILON)
    return centered * factor, factor


def norm_back(grad, gain, xhat, factor):
    scaled = grad * gain
    mean_scaled = jnp.mean(scaled, -1, keepdims=True)
    mean_cross = jnp.mean(scaled * xhat, -1, keepdims=True)
    return factor * (scaled - mean_scaled - xhat * mean_cross)


def slot_matrix(slot_row, slot_total):
    tok_rows = slot_row.shape[1]
    return (iota((slot_total, tok_rows), 0) == slot_row).astype(F32).astype(BF16)


def route_kernel(
    expert_count, capacity, flip_ref, ids_ref, table_ref, grad_ref, slot_ref, *buffer_refs
):
    tok_rows = ids_ref.shape[1]
    ids = ids_ref[...]
    table_rows = table_ref.shape[0]
    high = ids // LANES
    low = ids - high * LANES
    high_hot = (iota((table_rows, tok_rows), 0) == high).astype(F32).astype(BF16)
    picked = dot_tn(table_ref[...].astype(F32).astype(BF16), high_hot)
    low_hot = iota((LANES, tok_rows), 0) == low
    expert = jnp.sum(jnp.where(low_hot, picked, 0.0), 0, keepdims=True).astype(jnp.int32)
    expert_hot = (iota((expert_count, tok_rows), 0) == expert).astype(F32)
    before = (iota((tok_rows, tok_rows), 0) < iota((tok_rows, tok_rows), 1)).astype(F32)
    earlier = dot_nn(expert_hot.astype(BF16), before.astype(BF16))
    rank = jnp.sum(earlier * expert_hot, 0, keepdims=True).astype(jnp.int32)
    slot = (expert ^ flip_ref[0]) * capacity + rank
    slot_ref[...] = slot
    slot_hot = slot_matrix(slot, expert_count * capacity)
    store_blocks(buffer_refs, dot_nn(slot_hot, grad_ref[...]).astype(BF16))


def route(flip, token_ids, hash_table, out_grad, expert_count, capacity, block_shape):
    tok_rows, width = out_grad.shape
    slot_total = expert_count * capacity
    table_rows = hash_table.shape[0] // LANES
    blocks = slot_total // (block_shape[0] * block_shape[1])
    return pl.pallas_call(
        functools.partial(route_kernel, expert_count, capacity),
        in_specs=[
            pl.BlockSpec(memory_space=pltpu.SMEM),
            whole((1, tok_rows)),
            whole((table_rows, LANES)),
            whole((tok_rows, width)),
        ],
        out_specs=(whole((1, tok_rows)),) + (whole(block_shape),) * blocks,
        out_shape=(jax.ShapeDtypeStruct((1, tok_rows), jnp.int32),)
        + (jax.ShapeDtypeStruct(block_shape, BF16),) * blocks,
        cost_estimate=LIGHT,
        name="route",
    )(flip, token_ids.reshape(1, tok_rows), hash_table.reshape(table_rows, LANES), out_grad)


def front_kernel(
    slot_total,
    head_size,
    lengths_ref,
    tokens_ref,
    slot_ref,
    gain_one_ref,
    shift_one_ref,
    query_weight_ref,
    key_weight_ref,
    value_weight_ref,
    out_weight_ref,
    gain_two_ref,
    shift_two_ref,
    normed_ref,
    query_ref,
    key_ref,
    value_ref,
    probs_ref,
    mixture_ref,
    hidden_ref,
    *refs,
):
    buffer_refs, mask_ref = refs[:-1], refs[-1]
    step = pl.program_id(0)
    tok_rows = tokens_ref.shape[0]
    group_width = query_ref.shape[1]

    @pl.when(step == 0)
    def _():
        inputs = tokens_ref[...].astype(F32)
        xhat, _ = norm_parts(inputs)
        normed_ref[...] = (xhat * gain_one_ref[...] + shift_one_ref[...]).astype(BF16)
        position = iota((1, tok_rows), 1)
        start = jnp.zeros((1, tok_rows), jnp.int32)
        bound = jnp.int32(0)
        for index in range(lengths_ref.shape[1]):
            bound = bound + lengths_ref[0, index]
            start = jnp.where(position >= bound, bound, start)
        key_position = iota((tok_rows, tok_rows), 0)
        allowed = jnp.logical_and(key_position >= start, key_position <= position)
        mask_ref[...] = jnp.where(allowed, 0.0, NEG_LARGE)
        hidden_ref[...] = inputs

    normed = normed_ref[...]
    query = dot_nn(normed, query_weight_ref[...]).astype(BF16)
    key = dot_nn(normed, key_weight_ref[...]).astype(BF16)
    value = dot_nn(normed, value_weight_ref[...]).astype(BF16)
    query_ref[...] = query
    key_ref[...] = key
    value_ref[...] = value
    lane_head = iota((1, group_width), 1) // head_size
    scale = 1.0 / math.sqrt(head_size)
    total = jnp.zeros((tok_rows, group_width), F32)
    for head in range(GROUP):
        chosen = lane_head == head
        key_part = key * jnp.where(chosen, scale, 0.0).astype(BF16)
        value_part = value * jnp.where(chosen, 1.0, 0.0).astype(BF16)
        scores = dot_nt(key_part, query) + mask_ref[...]
        exponent = jnp.exp(scores - jnp.max(scores, 0, keepdims=True))
        inverse = 1.0 / jnp.sum(exponent, 0, keepdims=True)
        weights = (exponent * inverse).astype(BF16)
        probs_ref[head] = weights
        total = total + dot_tn(weights, value_part)
    mixture = total.astype(BF16)
    mixture_ref[...] = mixture
    hidden_ref[...] += dot_nn(mixture, out_weight_ref[...])

    @pl.when(step == pl.num_programs(0) - 1)
    def _():
        xhat, _ = norm_parts(hidden_ref[...])
        routed = (xhat * gain_two_ref[...] + shift_two_ref[...]).astype(BF16)
        slot_hot = slot_matrix(slot_ref[...], slot_total)
        store_blocks(buffer_refs, dot_nn(slot_hot, routed).astype(BF16))


def front(
    doc_lengths,
    tokens_in,
    slot_row,
    gain_one,
    shift_one,
    project_in,
    project_out,
    gain_two,
    shift_two,
    slot_total,
    block_shape,
):
    tok_rows, width = tokens_in.shape
    head_size = width // HEADS
    group_width = GROUP * head_size
    steps = HEADS // GROUP
    vector = whole((1, width))
    blocks = slot_total // (block_shape[0] * block_shape[1])

    def weight_spec(part):
        return pl.BlockSpec((width, group_width), lambda step: (0, part * steps + step))

    column_spec = pl.BlockSpec((tok_rows, group_width), lambda step: (0, step))
    return pl.pallas_call(
        functools.partial(front_kernel, slot_total, head_size),
        grid=(steps,),
        in_specs=[
            pl.BlockSpec(memory_space=pltpu.SMEM),
            whole((tok_rows, width)),
            whole((1, tok_rows)),
            vector,
            vector,
            weight_spec(0),
            weight_spec(1),
            weight_spec(2),
            pl.BlockSpec((group_width, width), lambda step: (step, 0)),
            vector,
            vector,
        ],
        out_specs=(
            whole((tok_rows, width)),
            column_spec,
            column_spec,
            column_spec,
            pl.BlockSpec((GROUP, tok_rows, tok_rows), lambda step: (step, 0, 0)),
            column_spec,
            whole((tok_rows, width)),
        )
        + (whole(block_shape),) * blocks,
        out_shape=(
            jax.ShapeDtypeStruct((tok_rows, width), BF16),
            jax.ShapeDtypeStruct((tok_rows, width), BF16),
            jax.ShapeDtypeStruct((tok_rows, width), BF16),
            jax.ShapeDtypeStruct((tok_rows, width), BF16),
            jax.ShapeDtypeStruct((HEADS, tok_rows, tok_rows), BF16),
            jax.ShapeDtypeStruct((tok_rows, width), BF16),
            jax.ShapeDtypeStruct((tok_rows, width), F32),
        )
        + (jax.ShapeDtypeStruct(block_shape, BF16),) * blocks,
        scratch_shapes=[pltpu.VMEM((tok_rows, tok_rows), F32)],
        cost_estimate=LIGHT,
        name="front",
    )(
        doc_lengths,
        tokens_in,
        slot_row,
        gain_one.reshape(1, width),
        shift_one.reshape(1, width),
        project_in,
        project_in,
        project_in,
        project_out,
        gain_two.reshape(1, width),
        shift_two.reshape(1, width),
    )


def spread_bits(index, layout):
    spot = 0
    for place, bit in enumerate(layout):
        spot = spot | (((index >> bit) & 1) << place)
    return spot


def store_rows(refs, first, column, values, tile, order, spot):
    keep_ref, send_ref = refs
    layout = order
    top = len(layout) - 1
    even_kept = (spot >> top) == 0
    for index in range(0, values.shape[0] // tile, 2):
        place = (spread_bits(first + index, layout) ^ spot) & ((1 << top) - 1)
        even = values[index * tile : (index + 1) * tile]
        odd = values[(index + 1) * tile : (index + 2) * tile]
        rows = pl.ds(pl.multiple_of(place * tile, tile), tile)
        keep_ref[rows, column] = jnp.where(even_kept, even, odd).astype(BF16)
        send_ref[rows, column] = jnp.where(even_kept, odd, even).astype(BF16)


def back_kernel(
    head_size,
    tile,
    orders,
    piece_count,
    spot_ref,
    slot_ref,
    hidden_ref,
    gain_two_ref,
    out_grad_ref,
    mixture_ref,
    out_weight_ref,
    query_ref,
    key_ref,
    value_ref,
    probs_ref,
    normed_ref,
    query_weight_ref,
    key_weight_ref,
    value_weight_ref,
    tokens_ref,
    gain_one_ref,
    *refs,
):
    piece_refs = refs[:piece_count]
    dense_a = refs[piece_count : piece_count + 2]
    dense_b = refs[piece_count + 2 : piece_count + 4]
    grad_in_ref, hidden_low_ref, normed_grad_ref, small_ref = refs[piece_count + 4 :]
    step = pl.program_id(0)
    width = tokens_ref.shape[1]
    group_width = query_ref.shape[1]

    @pl.when(step == 0)
    def _():
        buffer = stack_pieces(piece_refs)
        slot_hot = slot_matrix(slot_ref[...], buffer.shape[0])
        grad_routed = dot_tn(slot_hot, buffer)
        xhat, factor = norm_parts(hidden_ref[...])
        small_ref[0:1, :] = jnp.sum(grad_routed * xhat, 0, keepdims=True)
        small_ref[1:2, :] = jnp.sum(grad_routed, 0, keepdims=True)
        grad_hidden = out_grad_ref[...].astype(F32) + norm_back(
            grad_routed, gain_two_ref[...], xhat, factor
        )
        grad_in_ref[...] = grad_hidden
        hidden_low_ref[...] = grad_hidden.astype(BF16)
        normed_grad_ref[...] = jnp.zeros_like(normed_grad_ref)
        small_ref[4:, :] = jnp.zeros((LANES - 4, width), F32)

    hidden_low = hidden_low_ref[...]
    store_rows(
        dense_b,
        step * (group_width // tile),
        slice(width, 2 * width),
        dot_tn(mixture_ref[...], hidden_low),
        tile,
        orders[1],
        spot_ref[1],
    )
    grad_mixture = dot_nt(hidden_low, out_weight_ref[...]).astype(BF16)
    query, key, value = query_ref[...], key_ref[...], value_ref[...]
    lane_head = iota((1, group_width), 1) // head_size
    scale = 1.0 / math.sqrt(head_size)
    grad_query = jnp.zeros(query.shape, F32)
    grad_key = jnp.zeros(query.shape, F32)
    grad_value = jnp.zeros(query.shape, F32)
    for head in range(GROUP):
        chosen = jnp.where(lane_head == head, 1.0, 0.0).astype(BF16)
        scaled = jnp.where(lane_head == head, scale, 0.0).astype(BF16)
        grad_part = grad_mixture * chosen
        weights_low = probs_ref[head]
        weights = weights_low.astype(F32)
        grad_weights = dot_nt(value, grad_part)
        inner = jnp.sum(weights * grad_weights, 0, keepdims=True)
        grad_scores = (weights * (grad_weights - inner)).astype(BF16)
        grad_query = grad_query + dot_tn(grad_scores, key * scaled)
        grad_key = grad_key + dot_nn(grad_scores, query * scaled)
        grad_value = grad_value + dot_nn(weights_low, grad_part)
    normed = normed_ref[...]
    for part, (grad, weight_ref) in enumerate(
        (
            (grad_query, query_weight_ref),
            (grad_key, key_weight_ref),
            (grad_value, value_weight_ref),
        )
    ):
        grad = grad.astype(BF16)
        index = part // 2
        column = pl.multiple_of((part % 2) * width + step * group_width, group_width)
        store_rows(
            (dense_a, dense_b)[index],
            0,
            pl.ds(column, group_width),
            dot_tn(normed, grad),
            tile,
            orders[index],
            spot_ref[index],
        )
        normed_grad_ref[...] += dot_nt(grad, weight_ref[...])

    @pl.when(step == pl.num_programs(0) - 1)
    def _():
        grad_normed = normed_grad_ref[...]
        xhat, factor = norm_parts(tokens_ref[...].astype(F32))
        small_ref[2:3, :] = jnp.sum(grad_normed * xhat, 0, keepdims=True)
        small_ref[3:4, :] = jnp.sum(grad_normed, 0, keepdims=True)
        store_rows(
            dense_a,
            0,
            slice(2 * width, 2 * width + LANES),
            small_ref[...].T,
            tile,
            orders[0],
            spot_ref[0],
        )
        grad_in_ref[...] += norm_back(grad_normed, gain_one_ref[...], xhat, factor)


def back(
    tile,
    orders,
    spots,
    pieces,
    slot_row,
    hidden,
    gain_two,
    out_grad,
    mixture,
    project_out,
    query,
    key,
    value,
    probs,
    normed,
    project_in,
    tokens_in,
    gain_one,
):
    tok_rows, width = tokens_in.shape
    head_size = width // HEADS
    group_width = GROUP * head_size
    steps = HEADS // GROUP
    vector = whole((1, width))
    tokens_spec = whole((tok_rows, width))

    def weight_spec(part):
        return pl.BlockSpec((width, group_width), lambda step: (0, part * steps + step))

    column_spec = pl.BlockSpec((tok_rows, group_width), lambda step: (0, step))
    return pl.pallas_call(
        functools.partial(back_kernel, head_size, tile, orders, len(pieces)),
        grid=(steps,),
        in_specs=[
            pl.BlockSpec(memory_space=pltpu.SMEM),
            whole((1, tok_rows)),
            tokens_spec,
            vector,
            tokens_spec,
            column_spec,
            pl.BlockSpec((group_width, width), lambda step: (step, 0)),
            column_spec,
            column_spec,
            column_spec,
            pl.BlockSpec((GROUP, tok_rows, tok_rows), lambda step: (step, 0, 0)),
            tokens_spec,
            weight_spec(0),
            weight_spec(1),
            weight_spec(2),
            tokens_spec,
            vector,
        ]
        + piece_specs(pieces),
        out_specs=(
            whole((width // 2, 2 * width + LANES)),
            whole((width // 2, 2 * width + LANES)),
            whole((width // 2, 2 * width)),
            whole((width // 2, 2 * width)),
            tokens_spec,
        ),
        out_shape=(
            jax.ShapeDtypeStruct((width // 2, 2 * width + LANES), BF16),
            jax.ShapeDtypeStruct((width // 2, 2 * width + LANES), BF16),
            jax.ShapeDtypeStruct((width // 2, 2 * width), BF16),
            jax.ShapeDtypeStruct((width // 2, 2 * width), BF16),
            jax.ShapeDtypeStruct((tok_rows, width), F32),
        ),
        scratch_shapes=[
            pltpu.VMEM((tok_rows, width), BF16),
            pltpu.VMEM((tok_rows, width), F32),
            pltpu.VMEM((LANES, width), F32),
        ],
        cost_estimate=LIGHT,
        name="back",
    )(
        spots,
        slot_row,
        hidden,
        gain_two.reshape(1, width),
        out_grad,
        mixture,
        project_out,
        query,
        key,
        value,
        probs,
        normed,
        project_in,
        project_in,
        project_in,
        tokens_in,
        gain_one.reshape(1, width),
        *[array for array, _ in pieces],
    )


def finish_kernel(hidden_ref, slot_ref, *refs):
    buffer = stack_pieces(refs[:-1])
    slot_hot = slot_matrix(slot_ref[...], buffer.shape[0])
    refs[-1][...] = (hidden_ref[...] + dot_tn(slot_hot, buffer)).astype(BF16)


def finish(hidden, slot_row, pieces):
    return pl.pallas_call(
        finish_kernel,
        grid=(1,),
        in_specs=[whole(hidden.shape), whole(slot_row.shape)] + piece_specs(pieces),
        out_specs=whole(hidden.shape),
        out_shape=jax.ShapeDtypeStruct(hidden.shape, BF16),
        cost_estimate=LIGHT,
        name="finish",
    )(hidden, slot_row, *[array for array, _ in pieces])


def grad_act_kernel(weight_ref, *refs):
    rows_ref, out_ref = refs[-2:]

    @pl.when(pl.program_id(0) == 0)
    def _():
        rows_ref[...] = stack_pieces(refs[:-2])

    out_ref[...] = dot_nt(rows_ref[...], weight_ref[...]).astype(BF16)


def grad_act_of(weight, pieces, chunk=1024):
    hidden_units, width = weight.shape
    rows = sum(array.shape[1] for array, _ in pieces)
    return pl.pallas_call(
        grad_act_kernel,
        grid=(hidden_units // chunk,),
        in_specs=[pl.BlockSpec((chunk, width), lambda step: (step, 0))] + piece_specs(pieces),
        out_specs=(whole((rows, width)), pl.BlockSpec((rows, chunk), lambda step: (0, step))),
        out_shape=(
            jax.ShapeDtypeStruct((rows, width), BF16),
            jax.ShapeDtypeStruct((rows, hidden_units), BF16),
        ),
        cost_estimate=LIGHT,
        name="grad_act",
    )(weight, *[array for array, _ in pieces])


def result_kernel(act_a_ref, act_b_ref, weight_ref, *refs, places):
    step = pl.program_id(0)
    total_ref = refs[-1]
    half = act_a_ref.shape[0]

    @pl.when(step == 0)
    def _():
        total_ref[...] = jnp.zeros_like(total_ref)

    total_ref[:half] += dot_nn(act_a_ref[...], weight_ref[...])
    total_ref[half:] += dot_nn(act_b_ref[...], weight_ref[...])

    @pl.when(step == pl.num_programs(0) - 1)
    def _():
        store_places(refs[:-1], total_ref, places)


def store_places(refs, total_ref, places):
    for ref, firsts in zip(refs, places):
        for block, first in enumerate(firsts):
            ref[block] = total_ref[first : first + ref.shape[1]].astype(BF16)


def result_of(act_a, act_b, weight, places, block_rows, chunk=1024):
    half, hidden_units = act_a.shape
    width = weight.shape[1]
    shapes = [(len(firsts), block_rows, width) for firsts in places]
    act_spec = pl.BlockSpec((half, chunk), lambda step: (0, step))
    return pl.pallas_call(
        functools.partial(result_kernel, places=places),
        grid=(hidden_units // chunk,),
        in_specs=[act_spec, act_spec, pl.BlockSpec((chunk, width), lambda step: (step, 0))],
        out_specs=tuple(whole(shape) for shape in shapes),
        out_shape=tuple(jax.ShapeDtypeStruct(shape, BF16) for shape in shapes),
        scratch_shapes=[pltpu.VMEM((2 * half, width), F32)],
        cost_estimate=LIGHT,
        name="result",
    )(act_a, act_b, weight)


def gate_parts(pre):
    square = pre * pre
    curve = jnp.tanh(pre * (GATE_A + GATE_B * square))
    half = 0.5 * curve + 0.5
    slope = half + (0.5 * pre) * (1.0 - curve * curve) * (GATE_A + (3.0 * GATE_B) * square)
    return pre * half, slope


def expert_kernel(tile, places, piece_count, grad_act_ref, weight_ref, *refs):
    step = pl.program_id(0)
    act_ref, grad_pre_ref, rows_ref = refs[piece_count : piece_count + 3]
    out_refs, total_ref = refs[piece_count + 3 : -1], refs[-1]

    @pl.when(step == 0)
    def _():
        rows_ref[...] = stack_pieces(refs[:piece_count])
        total_ref[...] = jnp.zeros_like(total_ref)

    weight = weight_ref[...]
    for first in range(0, rows_ref.shape[0], tile):
        rows = slice(first, first + tile)
        act, slope = gate_parts(dot_nn(rows_ref[rows, :], weight))
        act_ref[rows, :] = act.astype(BF16)
        grad_pre = (grad_act_ref[rows, :].astype(F32) * slope).astype(BF16)
        grad_pre_ref[rows, :] = grad_pre
        total_ref[rows, :] += dot_nt(grad_pre, weight)

    @pl.when(step == pl.num_programs(0) - 1)
    def _():
        store_places(out_refs, total_ref, places)


def expert(half, grad_act, weight, pieces, places, block_rows, chunk=1024, tile=256):
    width, hidden_units = weight.shape
    rows = grad_act.shape[0] // 2
    column_spec = pl.BlockSpec((rows, chunk), lambda step: (0, step))
    shapes = [(len(firsts), block_rows, width) for firsts in places]
    return pl.pallas_call(
        functools.partial(expert_kernel, tile, places, len(pieces)),
        grid=(hidden_units // chunk,),
        in_specs=[
            pl.BlockSpec((rows, chunk), lambda step: (half, step)),
            pl.BlockSpec((width, chunk), lambda step: (0, step)),
        ]
        + piece_specs(pieces),
        out_specs=(column_spec, column_spec, whole((rows, width)))
        + tuple(whole(shape) for shape in shapes),
        out_shape=(
            jax.ShapeDtypeStruct((rows, hidden_units), BF16),
            jax.ShapeDtypeStruct((rows, hidden_units), BF16),
            jax.ShapeDtypeStruct((rows, width), BF16),
        )
        + tuple(jax.ShapeDtypeStruct(shape, BF16) for shape in shapes),
        scratch_shapes=[pltpu.VMEM((rows, width), F32)],
        cost_estimate=LIGHT,
        name="expert",
    )(grad_act, weight, *[array for array, _ in pieces])


def first_grad_kernel(flip_ref, rows_a_ref, rows_b_ref, grad_a_ref, grad_b_ref, *refs):
    step = pl.program_id(0)
    half_steps = pl.num_programs(0) // 2
    product_ref = refs[-1]
    product = dot_tn(rows_a_ref[...], grad_a_ref[...]) + dot_tn(rows_b_ref[...], grad_b_ref[...])
    product_ref[...] = product.astype(BF16)
    owned = product_ref.shape[0] // 4

    def piece(place):
        row = pl.multiple_of((place ^ flip_ref[0]) * owned, owned)
        return product_ref[pl.ds(row, owned), :]

    keep_a, send_a, keep_b, send_b = refs[:-1]

    @pl.when(step < half_steps)
    def _():
        for index, (kept, sent) in enumerate(((0, 1), (2, 3))):
            keep_a[index] = piece(kept)
            send_a[index] = piece(sent)

    @pl.when(step >= half_steps)
    def _():
        for index, (kept, sent) in enumerate(((0, 2), (1, 3))):
            keep_b[index] = piece(kept)
            send_b[index] = piece(sent)


def first_grad(flip, rows_a, rows_b, grad_a, grad_b, chunk=1024):
    rows, width = rows_a.shape
    columns = grad_a.shape[1]
    steps = columns // chunk
    shape = jax.ShapeDtypeStruct((2, width // 4, columns // 2), BF16)
    block = (2, width // 4, chunk)
    spec_a = pl.BlockSpec(block, lambda step: (0, 0, jnp.minimum(step, steps // 2 - 1)))
    spec_b = pl.BlockSpec(block, lambda step: (0, 0, jnp.maximum(step - steps // 2, 0)))
    return pl.pallas_call(
        first_grad_kernel,
        grid=(steps,),
        in_specs=[
            pl.BlockSpec(memory_space=pltpu.SMEM),
            whole((rows, width)),
            whole((rows, width)),
            pl.BlockSpec((rows, chunk), lambda step: (0, step)),
            pl.BlockSpec((rows, chunk), lambda step: (0, step)),
        ],
        out_specs=(spec_a, spec_a, spec_b, spec_b),
        out_shape=(shape,) * 4,
        scratch_shapes=[pltpu.VMEM((width, chunk), BF16)],
        cost_estimate=LIGHT,
        name="first_grad",
    )(flip, rows_a, rows_b, grad_a, grad_b)


def second_grad_kernel(
    flip_ref, act_a_ref, act_b_ref, grad_ref, keep_a, send_a, keep_b, send_b
):
    step = pl.program_id(0)
    rows = act_a_ref.shape[0]
    product = dot_tn(act_a_ref[...], grad_ref[:rows]) + dot_tn(act_b_ref[...], grad_ref[rows:])
    product = product.astype(BF16)
    half = product.shape[1] // 2

    @pl.when(step == 0)
    def _():
        send_a[0] = product[:, :half]
        send_b[0] = product[:, half:]

    @pl.when(step == 1)
    def _():
        send_a[0] = product[:, :half]
        keep_b[0] = product[:, half:]

    @pl.when(step == 2)
    def _():
        keep_a[0] = product[:, :half]
        send_b[0] = product[:, half:]

    @pl.when(step == 3)
    def _():
        keep_a[0] = product[:, :half]
        keep_b[0] = product[:, half:]


def second_grad(flip, act_a, act_b, grad):
    rows, width = grad.shape
    owned = act_a.shape[1] // 4
    act_spec = pl.BlockSpec(
        (rows // 2, owned), lambda step, flip_ref: (0, place_of(step) ^ flip_ref[0])
    )
    shape = jax.ShapeDtypeStruct((2, owned, width // 2), BF16)
    block = (1, owned, width // 2)

    def spec(first_step):
        return pl.BlockSpec(
            block, lambda step, flip_ref: (1 - (step >= first_step).astype(jnp.int32), 0, 0)
        )

    return pl.pallas_call(
        second_grad_kernel,
        grid_spec=pltpu.PrefetchScalarGridSpec(
            num_scalar_prefetch=1,
            grid=(4,),
            in_specs=[
                act_spec,
                act_spec,
                pl.BlockSpec((rows, width), lambda step, flip_ref: (0, 0)),
            ],
            out_specs=(spec(3), spec(1), spec(3), spec(2)),
        ),
        out_shape=(shape,) * 4,
        cost_estimate=LIGHT,
        name="second_grad",
    )(flip, act_a, act_b, grad)


def place_of(step):
    return jnp.where(step == 0, 3, jnp.where(step == 3, 0, step))


def swap(values, axis, bits):
    size = lax.axis_size(axis)
    return lax.ppermute(values, axis, [(index, index ^ bits) for index in range(size)])


def swap_copies(parts):
    return swap(parts[1], "rep", 1), swap(parts[3], "rep", 2)


def half_sum_kernel(keep_a, got_a, keep_b, got_b, out_a, out_b):
    out_a[...] = add_low(keep_a[...], got_a[...])
    out_b[...] = add_low(keep_b[...], got_b[...])


def half_sums(parts, got, chunks=2):
    _, rows, width = got[0].shape
    block = (None, rows // chunks, width)
    out_spec = pl.BlockSpec(block[1:], lambda step: (step, 0))
    return pl.pallas_call(
        half_sum_kernel,
        grid=(chunks,),
        in_specs=[pl.BlockSpec(block, lambda step: (1, step, 0))] * 4,
        out_specs=(out_spec,) * 2,
        out_shape=(jax.ShapeDtypeStruct((rows, width), BF16),) * 2,
        cost_estimate=LIGHT,
        name="half_sum",
    )(parts[0], got[0], parts[2], got[1])


def copy_sum_kernel(*refs):
    out_ref = refs[-1]
    half = out_ref.shape[1] // 2
    for index, columns in ((0, slice(0, half)), (3, slice(half, 2 * half))):
        keep, got, more = [ref[...].astype(F32) for ref in refs[index : index + 3]]
        out_ref[:, columns] = keep + got + more


def copy_sum(parts, got, more):
    keep_a, _, keep_b, _ = parts
    chunks = 4
    _, rows, width = keep_a.shape
    first = pl.BlockSpec((None, rows // chunks, width), lambda step: (0, step, 0))
    plain = pl.BlockSpec((rows // chunks, width), lambda step: (step, 0))
    return pl.pallas_call(
        copy_sum_kernel,
        grid=(chunks,),
        in_specs=[first, first, plain] * 2,
        out_specs=pl.BlockSpec((rows // chunks, 2 * width), lambda step: (step, 0)),
        out_shape=jax.ShapeDtypeStruct((rows, 2 * width), F32),
        cost_estimate=LIGHT,
        name="copy_sum",
    )(keep_a, got[0], more[0], keep_b, got[1], more[1])


def split_sum_kernel(keep_low, keep_high, got_low, got_high, low_ref, high_ref):
    low_ref[...] = add_low(keep_low[...], got_low[...])
    high_ref[...] = add_low(keep_high[...], got_high[...])


def split_sum(keep, got, cost=LIGHT):
    half, width = keep.shape[0] // 2, keep.shape[1]
    if half < 64:
        total = add_low(keep, got)
        return total[:half], total[half:]
    chunks = 2 if half % 128 == 0 else 1
    block = (half // chunks, width)
    low = pl.BlockSpec(block, lambda step: (step, 0))
    high = pl.BlockSpec(block, lambda step: (step + chunks, 0))
    return pl.pallas_call(
        split_sum_kernel,
        grid=(chunks,),
        in_specs=[low, high, low, high],
        out_specs=(low, low),
        out_shape=(jax.ShapeDtypeStruct((half, width), BF16),) * 2,
        cost_estimate=cost,
        name="split_sum",
    )(keep, keep, got, got)


def swap_halves(dense, steps):
    return [swap(send, axis, 1 << bit) for (_, send), (axis, bit) in zip(dense, steps)]


def swap_sums(sums):
    return swap(sums[0], "rep", 2), swap(sums[1], "rep", 1)


def add_low(left, right):
    return (left.astype(F32) + right.astype(F32)).astype(BF16)


def spread(blocks):
    return {bits: swap(block, "ep", bits) if bits else block for bits, block in blocks.items()}


def gather_kernel(*refs):
    for index, ref in enumerate(refs[:-1]):
        refs[-1][index] = ref[...]


def cross(blocks, members):
    return swap(jnp.concatenate([blocks[bits][1:] for bits in members], 0), "ep", 1)


def cross_late(blocks, members):
    pieces = [(blocks[bits], 1) for bits in members]
    shape = (len(pieces),) + blocks[members[0]].shape[1:]
    gathered = pl.pallas_call(
        gather_kernel,
        grid=(1,),
        in_specs=piece_specs(pieces),
        out_specs=whole(shape),
        out_shape=jax.ShapeDtypeStruct(shape, BF16),
        cost_estimate=LIGHT,
        name="gather_sum",
    )(*[array for array, _ in pieces])
    return swap(gathered, "ep", 1)


def paired_pieces(blocks, members, cross):
    crossed = cross(blocks, members)
    pieces = [((blocks[bits], 0), (crossed, place)) for place, bits in enumerate(members)]
    return [piece for pair in pieces for piece in pair]


def exchange(buffer):
    return lax.all_to_all(buffer, "ep", split_axis=0, concat_axis=0, tiled=True)


def local(
    tokens_in,
    token_ids,
    hash_table,
    doc_lengths,
    gain_one,
    shift_one,
    project_in,
    project_out,
    gain_two,
    shift_two,
    expert_in,
    expert_out,
    out_grad,
):
    tok_rows, width = tokens_in.shape
    rep_size, ep_size = lax.axis_size("rep"), lax.axis_size("ep")
    rep_bits, ep_bits = rep_size.bit_length() - 1, ep_size.bit_length() - 1
    expert_count = expert_in.shape[0] * ep_size
    capacity = 2 * tok_rows // expert_count
    slot_total = expert_count * capacity
    tile = width // (rep_size * ep_size)
    paired = expert_count <= 8
    first_weight, second_weight = expert_in[0], expert_out[0]
    rep_index, ep_index = lax.axis_index("rep"), lax.axis_index("ep")
    ep_flip = jnp.reshape(ep_index if paired else 0, (1,)).astype(jnp.int32)
    rep_flip = jnp.reshape(rep_index, (1,)).astype(jnp.int32)
    ep_steps = [("ep", bit) for bit in range(1, ep_bits)]
    rep_steps = [("rep", bit) for bit in range(rep_bits)]
    steps_a, steps_b = ep_steps + rep_steps, ep_steps[::-1] + rep_steps[::-1]
    orders, spots = [], []
    for steps in (steps_a, steps_b):
        places = [bit + (ep_bits if axis == "rep" else 0) for axis, bit in reversed(steps)] + [0]
        orders.append(tuple(places))
        spots.append(spread_bits(rep_index * ep_size + ep_index, places))
    spots = jnp.stack(spots).astype(jnp.int32)

    fronts = (
        doc_lengths,
        tokens_in,
        gain_one,
        shift_one,
        project_in,
        project_out,
        gain_two,
        shift_two,
    )
    half_rows = slot_total // 2
    if paired:
        members = tuple(range(0, expert_count, 2))
        order = members[::2] + members[1::2][::-1]
        halves = (members[::2], members[1::2][::-1])
        block_rows, block_shape = capacity, (2, capacity, width)
    else:
        block_rows, block_shape = half_rows, (expert_count, capacity, width)
    slot_row, *buffers = route(
        ep_flip, token_ids, hash_table, out_grad, expert_count, capacity, block_shape
    )
    grads = spread(dict(zip(members, buffers))) if paired else exchange(buffers[0])
    normed, query, key, value, probs, mixture, hidden, *buffers = front(
        *fronts[:2], slot_row, *fronts[2:], slot_total, block_shape
    )
    if paired:
        blocks, hidden = lax.optimization_barrier(([grads[bits] for bits in members], hidden))
        grads = dict(zip(members, blocks))
        crossed = cross(grads, order)
        grad_pieces = []
        for index, half in enumerate(halves):
            grad_pieces += [(grads[bits], 0) for bits in half]
            grad_pieces += [(crossed, index * len(half) + place) for place in range(len(half))]
    else:
        grads = grads.reshape(2, half_rows, width)
        grad_pieces = [(grads, 0), (grads, 1)]
    grad_rows, grad_act = grad_act_of(second_weight, grad_pieces)
    outs = []
    if paired:
        received = spread(dict(zip(members, buffers)))
        count = len(halves[0])
        places = [[place * capacity, (count + place) * capacity] for place in range(count)]
        sent = {}
        done = grad_rows
        for index, half in ((1, halves[1]), (0, halves[0])):
            blocks, done = lax.optimization_barrier(([received[bits] for bits in half], done))
            received.update(zip(half, blocks))
            if index:
                grad_rows = done
            else:
                outs[0][2] = done
            pieces = [(received[bits], 0) for bits in half]
            pieces += [(swap(received[bits][1:], "ep", 1), 0) for bits in half]
            *out, = expert(index, grad_act, first_weight, pieces, places, capacity)
            outs.append(out[:3])
            done = out[2]
            sent.update(spread(dict(zip(half, out[3:]))))
        places += [[first + half_rows for first in firsts] for firsts in places]
    else:
        received = exchange(buffers[0]).reshape(2, half_rows, width)
        places = [[0]]
        for index in range(2):
            *out, = expert(index, grad_act, first_weight, [(received, index)], places, half_rows)
            outs.append(out)
        sent = jnp.concatenate([outs[0][3], outs[1][3]], 0).reshape(buffers[0].shape)
        back_pieces = [(exchange(sent).reshape(1, slot_total, width), 0)]
        places = [[0, half_rows]]
    if paired:
        outs = outs[::-1]
    (act_a, grad_pre_a, rows_a), (act_b, grad_pre_b, rows_b) = outs[0][:3], outs[1][:3]
    second_parts = second_grad(rep_flip, act_a, act_b, grad_rows)
    act_a, second_parts = lax.optimization_barrier((act_a, second_parts))
    results = result_of(act_a, act_b, second_weight, places, block_rows)
    got_second = swap_copies(second_parts)
    if paired:
        blocks, results = lax.optimization_barrier(([sent[bits] for bits in members], results))
        back_pieces = paired_pieces(dict(zip(members, blocks)), members, cross)
    returned = spread(dict(zip(order, results))) if paired else exchange(
        results[0].reshape(expert_count, capacity, width)
    )
    keep_a, send_a, keep_b, send_b, grad_in = back(
        tile,
        orders,
        spots,
        back_pieces,
        slot_row,
        hidden,
        gain_two,
        out_grad,
        mixture,
        project_out,
        query,
        key,
        value,
        probs,
        normed,
        project_in,
        tokens_in,
        gain_one,
    )
    sends = (send_a, send_b)
    sends, got_second, returned = lax.optimization_barrier((sends, got_second, returned))
    got_a, got_b = swap(sends[0], "ep", 1), swap(sends[1], "ep", 1)
    sums_second = half_sums(second_parts, got_second)
    dense = [split_sum(keep_a, got_a), split_sum(keep_b, got_b)]
    rows_a, sums_second, dense = lax.optimization_barrier((rows_a, sums_second, dense))
    more_second = swap_sums(sums_second)
    first_parts = first_grad(rep_flip, rows_a, rows_b, grad_pre_a, grad_pre_b)
    first_parts, more_second = lax.optimization_barrier((first_parts, more_second))
    got_first = swap_copies(first_parts)
    summed_second = copy_sum(second_parts, got_second, more_second)
    if paired:
        pieces = paired_pieces(returned, members, cross_late)
    else:
        pieces = [(returned.reshape(1, slot_total, width), 0)]
    hidden, _ = lax.optimization_barrier((hidden, first_parts[0]))
    block_out = finish(hidden, slot_row, pieces)
    for index, pair in enumerate(zip(steps_a, steps_b)):
        got = swap_halves(dense, pair)
        if index == 0:
            got, summed_second, block_out = lax.optimization_barrier(
                (got, summed_second, block_out)
            )
        if index == 1:
            got, _ = lax.optimization_barrier((got, sums_first))
        if index == 2:
            got, more_first = lax.optimization_barrier((got, more_first))
            summed_first = copy_sum(first_parts, got_first, more_first)
        if index < len(steps_a) - 1:
            cost = LIGHT if index > 1 else HEAVY
            dense = [split_sum(keep, more, cost) for (keep, _), more in zip(dense, got)]
        if index == 0:
            (keep, send), other = dense
            got_first, keep = lax.optimization_barrier((got_first, keep))
            dense = [(keep, send), other]
            sums_first = half_sums(first_parts, got_first)
            more_first = swap_sums(sums_first)
    dense_a, dense_b = [keep.astype(F32) + more.astype(F32) for (keep, _), more in zip(dense, got)]
    return (
        block_out,
        grad_in,
        jnp.concatenate([dense_a[:, : 2 * width], dense_b[:, :width]], 1),
        dense_b[:, width:],
        dense_a[:, 2 * width + 2],
        dense_a[:, 2 * width + 3],
        dense_a[:, 2 * width],
        dense_a[:, 2 * width + 1],
        summed_first[None],
        summed_second[None],
    )


def solution(mesh):
    in_specs = (
        P(("rep", "ep"), None),
        P(("rep", "ep")),
        P(),
        P(("rep", "ep"), None),
        P(),
        P(),
        P(),
        P(),
        P(),
        P(),
        P("ep", None, None),
        P("ep", None, None),
        P(("rep", "ep"), None),
    )
    out_specs = (
        P(("rep", "ep"), None),
        P(("rep", "ep"), None),
        P(("rep", "ep"), None),
        P(("rep", "ep"), None),
        P(("rep", "ep")),
        P(("rep", "ep")),
        P(("rep", "ep")),
        P(("rep", "ep")),
        P("ep", "rep", None),
        P("ep", "rep", None),
    )
    return jax.shard_map(local, mesh=mesh, in_specs=in_specs, out_specs=out_specs, check_vma=False)
```

```python
import functools
import math

import jax
import jax.numpy as jnp
from jax import lax
from jax.experimental import pallas as pl
from jax.experimental.pallas import tpu as pltpu
from jax.sharding import PartitionSpec as P

HEADS = 16
GROUP = 4
LANES = 128
NEG_LARGE = -1e30
EPSILON = 1e-05
BF16 = jnp.bfloat16
F32 = jnp.float32
GATE_A = math.sqrt(2.0 / math.pi)
GATE_B = GATE_A * 0.044715
HEAVY = pl.CostEstimate(flops=10000000000, bytes_accessed=1 << 16, transcendentals=0)
LIGHT = pl.CostEstimate(flops=1 << 20, bytes_accessed=1 << 16, transcendentals=0)


def dot_nn(a, b):
    return lax.dot_general(a, b, (((1,), (0,)), ((), ())), preferred_element_type=F32)


def dot_nt(a, b):
    return lax.dot_general(a, b, (((1,), (1,)), ((), ())), preferred_element_type=F32)


def dot_tn(a, b):
    return lax.dot_general(a, b, (((0,), (0,)), ((), ())), preferred_element_type=F32)


def iota(shape, axis):
    return lax.broadcasted_iota(jnp.int32, shape, axis)


def whole(shape):
    return pl.BlockSpec(shape, lambda *_: (0,) * len(shape))


def piece_specs(pieces):
    def spec(array, block):
        return pl.BlockSpec((None,) + array.shape[1:], lambda *_: (block, 0, 0))

    return [spec(array, block) for array, block in pieces]


def stack_pieces(refs):
    return jnp.concatenate([ref[...] for ref in refs], 0)


def store_blocks(refs, values):
    first = 0
    for ref in refs:
        for block in range(ref.shape[0]):
            ref[block] = values[first : first + ref.shape[1]]
            first += ref.shape[1]


def norm_parts(values):
    center = jnp.mean(values, -1, keepdims=True)
    centered = values - center
    spread = jnp.mean(centered * centered, -1, keepdims=True)
    factor = lax.rsqrt(spread + EPSILON)
    return centered * factor, factor


def norm_back(grad, gain, xhat, factor):
    scaled = grad * gain
    mean_scaled = jnp.mean(scaled, -1, keepdims=True)
    mean_cross = jnp.mean(scaled * xhat, -1, keepdims=True)
    return factor * (scaled - mean_scaled - xhat * mean_cross)


def slot_matrix(slot_row, slot_total):
    tok_rows = slot_row.shape[1]
    return (iota((slot_total, tok_rows), 0) == slot_row).astype(F32).astype(BF16)


def route_kernel(
    expert_count, capacity, flip_ref, ids_ref, table_ref, grad_ref, slot_ref, *buffer_refs
):
    tok_rows = ids_ref.shape[1]
    ids = ids_ref[...]
    table_rows = table_ref.shape[0]
    high = ids // LANES
    low = ids - high * LANES
    high_hot = (iota((table_rows, tok_rows), 0) == high).astype(F32).astype(BF16)
    picked = dot_tn(table_ref[...].astype(F32).astype(BF16), high_hot)
    low_hot = iota((LANES, tok_rows), 0) == low
    expert = jnp.sum(jnp.where(low_hot, picked, 0.0), 0, keepdims=True).astype(jnp.int32)
    expert_hot = (iota((expert_count, tok_rows), 0) == expert).astype(F32)
    before = (iota((tok_rows, tok_rows), 0) < iota((tok_rows, tok_rows), 1)).astype(F32)
    earlier = dot_nn(expert_hot.astype(BF16), before.astype(BF16))
    rank = jnp.sum(earlier * expert_hot, 0, keepdims=True).astype(jnp.int32)
    slot = (expert ^ flip_ref[0]) * capacity + rank
    slot_ref[...] = slot
    slot_hot = slot_matrix(slot, expert_count * capacity)
    store_blocks(buffer_refs, dot_nn(slot_hot, grad_ref[...]).astype(BF16))


def route(flip, token_ids, hash_table, out_grad, expert_count, capacity, block_shape):
    tok_rows, width = out_grad.shape
    slot_total = expert_count * capacity
    table_rows = hash_table.shape[0] // LANES
    blocks = slot_total // (block_shape[0] * block_shape[1])
    return pl.pallas_call(
        functools.partial(route_kernel, expert_count, capacity),
        in_specs=[
            pl.BlockSpec(memory_space=pltpu.SMEM),
            whole((1, tok_rows)),
            whole((table_rows, LANES)),
            whole((tok_rows, width)),
        ],
        out_specs=(whole((1, tok_rows)),) + (whole(block_shape),) * blocks,
        out_shape=(jax.ShapeDtypeStruct((1, tok_rows), jnp.int32),)
        + (jax.ShapeDtypeStruct(block_shape, BF16),) * blocks,
        cost_estimate=LIGHT,
        name="route",
    )(flip, token_ids.reshape(1, tok_rows), hash_table.reshape(table_rows, LANES), out_grad)


def front_kernel(
    slot_total,
    head_size,
    lengths_ref,
    tokens_ref,
    slot_ref,
    gain_one_ref,
    shift_one_ref,
    query_weight_ref,
    key_weight_ref,
    value_weight_ref,
    out_weight_ref,
    gain_two_ref,
    shift_two_ref,
    normed_ref,
    query_ref,
    key_ref,
    value_ref,
    probs_ref,
    mixture_ref,
    hidden_ref,
    *refs,
):
    buffer_refs, mask_ref = refs[:-1], refs[-1]
    step = pl.program_id(0)
    tok_rows = tokens_ref.shape[0]
    group_width = query_ref.shape[1]

    @pl.when(step == 0)
    def _():
        inputs = tokens_ref[...].astype(F32)
        xhat, _ = norm_parts(inputs)
        normed_ref[...] = (xhat * gain_one_ref[...] + shift_one_ref[...]).astype(BF16)
        position = iota((1, tok_rows), 1)
        start = jnp.zeros((1, tok_rows), jnp.int32)
        bound = jnp.int32(0)
        for index in range(lengths_ref.shape[1]):
            bound = bound + lengths_ref[0, index]
            start = jnp.where(position >= bound, bound, start)
        key_position = iota((tok_rows, tok_rows), 0)
        allowed = jnp.logical_and(key_position >= start, key_position <= position)
        mask_ref[...] = jnp.where(allowed, 0.0, NEG_LARGE)
        hidden_ref[...] = inputs

    normed = normed_ref[...]
    query = dot_nn(normed, query_weight_ref[...]).astype(BF16)
    key = dot_nn(normed, key_weight_ref[...]).astype(BF16)
    value = dot_nn(normed, value_weight_ref[...]).astype(BF16)
    query_ref[...] = query
    key_ref[...] = key
    value_ref[...] = value
    lane_head = iota((1, group_width), 1) // head_size
    scale = 1.0 / math.sqrt(head_size)
    total = jnp.zeros((tok_rows, group_width), F32)
    for head in range(GROUP):
        chosen = lane_head == head
        key_part = key * jnp.where(chosen, scale, 0.0).astype(BF16)
        value_part = value * jnp.where(chosen, 1.0, 0.0).astype(BF16)
        scores = dot_nt(key_part, query) + mask_ref[...]
        exponent = jnp.exp(scores - jnp.max(scores, 0, keepdims=True))
        inverse = 1.0 / jnp.sum(exponent, 0, keepdims=True)
        weights = (exponent * inverse).astype(BF16)
        probs_ref[head] = weights
        total = total + dot_tn(weights, value_part)
    mixture = total.astype(BF16)
    mixture_ref[...] = mixture
    hidden_ref[...] += dot_nn(mixture, out_weight_ref[...])

    @pl.when(step == pl.num_programs(0) - 1)
    def _():
        xhat, _ = norm_parts(hidden_ref[...])
        routed = (xhat * gain_two_ref[...] + shift_two_ref[...]).astype(BF16)
        slot_hot = slot_matrix(slot_ref[...], slot_total)
        store_blocks(buffer_refs, dot_nn(slot_hot, routed).astype(BF16))


def front(
    doc_lengths,
    tokens_in,
    slot_row,
    gain_one,
    shift_one,
    project_in,
    project_out,
    gain_two,
    shift_two,
    slot_total,
    block_shape,
):
    tok_rows, width = tokens_in.shape
    head_size = width // HEADS
    group_width = GROUP * head_size
    steps = HEADS // GROUP
    vector = whole((1, width))
    blocks = slot_total // (block_shape[0] * block_shape[1])

    def weight_spec(part):
        return pl.BlockSpec((width, group_width), lambda step: (0, part * steps + step))

    column_spec = pl.BlockSpec((tok_rows, group_width), lambda step: (0, step))
    return pl.pallas_call(
        functools.partial(front_kernel, slot_total, head_size),
        grid=(steps,),
        in_specs=[
            pl.BlockSpec(memory_space=pltpu.SMEM),
            whole((tok_rows, width)),
            whole((1, tok_rows)),
            vector,
            vector,
            weight_spec(0),
            weight_spec(1),
            weight_spec(2),
            pl.BlockSpec((group_width, width), lambda step: (step, 0)),
            vector,
            vector,
        ],
        out_specs=(
            whole((tok_rows, width)),
            column_spec,
            column_spec,
            column_spec,
            pl.BlockSpec((GROUP, tok_rows, tok_rows), lambda step: (step, 0, 0)),
            column_spec,
            whole((tok_rows, width)),
        )
        + (whole(block_shape),) * blocks,
        out_shape=(
            jax.ShapeDtypeStruct((tok_rows, width), BF16),
            jax.ShapeDtypeStruct((tok_rows, width), BF16),
            jax.ShapeDtypeStruct((tok_rows, width), BF16),
            jax.ShapeDtypeStruct((tok_rows, width), BF16),
            jax.ShapeDtypeStruct((HEADS, tok_rows, tok_rows), BF16),
            jax.ShapeDtypeStruct((tok_rows, width), BF16),
            jax.ShapeDtypeStruct((tok_rows, width), F32),
        )
        + (jax.ShapeDtypeStruct(block_shape, BF16),) * blocks,
        scratch_shapes=[pltpu.VMEM((tok_rows, tok_rows), F32)],
        cost_estimate=LIGHT,
        name="front",
    )(
        doc_lengths,
        tokens_in,
        slot_row,
        gain_one.reshape(1, width),
        shift_one.reshape(1, width),
        project_in,
        project_in,
        project_in,
        project_out,
        gain_two.reshape(1, width),
        shift_two.reshape(1, width),
    )


def spread_bits(index, layout):
    spot = 0
    for place, bit in enumerate(layout):
        spot = spot | (((index >> bit) & 1) << place)
    return spot


def store_rows(refs, first, column, values, tile, order, spot):
    keep_ref, send_ref = refs
    layout = order
    top = len(layout) - 1
    even_kept = (spot >> top) == 0
    for index in range(0, values.shape[0] // tile, 2):
        place = (spread_bits(first + index, layout) ^ spot) & ((1 << top) - 1)
        even = values[index * tile : (index + 1) * tile]
        odd = values[(index + 1) * tile : (index + 2) * tile]
        rows = pl.ds(pl.multiple_of(place * tile, tile), tile)
        keep_ref[rows, column] = jnp.where(even_kept, even, odd).astype(BF16)
        send_ref[rows, column] = jnp.where(even_kept, odd, even).astype(BF16)


def back_kernel(
    head_size,
    tile,
    orders,
    piece_count,
    spot_ref,
    slot_ref,
    hidden_ref,
    gain_two_ref,
    out_grad_ref,
    mixture_ref,
    out_weight_ref,
    query_ref,
    key_ref,
    value_ref,
    probs_ref,
    normed_ref,
    query_weight_ref,
    key_weight_ref,
    value_weight_ref,
    tokens_ref,
    gain_one_ref,
    *refs,
):
    piece_refs = refs[:piece_count]
    dense_a = refs[piece_count : piece_count + 2]
    dense_b = refs[piece_count + 2 : piece_count + 4]
    grad_in_ref, hidden_low_ref, normed_grad_ref, small_ref = refs[piece_count + 4 :]
    step = pl.program_id(0)
    width = tokens_ref.shape[1]
    group_width = query_ref.shape[1]

    @pl.when(step == 0)
    def _():
        buffer = stack_pieces(piece_refs)
        slot_hot = slot_matrix(slot_ref[...], buffer.shape[0])
        grad_routed = dot_tn(slot_hot, buffer)
        xhat, factor = norm_parts(hidden_ref[...])
        small_ref[0:1, :] = jnp.sum(grad_routed * xhat, 0, keepdims=True)
        small_ref[1:2, :] = jnp.sum(grad_routed, 0, keepdims=True)
        grad_hidden = out_grad_ref[...].astype(F32) + norm_back(
            grad_routed, gain_two_ref[...], xhat, factor
        )
        grad_in_ref[...] = grad_hidden
        hidden_low_ref[...] = grad_hidden.astype(BF16)
        normed_grad_ref[...] = jnp.zeros_like(normed_grad_ref)
        small_ref[4:, :] = jnp.zeros((LANES - 4, width), F32)

    hidden_low = hidden_low_ref[...]
    store_rows(
        dense_b,
        step * (group_width // tile),
        slice(width, 2 * width),
        dot_tn(mixture_ref[...], hidden_low),
        tile,
        orders[1],
        spot_ref[1],
    )
    grad_mixture = dot_nt(hidden_low, out_weight_ref[...]).astype(BF16)
    query, key, value = query_ref[...], key_ref[...], value_ref[...]
    lane_head = iota((1, group_width), 1) // head_size
    scale = 1.0 / math.sqrt(head_size)
    grad_query = jnp.zeros(query.shape, F32)
    grad_key = jnp.zeros(query.shape, F32)
    grad_value = jnp.zeros(query.shape, F32)
    for head in range(GROUP):
        chosen = jnp.where(lane_head == head, 1.0, 0.0).astype(BF16)
        scaled = jnp.where(lane_head == head, scale, 0.0).astype(BF16)
        grad_part = grad_mixture * chosen
        weights_low = probs_ref[head]
        weights = weights_low.astype(F32)
        grad_weights = dot_nt(value, grad_part)
        inner = jnp.sum(weights * grad_weights, 0, keepdims=True)
        grad_scores = (weights * (grad_weights - inner)).astype(BF16)
        grad_query = grad_query + dot_tn(grad_scores, key * scaled)
        grad_key = grad_key + dot_nn(grad_scores, query * scaled)
        grad_value = grad_value + dot_nn(weights_low, grad_part)
    normed = normed_ref[...]
    for part, (grad, weight_ref) in enumerate(
        (
            (grad_query, query_weight_ref),
            (grad_key, key_weight_ref),
            (grad_value, value_weight_ref),
        )
    ):
        grad = grad.astype(BF16)
        index = part // 2
        column = pl.multiple_of((part % 2) * width + step * group_width, group_width)
        store_rows(
            (dense_a, dense_b)[index],
            0,
            pl.ds(column, group_width),
            dot_tn(normed, grad),
            tile,
            orders[index],
            spot_ref[index],
        )
        normed_grad_ref[...] += dot_nt(grad, weight_ref[...])

    @pl.when(step == pl.num_programs(0) - 1)
    def _():
        grad_normed = normed_grad_ref[...]
        xhat, factor = norm_parts(tokens_ref[...].astype(F32))
        small_ref[2:3, :] = jnp.sum(grad_normed * xhat, 0, keepdims=True)
        small_ref[3:4, :] = jnp.sum(grad_normed, 0, keepdims=True)
        store_rows(
            dense_a,
            0,
            slice(2 * width, 2 * width + LANES),
            small_ref[...].T,
            tile,
            orders[0],
            spot_ref[0],
        )
        grad_in_ref[...] += norm_back(grad_normed, gain_one_ref[...], xhat, factor)


def back(
    tile,
    orders,
    spots,
    pieces,
    slot_row,
    hidden,
    gain_two,
    out_grad,
    mixture,
    project_out,
    query,
    key,
    value,
    probs,
    normed,
    project_in,
    tokens_in,
    gain_one,
):
    tok_rows, width = tokens_in.shape
    head_size = width // HEADS
    group_width = GROUP * head_size
    steps = HEADS // GROUP
    vector = whole((1, width))
    tokens_spec = whole((tok_rows, width))

    def weight_spec(part):
        return pl.BlockSpec((width, group_width), lambda step: (0, part * steps + step))

    column_spec = pl.BlockSpec((tok_rows, group_width), lambda step: (0, step))
    return pl.pallas_call(
        functools.partial(back_kernel, head_size, tile, orders, len(pieces)),
        grid=(steps,),
        in_specs=[
            pl.BlockSpec(memory_space=pltpu.SMEM),
            whole((1, tok_rows)),
            tokens_spec,
            vector,
            tokens_spec,
            column_spec,
            pl.BlockSpec((group_width, width), lambda step: (step, 0)),
            column_spec,
            column_spec,
            column_spec,
            pl.BlockSpec((GROUP, tok_rows, tok_rows), lambda step: (step, 0, 0)),
            tokens_spec,
            weight_spec(0),
            weight_spec(1),
            weight_spec(2),
            tokens_spec,
            vector,
        ]
        + piece_specs(pieces),
        out_specs=(
            whole((width // 2, 2 * width + LANES)),
            whole((width // 2, 2 * width + LANES)),
            whole((width // 2, 2 * width)),
            whole((width // 2, 2 * width)),
            tokens_spec,
        ),
        out_shape=(
            jax.ShapeDtypeStruct((width // 2, 2 * width + LANES), BF16),
            jax.ShapeDtypeStruct((width // 2, 2 * width + LANES), BF16),
            jax.ShapeDtypeStruct((width // 2, 2 * width), BF16),
            jax.ShapeDtypeStruct((width // 2, 2 * width), BF16),
            jax.ShapeDtypeStruct((tok_rows, width), F32),
        ),
        scratch_shapes=[
            pltpu.VMEM((tok_rows, width), BF16),
            pltpu.VMEM((tok_rows, width), F32),
            pltpu.VMEM((LANES, width), F32),
        ],
        cost_estimate=LIGHT,
        name="back",
    )(
        spots,
        slot_row,
        hidden,
        gain_two.reshape(1, width),
        out_grad,
        mixture,
        project_out,
        query,
        key,
        value,
        probs,
        normed,
        project_in,
        project_in,
        project_in,
        tokens_in,
        gain_one.reshape(1, width),
        *[array for array, _ in pieces],
    )


def finish_kernel(hidden_ref, slot_ref, *refs):
    buffer = stack_pieces(refs[:-1])
    slot_hot = slot_matrix(slot_ref[...], buffer.shape[0])
    refs[-1][...] = (hidden_ref[...] + dot_tn(slot_hot, buffer)).astype(BF16)


def finish(hidden, slot_row, pieces):
    return pl.pallas_call(
        finish_kernel,
        grid=(1,),
        in_specs=[whole(hidden.shape), whole(slot_row.shape)] + piece_specs(pieces),
        out_specs=whole(hidden.shape),
        out_shape=jax.ShapeDtypeStruct(hidden.shape, BF16),
        cost_estimate=LIGHT,
        name="finish",
    )(hidden, slot_row, *[array for array, _ in pieces])


def grad_act_kernel(weight_ref, *refs):
    rows_ref, out_ref = refs[-2:]

    @pl.when(pl.program_id(0) == 0)
    def _():
        rows_ref[...] = stack_pieces(refs[:-2])

    out_ref[...] = dot_nt(rows_ref[...], weight_ref[...]).astype(BF16)


def grad_act_of(weight, pieces, chunk=1024):
    hidden_units, width = weight.shape
    rows = sum(array.shape[1] for array, _ in pieces)
    return pl.pallas_call(
        grad_act_kernel,
        grid=(hidden_units // chunk,),
        in_specs=[pl.BlockSpec((chunk, width), lambda step: (step, 0))] + piece_specs(pieces),
        out_specs=(whole((rows, width)), pl.BlockSpec((rows, chunk), lambda step: (0, step))),
        out_shape=(
            jax.ShapeDtypeStruct((rows, width), BF16),
            jax.ShapeDtypeStruct((rows, hidden_units), BF16),
        ),
        cost_estimate=LIGHT,
        name="grad_act",
    )(weight, *[array for array, _ in pieces])


def result_kernel(act_a_ref, act_b_ref, weight_ref, *refs, places):
    step = pl.program_id(0)
    total_ref = refs[-1]
    half = act_a_ref.shape[0]

    @pl.when(step == 0)
    def _():
        total_ref[...] = jnp.zeros_like(total_ref)

    total_ref[:half] += dot_nn(act_a_ref[...], weight_ref[...])
    total_ref[half:] += dot_nn(act_b_ref[...], weight_ref[...])

    @pl.when(step == pl.num_programs(0) - 1)
    def _():
        store_places(refs[:-1], total_ref, places)


def store_places(refs, total_ref, places):
    for ref, firsts in zip(refs, places):
        for block, first in enumerate(firsts):
            ref[block] = total_ref[first : first + ref.shape[1]].astype(BF16)


def result_of(act_a, act_b, weight, places, block_rows, chunk=1024):
    half, hidden_units = act_a.shape
    width = weight.shape[1]
    shapes = [(len(firsts), block_rows, width) for firsts in places]
    act_spec = pl.BlockSpec((half, chunk), lambda step: (0, step))
    return pl.pallas_call(
        functools.partial(result_kernel, places=places),
        grid=(hidden_units // chunk,),
        in_specs=[act_spec, act_spec, pl.BlockSpec((chunk, width), lambda step: (step, 0))],
        out_specs=tuple(whole(shape) for shape in shapes),
        out_shape=tuple(jax.ShapeDtypeStruct(shape, BF16) for shape in shapes),
        scratch_shapes=[pltpu.VMEM((2 * half, width), F32)],
        cost_estimate=LIGHT,
        name="result",
    )(act_a, act_b, weight)


def gate_parts(pre):
    square = pre * pre
    curve = jnp.tanh(pre * (GATE_A + GATE_B * square))
    half = 0.5 * curve + 0.5
    slope = half + (0.5 * pre) * (1.0 - curve * curve) * (GATE_A + (3.0 * GATE_B) * square)
    return pre * half, slope


def expert_kernel(tile, places, piece_count, grad_act_ref, weight_ref, *refs):
    step = pl.program_id(0)
    act_ref, grad_pre_ref, rows_ref = refs[piece_count : piece_count + 3]
    out_refs, total_ref = refs[piece_count + 3 : -1], refs[-1]

    @pl.when(step == 0)
    def _():
        rows_ref[...] = stack_pieces(refs[:piece_count])
        total_ref[...] = jnp.zeros_like(total_ref)

    weight = weight_ref[...]
    for first in range(0, rows_ref.shape[0], tile):
        rows = slice(first, first + tile)
        act, slope = gate_parts(dot_nn(rows_ref[rows, :], weight))
        act_ref[rows, :] = act.astype(BF16)
        grad_pre = (grad_act_ref[rows, :].astype(F32) * slope).astype(BF16)
        grad_pre_ref[rows, :] = grad_pre
        total_ref[rows, :] += dot_nt(grad_pre, weight)

    @pl.when(step == pl.num_programs(0) - 1)
    def _():
        store_places(out_refs, total_ref, places)


def expert(half, grad_act, weight, pieces, places, block_rows, chunk=1024, tile=256):
    width, hidden_units = weight.shape
    rows = grad_act.shape[0] // 2
    column_spec = pl.BlockSpec((rows, chunk), lambda step: (0, step))
    shapes = [(len(firsts), block_rows, width) for firsts in places]
    return pl.pallas_call(
        functools.partial(expert_kernel, tile, places, len(pieces)),
        grid=(hidden_units // chunk,),
        in_specs=[
            pl.BlockSpec((rows, chunk), lambda step: (half, step)),
            pl.BlockSpec((width, chunk), lambda step: (0, step)),
        ]
        + piece_specs(pieces),
        out_specs=(column_spec, column_spec, whole((rows, width)))
        + tuple(whole(shape) for shape in shapes),
        out_shape=(
            jax.ShapeDtypeStruct((rows, hidden_units), BF16),
            jax.ShapeDtypeStruct((rows, hidden_units), BF16),
            jax.ShapeDtypeStruct((rows, width), BF16),
        )
        + tuple(jax.ShapeDtypeStruct(shape, BF16) for shape in shapes),
        scratch_shapes=[pltpu.VMEM((rows, width), F32)],
        cost_estimate=LIGHT,
        name="expert",
    )(grad_act, weight, *[array for array, _ in pieces])


def first_grad_kernel(flip_ref, rows_a_ref, rows_b_ref, grad_a_ref, grad_b_ref, *refs):
    step = pl.program_id(0)
    half_steps = pl.num_programs(0) // 2
    product_ref = refs[-1]
    product = dot_tn(rows_a_ref[...], grad_a_ref[...]) + dot_tn(rows_b_ref[...], grad_b_ref[...])
    product_ref[...] = product.astype(BF16)
    owned = product_ref.shape[0] // 4

    def piece(place):
        row = pl.multiple_of((place ^ flip_ref[0]) * owned, owned)
        return product_ref[pl.ds(row, owned), :]

    keep_a, send_a, keep_b, send_b = refs[:-1]

    @pl.when(step < half_steps)
    def _():
        for index, (kept, sent) in enumerate(((0, 1), (2, 3))):
            keep_a[index] = piece(kept)
            send_a[index] = piece(sent)

    @pl.when(step >= half_steps)
    def _():
        for index, (kept, sent) in enumerate(((0, 2), (1, 3))):
            keep_b[index] = piece(kept)
            send_b[index] = piece(sent)


def first_grad(flip, rows_a, rows_b, grad_a, grad_b, chunk=1024):
    rows, width = rows_a.shape
    columns = grad_a.shape[1]
    steps = columns // chunk
    shape = jax.ShapeDtypeStruct((2, width // 4, columns // 2), BF16)
    block = (2, width // 4, chunk)
    spec_a = pl.BlockSpec(block, lambda step: (0, 0, jnp.minimum(step, steps // 2 - 1)))
    spec_b = pl.BlockSpec(block, lambda step: (0, 0, jnp.maximum(step - steps // 2, 0)))
    return pl.pallas_call(
        first_grad_kernel,
        grid=(steps,),
        in_specs=[
            pl.BlockSpec(memory_space=pltpu.SMEM),
            whole((rows, width)),
            whole((rows, width)),
            pl.BlockSpec((rows, chunk), lambda step: (0, step)),
            pl.BlockSpec((rows, chunk), lambda step: (0, step)),
        ],
        out_specs=(spec_a, spec_a, spec_b, spec_b),
        out_shape=(shape,) * 4,
        scratch_shapes=[pltpu.VMEM((width, chunk), BF16)],
        cost_estimate=LIGHT,
        name="first_grad",
    )(flip, rows_a, rows_b, grad_a, grad_b)


def second_grad_kernel(
    flip_ref, act_a_ref, act_b_ref, grad_ref, keep_a, send_a, keep_b, send_b
):
    step = pl.program_id(0)
    rows = act_a_ref.shape[0]
    product = dot_tn(act_a_ref[...], grad_ref[:rows]) + dot_tn(act_b_ref[...], grad_ref[rows:])
    product = product.astype(BF16)
    half = product.shape[1] // 2

    @pl.when(step == 0)
    def _():
        send_a[0] = product[:, :half]
        send_b[0] = product[:, half:]

    @pl.when(step == 1)
    def _():
        send_a[0] = product[:, :half]
        keep_b[0] = product[:, half:]

    @pl.when(step == 2)
    def _():
        keep_a[0] = product[:, :half]
        send_b[0] = product[:, half:]

    @pl.when(step == 3)
    def _():
        keep_a[0] = product[:, :half]
        keep_b[0] = product[:, half:]


def second_grad(flip, act_a, act_b, grad):
    rows, width = grad.shape
    owned = act_a.shape[1] // 4
    act_spec = pl.BlockSpec(
        (rows // 2, owned), lambda step, flip_ref: (0, place_of(step) ^ flip_ref[0])
    )
    shape = jax.ShapeDtypeStruct((2, owned, width // 2), BF16)
    block = (1, owned, width // 2)

    def spec(first_step):
        return pl.BlockSpec(
            block, lambda step, flip_ref: (1 - (step >= first_step).astype(jnp.int32), 0, 0)
        )

    return pl.pallas_call(
        second_grad_kernel,
        grid_spec=pltpu.PrefetchScalarGridSpec(
            num_scalar_prefetch=1,
            grid=(4,),
            in_specs=[
                act_spec,
                act_spec,
                pl.BlockSpec((rows, width), lambda step, flip_ref: (0, 0)),
            ],
            out_specs=(spec(3), spec(1), spec(3), spec(2)),
        ),
        out_shape=(shape,) * 4,
        cost_estimate=LIGHT,
        name="second_grad",
    )(flip, act_a, act_b, grad)


def place_of(step):
    return jnp.where(step == 0, 3, jnp.where(step == 3, 0, step))


def swap(values, axis, bits):
    size = lax.axis_size(axis)
    return lax.ppermute(values, axis, [(index, index ^ bits) for index in range(size)])


def swap_copies(parts):
    return swap(parts[1], "rep", 1), swap(parts[3], "rep", 2)


def half_sum_kernel(keep_a, got_a, keep_b, got_b, out_a, out_b):
    out_a[...] = add_low(keep_a[...], got_a[...])
    out_b[...] = add_low(keep_b[...], got_b[...])


def half_sums(parts, got, chunks=2):
    _, rows, width = got[0].shape
    block = (None, rows // chunks, width)
    out_spec = pl.BlockSpec(block[1:], lambda step: (step, 0))
    return pl.pallas_call(
        half_sum_kernel,
        grid=(chunks,),
        in_specs=[pl.BlockSpec(block, lambda step: (1, step, 0))] * 4,
        out_specs=(out_spec,) * 2,
        out_shape=(jax.ShapeDtypeStruct((rows, width), BF16),) * 2,
        cost_estimate=LIGHT,
        name="half_sum",
    )(parts[0], got[0], parts[2], got[1])


def copy_sum_kernel(*refs):
    out_ref = refs[-1]
    half = out_ref.shape[1] // 2
    for index, columns in ((0, slice(0, half)), (3, slice(half, 2 * half))):
        keep, got, more = [ref[...].astype(F32) for ref in refs[index : index + 3]]
        out_ref[:, columns] = keep + got + more


def copy_sum(parts, got, more):
    keep_a, _, keep_b, _ = parts
    chunks = 4
    _, rows, width = keep_a.shape
    first = pl.BlockSpec((None, rows // chunks, width), lambda step: (0, step, 0))
    plain = pl.BlockSpec((rows // chunks, width), lambda step: (step, 0))
    return pl.pallas_call(
        copy_sum_kernel,
        grid=(chunks,),
        in_specs=[first, first, plain] * 2,
        out_specs=pl.BlockSpec((rows // chunks, 2 * width), lambda step: (step, 0)),
        out_shape=jax.ShapeDtypeStruct((rows, 2 * width), F32),
        cost_estimate=LIGHT,
        name="copy_sum",
    )(keep_a, got[0], more[0], keep_b, got[1], more[1])


def split_sum_kernel(keep_low, keep_high, got_low, got_high, low_ref, high_ref):
    low_ref[...] = add_low(keep_low[...], got_low[...])
    high_ref[...] = add_low(keep_high[...], got_high[...])


def split_sum(keep, got, cost=LIGHT):
    half, width = keep.shape[0] // 2, keep.shape[1]
    if half < 64:
        total = add_low(keep, got)
        return total[:half], total[half:]
    chunks = 2 if half % 128 == 0 else 1
    block = (half // chunks, width)
    low = pl.BlockSpec(block, lambda step: (step, 0))
    high = pl.BlockSpec(block, lambda step: (step + chunks, 0))
    return pl.pallas_call(
        split_sum_kernel,
        grid=(chunks,),
        in_specs=[low, high, low, high],
        out_specs=(low, low),
        out_shape=(jax.ShapeDtypeStruct((half, width), BF16),) * 2,
        cost_estimate=cost,
        name="split_sum",
    )(keep, keep, got, got)


def swap_halves(dense, steps):
    return [swap(send, axis, 1 << bit) for (_, send), (axis, bit) in zip(dense, steps)]


def swap_sums(sums):
    return swap(sums[0], "rep", 2), swap(sums[1], "rep", 1)


def add_low(left, right):
    return (left.astype(F32) + right.astype(F32)).astype(BF16)


def spread(blocks):
    return {bits: swap(block, "ep", bits) if bits else block for bits, block in blocks.items()}


def gather_kernel(*refs):
    for index, ref in enumerate(refs[:-1]):
        refs[-1][index] = ref[...]


def cross(blocks, members):
    return swap(jnp.concatenate([blocks[bits][1:] for bits in members], 0), "ep", 1)


def cross_late(blocks, members):
    pieces = [(blocks[bits], 1) for bits in members]
    shape = (len(pieces),) + blocks[members[0]].shape[1:]
    gathered = pl.pallas_call(
        gather_kernel,
        grid=(1,),
        in_specs=piece_specs(pieces),
        out_specs=whole(shape),
        out_shape=jax.ShapeDtypeStruct(shape, BF16),
        cost_estimate=LIGHT,
        name="gather_sum",
    )(*[array for array, _ in pieces])
    return swap(gathered, "ep", 1)


def paired_pieces(blocks, members, cross):
    crossed = cross(blocks, members)
    pieces = [((blocks[bits], 0), (crossed, place)) for place, bits in enumerate(members)]
    return [piece for pair in pieces for piece in pair]


def exchange(buffer):
    return lax.all_to_all(buffer, "ep", split_axis=0, concat_axis=0, tiled=True)


def local(
    tokens_in,
    token_ids,
    hash_table,
    doc_lengths,
    gain_one,
    shift_one,
    project_in,
    project_out,
    gain_two,
    shift_two,
    expert_in,
    expert_out,
    out_grad,
):
    tok_rows, width = tokens_in.shape
    rep_size, ep_size = lax.axis_size("rep"), lax.axis_size("ep")
    rep_bits, ep_bits = rep_size.bit_length() - 1, ep_size.bit_length() - 1
    expert_count = expert_in.shape[0] * ep_size
    capacity = 2 * tok_rows // expert_count
    slot_total = expert_count * capacity
    tile = width // (rep_size * ep_size)
    paired = expert_count <= 8
    first_weight, second_weight = expert_in[0], expert_out[0]
    rep_index, ep_index = lax.axis_index("rep"), lax.axis_index("ep")
    ep_flip = jnp.reshape(ep_index if paired else 0, (1,)).astype(jnp.int32)
    rep_flip = jnp.reshape(rep_index, (1,)).astype(jnp.int32)
    ep_steps = [("ep", bit) for bit in range(1, ep_bits)]
    rep_steps = [("rep", bit) for bit in range(rep_bits)]
    steps_a, steps_b = ep_steps + rep_steps, ep_steps[::-1] + rep_steps[::-1]
    orders, spots = [], []
    for steps in (steps_a, steps_b):
        places = [bit + (ep_bits if axis == "rep" else 0) for axis, bit in reversed(steps)] + [0]
        orders.append(tuple(places))
        spots.append(spread_bits(rep_index * ep_size + ep_index, places))
    spots = jnp.stack(spots).astype(jnp.int32)

    fronts = (
        doc_lengths,
        tokens_in,
        gain_one,
        shift_one,
        project_in,
        project_out,
        gain_two,
        shift_two,
    )
    half_rows = slot_total // 2
    if paired:
        members = tuple(range(0, expert_count, 2))
        order = members[::2] + members[1::2][::-1]
        halves = (members[::2], members[1::2][::-1])
        block_rows, block_shape = capacity, (2, capacity, width)
    else:
        block_rows, block_shape = half_rows, (expert_count, capacity, width)
    slot_row, *buffers = route(
        ep_flip, token_ids, hash_table, out_grad, expert_count, capacity, block_shape
    )
    grads = spread(dict(zip(members, buffers))) if paired else exchange(buffers[0])
    normed, query, key, value, probs, mixture, hidden, *buffers = front(
        *fronts[:2], slot_row, *fronts[2:], slot_total, block_shape
    )
    if paired:
        blocks, hidden = lax.optimization_barrier(([grads[bits] for bits in members], hidden))
        grads = dict(zip(members, blocks))
        crossed = cross(grads, order)
        grad_pieces = []
        for index, half in enumerate(halves):
            grad_pieces += [(grads[bits], 0) for bits in half]
            grad_pieces += [(crossed, index * len(half) + place) for place in range(len(half))]
    else:
        grads = grads.reshape(2, half_rows, width)
        grad_pieces = [(grads, 0), (grads, 1)]
    grad_rows, grad_act = grad_act_of(second_weight, grad_pieces)
    outs = []
    if paired:
        received = spread(dict(zip(members, buffers)))
        count = len(halves[0])
        places = [[place * capacity, (count + place) * capacity] for place in range(count)]
        sent = {}
        done = grad_rows
        for index, half in ((1, halves[1]), (0, halves[0])):
            blocks, done = lax.optimization_barrier(([received[bits] for bits in half], done))
            received.update(zip(half, blocks))
            if index:
                grad_rows = done
            else:
                outs[0][2] = done
            pieces = [(received[bits], 0) for bits in half]
            pieces += [(swap(received[bits][1:], "ep", 1), 0) for bits in half]
            *out, = expert(index, grad_act, first_weight, pieces, places, capacity)
            outs.append(out[:3])
            done = out[2]
            sent.update(spread(dict(zip(half, out[3:]))))
        places += [[first + half_rows for first in firsts] for firsts in places]
    else:
        received = exchange(buffers[0]).reshape(2, half_rows, width)
        places = [[0]]
        for index in range(2):
            *out, = expert(index, grad_act, first_weight, [(received, index)], places, half_rows)
            outs.append(out)
        sent = jnp.concatenate([outs[0][3], outs[1][3]], 0).reshape(buffers[0].shape)
        back_pieces = [(exchange(sent).reshape(1, slot_total, width), 0)]
        places = [[0, half_rows]]
    if paired:
        outs = outs[::-1]
    (act_a, grad_pre_a, rows_a), (act_b, grad_pre_b, rows_b) = outs[0][:3], outs[1][:3]
    second_parts = second_grad(rep_flip, act_a, act_b, grad_rows)
    act_a, second_parts = lax.optimization_barrier((act_a, second_parts))
    results = result_of(act_a, act_b, second_weight, places, block_rows)
    got_second = swap_copies(second_parts)
    if paired:
        blocks, results = lax.optimization_barrier(([sent[bits] for bits in members], results))
        back_pieces = paired_pieces(dict(zip(members, blocks)), members, cross)
    returned = spread(dict(zip(order, results))) if paired else exchange(
        results[0].reshape(expert_count, capacity, width)
    )
    keep_a, send_a, keep_b, send_b, grad_in = back(
        tile,
        orders,
        spots,
        back_pieces,
        slot_row,
        hidden,
        gain_two,
        out_grad,
        mixture,
        project_out,
        query,
        key,
        value,
        probs,
        normed,
        project_in,
        tokens_in,
        gain_one,
    )
    sends = (send_a, send_b)
    sends, got_second, returned = lax.optimization_barrier((sends, got_second, returned))
    got_a, got_b = swap(sends[0], "ep", 1), swap(sends[1], "ep", 1)
    sums_second = half_sums(second_parts, got_second)
    dense = [split_sum(keep_a, got_a), split_sum(keep_b, got_b)]
    rows_a, sums_second, dense = lax.optimization_barrier((rows_a, sums_second, dense))
    more_second = swap_sums(sums_second)
    first_parts = first_grad(rep_flip, rows_a, rows_b, grad_pre_a, grad_pre_b)
    first_parts, more_second = lax.optimization_barrier((first_parts, more_second))
    got_first = swap_copies(first_parts)
    summed_second = copy_sum(second_parts, got_second, more_second)
    if paired:
        pieces = paired_pieces(returned, members, cross_late)
    else:
        pieces = [(returned.reshape(1, slot_total, width), 0)]
    hidden, _ = lax.optimization_barrier((hidden, first_parts[0]))
    block_out = finish(hidden, slot_row, pieces)
    for index, pair in enumerate(zip(ep_steps, ep_steps[::-1])):
        got = swap_halves(dense, pair)
        if index == 0:
            got, summed_second, block_out = lax.optimization_barrier(
                (got, summed_second, block_out)
            )
        if index == 1:
            got, _ = lax.optimization_barrier((got, sums_first))
        if index < len(ep_steps) - 1:
            cost = LIGHT if index else HEAVY
            dense = [split_sum(keep, more, cost) for (keep, _), more in zip(dense, got)]
        else:
            dense = [add_low(keep, more) for (keep, _), more in zip(dense, got)]
        if index == 0:
            (keep, send), other = dense
            got_first, keep = lax.optimization_barrier((got_first, keep))
            dense = [(keep, send), other]
            sums_first = half_sums(first_parts, got_first)
            more_first = swap_sums(sums_first)

    def quarters(place_a, place_b):
        rows = [slice(place * tile, (place + 1) * tile) for place in (place_a, place_b)]
        return jnp.concatenate([dense[0][rows[0]], dense[1][rows[1]]], 1)

    places_a = {1: 2, 2: 1, 3: 3}
    got = [swap(quarters(places_a[bits], bits), "rep", bits) for bits in (3, 1, 2)]
    summed_first = copy_sum(first_parts, got_first, more_first)
    got, _ = lax.optimization_barrier((got, summed_first))
    dense = quarters(0, 0).astype(F32) + sum(part.astype(F32) for part in got)
    return (
        block_out,
        grad_in,
        jnp.concatenate(
            [dense[:, : 2 * width], dense[:, 2 * width + LANES : 3 * width + LANES]], 1
        ),
        dense[:, 3 * width + LANES :],
        dense[:, 2 * width + 2],
        dense[:, 2 * width + 3],
        dense[:, 2 * width],
        dense[:, 2 * width + 1],
        summed_first[None],
        summed_second[None],
    )


def solution(mesh):
    in_specs = (
        P(("rep", "ep"), None),
        P(("rep", "ep")),
        P(),
        P(("rep", "ep"), None),
        P(),
        P(),
        P(),
        P(),
        P(),
        P(),
        P("ep", None, None),
        P("ep", None, None),
        P(("rep", "ep"), None),
    )
    out_specs = (
        P(("rep", "ep"), None),
        P(("rep", "ep"), None),
        P(("rep", "ep"), None),
        P(("rep", "ep"), None),
        P(("rep", "ep")),
        P(("rep", "ep")),
        P(("rep", "ep")),
        P(("rep", "ep")),
        P("ep", "rep", None),
        P("ep", "rep", None),
    )
    return jax.shard_map(local, mesh=mesh, in_specs=in_specs, out_specs=out_specs, check_vma=False)
```
